256 devices in a mesh: row: 4 (over x), col: 16 (over z, core), depth: 4 (over y).
Axes of the slice: x: 4, y: 4, z: 8, core: 2. Of those that a mesh axis runs over, the one named last changes fastest.
Arguments:
- blocks: bfloat16 [512, 16, 128, 128], P(('row', 'col'), 'depth'), may hold values from -2 to 2
- block_cols: int32 [512, 16], replicated, may hold values from 0 to 511, as said below
- product_cols: int32 [512, 24], P(('row', 'col')), may hold values from 0 to 511, as said below
Outputs:
- purified: bfloat16 [512, 24, 128, 128], P(('row', 'col'), 'depth')
The draws below stay inside these ranges and needn't reach their ends.
Inputs may be any that keep to these rules, and one draw needn't show every extreme that they name: `block_cols`: the 16 entries of a block row i are distinct, each within 8 of i counted cyclically modulo 512. `product_cols`: the 24 entries of a block row i are distinct, each within 16 of i counted cyclically modulo 512.
All inputs are finite; a program needn't handle non-finite values.
Results may differ from the reference program's by a relative error of at most 0.015.
Values may be sent and summed in bfloat16 or wider, within the bound.
A program may use at most 128 MiB of HBM per device.

```python
import jax
import jax.numpy as jnp
from jax import lax

B = 128
RD = 8
F = 16
G = 24
NB = 512
N_DEPTH = 4


def band_pattern(key, amount, radius, extent):
    row_ids = jnp.arange(extent, dtype=jnp.int32)
    subkeys = jax.random.split(key, extent)
    shuffled = jax.vmap(lambda sub_key: jax.random.permutation(sub_key, 2 * radius + 1))(subkeys)
    chosen = shuffled[:, :amount].astype(jnp.int32)
    return ((row_ids[:, None] + chosen - radius) % extent).astype(jnp.int32)


def draw_block_cols(key, part):
    return band_pattern(jax.random.fold_in(key, 11), F, RD, NB)


def draw_product_cols(key, part):
    return band_pattern(jax.random.fold_in(key, 29), G, 2 * RD, NB)


def block_levels(key, shape, shards, low, high):
    def one(dim, parts):
        heights = jax.random.uniform(jax.random.fold_in(jax.random.fold_in(key, 6), dim), (parts,), jnp.float32, low / len(shards), high / len(shards))
        return jnp.repeat(jnp.exp(heights), shape[dim] // parts).reshape((-1,) + (1,) * (len(shape) - dim - 1))

    factor_of = one(*shards[0])
    for cut in shards[1:]:
        factor_of = factor_of * one(*cut)
    return factor_of


def scatter_about(key, shape, deviation, reach, cuts=(), kind=jnp.bfloat16):
    result = jax.random.normal(key, shape, jnp.float32) * deviation
    if len(cuts) > 0:
        result = block_levels(key, shape, cuts, -0.22, 0.18) * result
    return jnp.clip(result, min=-reach, max=reach).astype(kind)


def setup_inputs(seed: int = 0) -> dict:
    streams_of = jax.random.split(jax.random.key(seed), 4)
    blocks = scatter_about(streams_of[0], (NB, F, B, B), 0.15, 2.0, ((0, 64), (1, 4)))
    block_cols = draw_block_cols(jax.random.fold_in(streams_of[3], 71), 0)
    product_cols = draw_product_cols(jax.random.fold_in(streams_of[3], 71), 0)
    return dict(blocks=blocks, block_cols=block_cols, product_cols=product_cols)


def select_blocks(blocks, block_cols, inner_rows, targets):
    cols_of = block_cols[inner_rows]
    matches = cols_of[:, :, None] == targets[None, None, :]
    has_match = jnp.any(matches, axis=1)
    slot_ids = jnp.arange(F, dtype=jnp.int32)[None, :, None]
    position = jnp.sum(jnp.where(matches, slot_ids, 0), axis=1).astype(jnp.int32)
    picked = blocks[inner_rows[:, None], position].astype(jnp.float32)
    return jnp.where(has_match[:, :, None, None], picked, jnp.zeros((), jnp.float32))


def depth_partials(left_blocks, right_blocks, groups):
    left_group = left_blocks.reshape(groups, -1, B, B)
    right_group = right_blocks.reshape(groups, -1, right_blocks.shape[1], B, B)
    partial_value = jnp.einsum('dsab,dstbc->dtac', left_group, right_group)
    rounded = lax.optimization_barrier(partial_value.astype(jnp.bfloat16))
    return jnp.sum(rounded.astype(jnp.float32), axis=0)


def reference(blocks, block_cols, product_cols):
    def one_row(row_id):
        left_blocks = blocks[row_id].astype(jnp.float32)
        inner_rows = block_cols[row_id]
        targets = product_cols[row_id]
        right_first = select_blocks(blocks, block_cols, inner_rows, targets)
        square = depth_partials(left_blocks, right_first, N_DEPTH).astype(jnp.bfloat16)
        right_second = select_blocks(blocks, block_cols, targets, targets)
        cubed = depth_partials(square.astype(jnp.float32), right_second, N_DEPTH)
        return (3.0 * square.astype(jnp.float32) - 2.0 * cubed).astype(jnp.bfloat16)

    return lax.map(one_row, jnp.arange(NB, dtype=jnp.int32))
```

```python
import functools

import jax
import jax.numpy as jnp
from jax import lax
from jax.experimental import pallas as pl
from jax.experimental.pallas import tpu as pltpu
from jax.sharding import PartitionSpec as P


def shifted(value, axis, steps):
    count = lax.axis_size(axis)
    pairs = [(source, (source + steps) % count) for source in range(count)]
    return lax.ppermute(value, axis, pairs)


def block_table(block_cols, rows, targets, start_row, order_total, fill_count, miss):
    cols_of = block_cols[rows]
    matches = cols_of[:, None, :, :] == targets[:, :, None, None]
    has_match = jnp.any(matches, axis=3)
    slot_ids = jnp.arange(fill_count, dtype=jnp.int32)[None, None, None, :]
    position = jnp.sum(jnp.where(matches, slot_ids, 0), axis=3)
    local_rows = (rows - start_row) % order_total
    flat = local_rows[:, None, :] * fill_count + position
    flat = jnp.clip(flat, 0, miss)
    return jnp.where(has_match, flat, miss).astype(jnp.int32)


def product_kernel(n_out, n_inner, final, idx_ref, left_ref, halo_ref, *rest):
    if final:
        own_ref, out_ref = rest
    else:
        (out_ref,) = rest
    edge = left_ref.shape[-1]

    def body(item, carry):
        row = item // n_out
        col = item % n_out
        acc = jnp.zeros((edge, edge), jnp.float32)
        for inner in range(n_inner):
            pick = idx_ref[item * n_inner + inner]
            acc += jnp.dot(
                left_ref[row, inner], halo_ref[pick], preferred_element_type=jnp.float32
            )
        if final:
            value = 3.0 * own_ref[row, col].astype(jnp.float32) - 2.0 * acc
        else:
            value = acc
        out_ref[row, col] = value.astype(out_ref.dtype)
        return carry

    lax.fori_loop(0, left_ref.shape[0] * n_out, body, 0)


def block_products(table, left, halo, own=None):
    rows, n_inner, edge = left.shape[0], left.shape[1], left.shape[2]
    n_out = table.shape[1]
    final = own is not None
    operands = [table.reshape(-1), left, halo] + ([own] if final else [])
    vmem = pl.BlockSpec(memory_space=pltpu.VMEM)
    flops = 2 * rows * n_out * n_inner * edge ** 3
    moved = sum(int(x.size) * x.dtype.itemsize for x in operands) + rows * n_out * edge * edge * 2
    return pl.pallas_call(
        functools.partial(product_kernel, n_out, n_inner, final),
        out_shape=jax.ShapeDtypeStruct((rows, n_out, edge, edge), jnp.bfloat16),
        in_specs=[pl.BlockSpec(memory_space=pltpu.SMEM)] + [vmem] * (len(operands) - 1),
        out_specs=vmem,
        compiler_params=pltpu.CompilerParams(vmem_limit_bytes=60 * 1024 * 1024),
        cost_estimate=pl.CostEstimate(flops=flops, transcendentals=0, bytes_accessed=moved),
    )(*operands)


def local(blocks, block_cols, product_cols):
    row_count = blocks.shape[0]
    block_edge = blocks.shape[2]
    fill_count = block_cols.shape[1]
    order_total = row_count * lax.axis_size(("row", "col"))
    row_place = lax.axis_index(("row", "col"))
    depth_index = lax.axis_index("depth")
    depth_count = lax.axis_size("depth")
    target_share = product_cols.shape[1] // depth_count
    zero = jnp.zeros((1, block_edge, block_edge), blocks.dtype)

    full_rows = lax.all_gather(blocks, "depth", axis=1, tiled=True)
    near = {offset: shifted(full_rows, ("row", "col"), offset) for offset in (2, 1, -1, -2)}
    near[0] = full_rows

    def halo_of(reach):
        pieces = [near[offset] for offset in range(reach, -reach - 1, -1)]
        flat = jnp.concatenate(pieces, axis=0).reshape(-1, block_edge, block_edge)
        return jnp.concatenate([flat, zero], axis=0)

    own_cols = lax.dynamic_slice_in_dim(block_cols, row_place * row_count, row_count, 0)
    own_targets = lax.dynamic_slice_in_dim(
        product_cols, depth_index * target_share, target_share, 1
    )

    halo_first = halo_of(1)
    table_first = block_table(
        block_cols, own_cols, own_targets, (row_place - 1) * row_count, order_total,
        fill_count, halo_first.shape[0] - 1,
    )
    square = block_products(table_first, full_rows, halo_first)

    square_rows = lax.all_gather(square, "depth", axis=1, tiled=True)
    halo_second = halo_of(2)
    table_second = block_table(
        block_cols, product_cols, own_targets, (row_place - 2) * row_count, order_total,
        fill_count, halo_second.shape[0] - 1,
    )
    return block_products(table_second, square_rows, halo_second, own=square)


def solution(mesh):
    placed = (P(("row", "col"), "depth", None, None), P(), P(("row", "col"), None))
    return jax.shard_map(
        local,
        mesh=mesh,
        in_specs=placed,
        out_specs=P(("row", "col"), "depth", None, None),
        check_vma=False,
    )
```

```python
import functools

import jax
import jax.numpy as jnp
from jax import lax
from jax.experimental import pallas as pl
from jax.experimental.pallas import tpu as pltpu
from jax.sharding import PartitionSpec as P


def shifted(value, axis, steps):
    count = lax.axis_size(axis)
    pairs = [(source, (source + steps) % count) for source in range(count)]
    return lax.ppermute(value, axis, pairs)


def block_table(block_cols, rows, targets, start_row, order_total, fill_count, miss):
    cols_of = block_cols[rows]
    matches = cols_of[:, None, :, :] == targets[:, :, None, None]
    has_match = jnp.any(matches, axis=3)
    slot_ids = jnp.arange(fill_count, dtype=jnp.int32)[None, None, None, :]
    position = jnp.sum(jnp.where(matches, slot_ids, 0), axis=3)
    local_rows = (rows - start_row) % order_total
    flat = local_rows[:, None, :] * fill_count + position
    flat = jnp.clip(flat, 0, miss)
    return jnp.where(has_match, flat, miss).astype(jnp.int32)


def product_kernel(n_out, n_inner, n_pieces, final, idx_ref, left_ref, *rest):
    pieces = rest[:n_pieces]
    rest = rest[n_pieces:]
    if final:
        own_ref, out_ref, halo, lcat, rcat, sems = rest
    else:
        out_ref, halo, lcat, rcat, sems = rest
    edge = left_ref.shape[-1]
    span = pieces[0].shape[0]
    copies = [
        pltpu.make_async_copy(piece, halo.at[pl.ds(k * span, span)], sems.at[k])
        for k, piece in enumerate(pieces)
    ]
    for copy in copies:
        copy.start()
    halo[n_pieces * span] = jnp.zeros((edge, edge), halo.dtype)
    for copy in copies:
        copy.wait()

    def row_body(row, carry):
        for inner in range(n_inner):
            lcat[:, inner * edge:(inner + 1) * edge] = left_ref[row, inner]

        def col_body(col, carry):
            item = row * n_out + col
            for inner in range(n_inner):
                pick = idx_ref[item * n_inner + inner]
                rcat[inner * edge:(inner + 1) * edge, :] = halo[pick]
            acc = jnp.dot(lcat[...], rcat[...], preferred_element_type=jnp.float32)
            if final:
                value = 3.0 * own_ref[row, col].astype(jnp.float32) - 2.0 * acc
            else:
                value = acc
            out_ref[row, col] = value.astype(out_ref.dtype)
            return carry

        return lax.fori_loop(0, n_out, col_body, carry)

    lax.fori_loop(0, left_ref.shape[0], row_body, 0)


def block_products(table, left, pieces, own=None):
    rows, n_inner, edge = left.shape[0], left.shape[1], left.shape[2]
    n_out = table.shape[1]
    final = own is not None
    flat_pieces = [piece.reshape(-1, edge, edge) for piece in pieces]
    span = flat_pieces[0].shape[0]
    operands = [table.reshape(-1), left] + flat_pieces + ([own] if final else [])
    vmem = pl.BlockSpec(memory_space=pltpu.VMEM)
    anywhere = pl.BlockSpec(memory_space=pl.ANY)
    in_specs = [pl.BlockSpec(memory_space=pltpu.SMEM), vmem] + [anywhere] * len(pieces)
    in_specs += [vmem] if final else []
    flops = 2 * rows * n_out * n_inner * edge ** 3
    moved = sum(int(x.size) * x.dtype.itemsize for x in operands) + rows * n_out * edge * edge * 2
    return pl.pallas_call(
        functools.partial(product_kernel, n_out, n_inner, len(pieces), final),
        out_shape=jax.ShapeDtypeStruct((rows, n_out, edge, edge), jnp.bfloat16),
        in_specs=in_specs,
        out_specs=vmem,
        scratch_shapes=[
            pltpu.VMEM((len(pieces) * span + 1, edge, edge), left.dtype),
            pltpu.VMEM((edge, n_inner * edge), left.dtype),
            pltpu.VMEM((n_inner * edge, edge), left.dtype),
            pltpu.SemaphoreType.DMA((len(pieces),)),
        ],
        compiler_params=pltpu.CompilerParams(vmem_limit_bytes=62 * 1024 * 1024),
        cost_estimate=pl.CostEstimate(flops=flops, transcendentals=0, bytes_accessed=moved),
    )(*operands)


def local(blocks, block_cols, product_cols):
    row_count = blocks.shape[0]
    block_edge = blocks.shape[2]
    fill_count = block_cols.shape[1]
    order_total = row_count * lax.axis_size(("row", "col"))
    row_place = lax.axis_index(("row", "col"))
    depth_index = lax.axis_index("depth")
    depth_count = lax.axis_size("depth")
    target_share = product_cols.shape[1] // depth_count

    full_rows = lax.all_gather(blocks, "depth", axis=1, tiled=True)
    near = {0: full_rows}
    near[1] = shifted(full_rows, ("row", "col"), 1)
    near[-1] = shifted(full_rows, ("row", "col"), -1)
    near[2] = shifted(near[1], ("row", "col"), 1)
    near[-2] = shifted(near[-1], ("row", "col"), -1)

    def halo_of(reach):
        return [near[offset] for offset in range(reach, -reach - 1, -1)]

    own_cols = lax.dynamic_slice_in_dim(block_cols, row_place * row_count, row_count, 0)
    own_targets = lax.dynamic_slice_in_dim(
        product_cols, depth_index * target_share, target_share, 1
    )

    halo_first = halo_of(1)
    table_first = block_table(
        block_cols, own_cols, own_targets, (row_place - 1) * row_count, order_total,
        fill_count, len(halo_first) * row_count * fill_count,
    )
    square = block_products(table_first, full_rows, halo_first)

    square_rows = lax.all_gather(square, "depth", axis=1, tiled=True)
    halo_second = halo_of(2)
    table_second = block_table(
        block_cols, product_cols, own_targets, (row_place - 2) * row_count, order_total,
        fill_count, len(halo_second) * row_count * fill_count,
    )
    return block_products(table_second, square_rows, halo_second, own=square)


def solution(mesh):
    placed = (P(("row", "col"), "depth", None, None), P(), P(("row", "col"), None))
    return jax.shard_map(
        local,
        mesh=mesh,
        in_specs=placed,
        out_specs=P(("row", "col"), "depth", None, None),
        check_vma=False,
    )
```

```python
import functools

import jax
import jax.numpy as jnp
from jax import lax
from jax.experimental import pallas as pl
from jax.experimental.pallas import tpu as pltpu
from jax.sharding import PartitionSpec as P


def shifted(value, axis, steps):
    count = lax.axis_size(axis)
    pairs = [(source, (source + steps) % count) for source in range(count)]
    return lax.ppermute(value, axis, pairs)


def block_table(block_cols, rows, targets, start_row, order_total, fill_count, miss):
    cols_of = block_cols[rows]
    matches = cols_of[:, None, :, :] == targets[:, :, None, None]
    has_match = jnp.any(matches, axis=3)
    slot_ids = jnp.arange(fill_count, dtype=jnp.int32)[None, None, None, :]
    position = jnp.sum(jnp.where(matches, slot_ids, 0), axis=3)
    local_rows = (rows - start_row) % order_total
    flat = local_rows[:, None, :] * fill_count + position
    flat = jnp.clip(flat, 0, miss)
    flat = jnp.where(has_match, flat, miss).astype(jnp.int32)
    inner = jnp.broadcast_to(jnp.arange(rows.shape[1], dtype=jnp.int32), flat.shape)
    order = jnp.argsort(jnp.logical_not(has_match).astype(jnp.int32), axis=2, stable=True)
    picks = jnp.take_along_axis(flat, order, axis=2)
    inners = jnp.take_along_axis(inner, order, axis=2)
    counts = jnp.sum(has_match.astype(jnp.int32), axis=2)
    return picks, inners, counts


def product_kernel(n_out, n_inner, n_pieces, final, idx_ref, inner_ref, count_ref, left_ref, *rest):
    pieces = rest[:n_pieces]
    rest = rest[n_pieces:]
    if final:
        own_ref, out_ref, halo, sems = rest
    else:
        out_ref, halo, sems = rest
    edge = left_ref.shape[-1]
    span = pieces[0].shape[0]
    copies = [
        pltpu.make_async_copy(piece, halo.at[pl.ds(k * span, span)], sems.at[k])
        for k, piece in enumerate(pieces)
    ]
    for copy in copies:
        copy.start()
    for copy in copies:
        copy.wait()

    def item_body(item, carry):
        row = item // n_out
        col = item % n_out
        base = item * n_inner

        def inner_body(k, acc):
            pick = idx_ref[base + k]
            slot = inner_ref[base + k]
            return acc + jnp.dot(
                left_ref[row, slot], halo[pick], preferred_element_type=jnp.float32
            )

        acc = lax.fori_loop(
            0, count_ref[item], inner_body, jnp.zeros((edge, edge), jnp.float32)
        )
        if final:
            value = 3.0 * own_ref[row, col].astype(jnp.float32) - 2.0 * acc
        else:
            value = acc
        out_ref[row, col] = value.astype(out_ref.dtype)
        return carry

    lax.fori_loop(0, left_ref.shape[0] * n_out, item_body, 0)


def block_products(table, left, pieces, own=None):
    picks, inners, counts = table
    rows, n_inner, edge = left.shape[0], left.shape[1], left.shape[2]
    n_out = picks.shape[1]
    final = own is not None
    flat_pieces = [piece.reshape(-1, edge, edge) for piece in pieces]
    span = flat_pieces[0].shape[0]
    tables = [picks.reshape(-1), inners.reshape(-1), counts.reshape(-1)]
    operands = tables + [left] + flat_pieces + ([own] if final else [])
    vmem = pl.BlockSpec(memory_space=pltpu.VMEM)
    smem = pl.BlockSpec(memory_space=pltpu.SMEM)
    anywhere = pl.BlockSpec(memory_space=pl.ANY)
    in_specs = [smem] * 3 + [vmem] + [anywhere] * len(pieces)
    in_specs += [vmem] if final else []
    flops = rows * n_out * n_inner * edge ** 3
    moved = sum(int(x.size) * x.dtype.itemsize for x in operands) + rows * n_out * edge * edge * 2
    return pl.pallas_call(
        functools.partial(product_kernel, n_out, n_inner, len(pieces), final),
        out_shape=jax.ShapeDtypeStruct((rows, n_out, edge, edge), jnp.bfloat16),
        in_specs=in_specs,
        out_specs=vmem,
        scratch_shapes=[
            pltpu.VMEM((len(pieces) * span, edge, edge), left.dtype),
            pltpu.SemaphoreType.DMA((len(pieces),)),
        ],
        compiler_params=pltpu.CompilerParams(vmem_limit_bytes=62 * 1024 * 1024),
        cost_estimate=pl.CostEstimate(flops=flops, transcendentals=0, bytes_accessed=moved),
    )(*operands)


def local(blocks, block_cols, product_cols):
    row_count = blocks.shape[0]
    block_edge = blocks.shape[2]
    fill_count = block_cols.shape[1]
    order_total = row_count * lax.axis_size(("row", "col"))
    row_place = lax.axis_index(("row", "col"))
    depth_index = lax.axis_index("depth")
    depth_count = lax.axis_size("depth")
    target_share = product_cols.shape[1] // depth_count

    full_rows = lax.all_gather(blocks, "depth", axis=1, tiled=True)
    near = {0: full_rows}
    near[1] = shifted(full_rows, ("row", "col"), 1)
    near[-1] = shifted(full_rows, ("row", "col"), -1)
    near[2] = shifted(near[1], ("row", "col"), 1)
    near[-2] = shifted(near[-1], ("row", "col"), -1)

    def halo_of(reach):
        return [near[offset] for offset in range(reach, -reach - 1, -1)]

    own_cols = lax.dynamic_slice_in_dim(block_cols, row_place * row_count, row_count, 0)
    own_targets = lax.dynamic_slice_in_dim(
        product_cols, depth_index * target_share, target_share, 1
    )

    halo_first = halo_of(1)
    table_first = block_table(
        block_cols, own_cols, own_targets, (row_place - 1) * row_count, order_total,
        fill_count, len(halo_first) * row_count * fill_count,
    )
    square = block_products(table_first, full_rows, halo_first)

    square_rows = lax.all_gather(square, "depth", axis=1, tiled=True)
    halo_second = halo_of(2)
    table_second = block_table(
        block_cols, product_cols, own_targets, (row_place - 2) * row_count, order_total,
        fill_count, len(halo_second) * row_count * fill_count,
    )
    return block_products(table_second, square_rows, halo_second, own=square)


def solution(mesh):
    placed = (P(("row", "col"), "depth", None, None), P(), P(("row", "col"), None))
    return jax.shard_map(
        local,
        mesh=mesh,
        in_specs=placed,
        out_specs=P(("row", "col"), "depth", None, None),
        check_vma=False,
    )
```

```python
import functools

import jax
import jax.numpy as jnp
from jax import lax
from jax.experimental import pallas as pl
from jax.experimental.pallas import tpu as pltpu
from jax.sharding import PartitionSpec as P


def shifted(value, axis, steps):
    count = lax.axis_size(axis)
    pairs = [(source, (source + steps) % count) for source in range(count)]
    return lax.ppermute(value, axis, pairs)


def block_table(block_cols, rows, targets, start_row, order_total, fill_count, miss):
    cols_of = block_cols[rows]
    matches = cols_of[:, None, :, :] == targets[:, :, None, None]
    has_match = jnp.any(matches, axis=3)
    slot_ids = jnp.arange(fill_count, dtype=jnp.int32)[None, None, None, :]
    position = jnp.sum(jnp.where(matches, slot_ids, 0), axis=3)
    local_rows = (rows - start_row) % order_total
    flat = local_rows[:, None, :] * fill_count + position
    flat = jnp.clip(flat, 0, miss)
    return jnp.where(has_match, flat, miss).astype(jnp.int32)


def product_kernel(n_out, n_inner, n_pieces, final, idx_ref, left_ref, *rest):
    pieces = rest[:n_pieces]
    rest = rest[n_pieces:]
    if final:
        own_ref, out_ref, halo, lcat, rcat, sems = rest
    else:
        out_ref, halo, lcat, rcat, sems = rest
    edge = left_ref.shape[-1]
    span = pieces[0].shape[0]
    copies = [
        pltpu.make_async_copy(piece, halo.at[pl.ds(k * span, span)], sems.at[k])
        for k, piece in enumerate(pieces)
    ]
    for copy in copies:
        copy.start()
    halo[n_pieces * span] = jnp.zeros((edge, edge), halo.dtype)
    for copy in copies:
        copy.wait()

    def row_body(row, carry):
        for inner in range(n_inner):
            lcat[:, inner * edge:(inner + 1) * edge] = left_ref[row, inner]

        def col_body(col, carry):
            item = row * n_out + col
            for inner in range(n_inner):
                pick = idx_ref[item * n_inner + inner]
                rcat[inner * edge:(inner + 1) * edge, :] = halo[pick]
            acc = jnp.dot(lcat[...], rcat[...], preferred_element_type=jnp.float32)
            if final:
                value = 3.0 * own_ref[row, col].astype(jnp.float32) - 2.0 * acc
            else:
                value = acc
            out_ref[row, col] = value.astype(out_ref.dtype)
            return carry

        return lax.fori_loop(0, n_out, col_body, carry)

    lax.fori_loop(0, left_ref.shape[0], row_body, 0)


def block_products(table, left, pieces, own=None):
    rows, n_inner, edge = left.shape[0], left.shape[1], left.shape[2]
    n_out = table.shape[1]
    final = own is not None
    flat_pieces = [piece.reshape(-1, edge, edge) for piece in pieces]
    span = flat_pieces[0].shape[0]
    operands = [table.reshape(-1), left] + flat_pieces + ([own] if final else [])
    vmem = pl.BlockSpec(memory_space=pltpu.VMEM)
    anywhere = pl.BlockSpec(memory_space=pl.ANY)
    in_specs = [pl.BlockSpec(memory_space=pltpu.SMEM), vmem] + [anywhere] * len(pieces)
    in_specs += [vmem] if final else []
    flops = 2 * rows * n_out * n_inner * edge ** 3
    moved = sum(int(x.size) * x.dtype.itemsize for x in operands) + rows * n_out * edge * edge * 2
    return pl.pallas_call(
        functools.partial(product_kernel, n_out, n_inner, len(pieces), final),
        out_shape=jax.ShapeDtypeStruct((rows, n_out, edge, edge), jnp.bfloat16),
        in_specs=in_specs,
        out_specs=vmem,
        scratch_shapes=[
            pltpu.VMEM((len(pieces) * span + 1, edge, edge), left.dtype),
            pltpu.VMEM((edge, n_inner * edge), left.dtype),
            pltpu.VMEM((n_inner * edge, edge), left.dtype),
            pltpu.SemaphoreType.DMA((len(pieces),)),
        ],
        compiler_params=pltpu.CompilerParams(vmem_limit_bytes=62 * 1024 * 1024),
        cost_estimate=pl.CostEstimate(flops=flops, transcendentals=0, bytes_accessed=moved),
    )(*operands)


MESH = pl.DeviceIdType.MESH


def square_kernel(n_out, n_inner, n_pieces, idx_ref, left_ref, *rest):
    pieces = rest[:n_pieces]
    out_ref, spread_ref, halo, lcat, rcat, sems, send_sems, recv_sems = rest[n_pieces:]
    edge = left_ref.shape[-1]
    span = pieces[0].shape[0]
    row_at = lax.axis_index("row")
    col_at = lax.axis_index("col")
    depth_at = lax.axis_index("depth")
    depth_count = lax.axis_size("depth")
    peers = [lax.rem(depth_at + k, depth_count) for k in range(depth_count)]

    barrier = pltpu.get_barrier_semaphore()
    for k in range(1, depth_count):
        pl.semaphore_signal(
            barrier, inc=1, device_id=(row_at, col_at, peers[k]), device_id_type=MESH
        )
    pl.semaphore_wait(barrier, depth_count - 1)

    copies = [
        pltpu.make_async_copy(piece, halo.at[pl.ds(k * span, span)], sems.at[k])
        for k, piece in enumerate(pieces)
    ]
    for copy in copies:
        copy.start()
    halo[n_pieces * span] = jnp.zeros((edge, edge), halo.dtype)
    for copy in copies:
        copy.wait()

    def spread(row, k):
        target = spread_ref.at[row, pl.ds(depth_at * n_out, n_out)]
        if k == 0:
            return pltpu.make_async_copy(out_ref.at[row], target, send_sems.at[row, 0])
        return pltpu.make_async_remote_copy(
            src_ref=out_ref.at[row],
            dst_ref=target,
            send_sem=send_sems.at[row, k],
            recv_sem=recv_sems.at[row, k],
            device_id=(row_at, col_at, peers[k]),
            device_id_type=MESH,
        )

    def row_body(row, carry):
        for inner in range(n_inner):
            lcat[:, inner * edge:(inner + 1) * edge] = left_ref[row, inner]

        def col_body(col, carry):
            item = row * n_out + col
            for inner in range(n_inner):
                pick = idx_ref[item * n_inner + inner]
                rcat[inner * edge:(inner + 1) * edge, :] = halo[pick]
            acc = jnp.dot(lcat[...], rcat[...], preferred_element_type=jnp.float32)
            out_ref[row, col] = acc.astype(out_ref.dtype)
            return carry

        carry = lax.fori_loop(0, n_out, col_body, carry)
        for k in range(depth_count):
            spread(row, k).start()
        return carry

    lax.fori_loop(0, left_ref.shape[0], row_body, 0)
    for row in range(left_ref.shape[0]):
        spread(row, 0).wait()
        for k in range(1, depth_count):
            spread(row, k).wait()


def square_products(table, left, pieces, depth_count):
    rows, n_inner, edge = left.shape[0], left.shape[1], left.shape[2]
    n_out = table.shape[1]
    flat_pieces = [piece.reshape(-1, edge, edge) for piece in pieces]
    span = flat_pieces[0].shape[0]
    operands = [table.reshape(-1), left] + flat_pieces
    vmem = pl.BlockSpec(memory_space=pltpu.VMEM)
    anywhere = pl.BlockSpec(memory_space=pl.ANY)
    in_specs = [pl.BlockSpec(memory_space=pltpu.SMEM), vmem] + [anywhere] * len(pieces)
    flops = 2 * rows * n_out * n_inner * edge ** 3
    moved = sum(int(x.size) * x.dtype.itemsize for x in operands) + rows * n_out * edge * edge * 8
    return pl.pallas_call(
        functools.partial(square_kernel, n_out, n_inner, len(pieces)),
        out_shape=(
            jax.ShapeDtypeStruct((rows, n_out, edge, edge), jnp.bfloat16),
            jax.ShapeDtypeStruct((rows, depth_count * n_out, edge, edge), jnp.bfloat16),
        ),
        in_specs=in_specs,
        out_specs=(vmem, anywhere),
        scratch_shapes=[
            pltpu.VMEM((len(pieces) * span + 1, edge, edge), left.dtype),
            pltpu.VMEM((edge, n_inner * edge), left.dtype),
            pltpu.VMEM((n_inner * edge, edge), left.dtype),
            pltpu.SemaphoreType.DMA((len(pieces),)),
            pltpu.SemaphoreType.DMA((rows, depth_count)),
            pltpu.SemaphoreType.DMA((rows, depth_count)),
        ],
        compiler_params=pltpu.CompilerParams(
            vmem_limit_bytes=62 * 1024 * 1024, collective_id=0, has_side_effects=True
        ),
        cost_estimate=pl.CostEstimate(flops=flops, transcendentals=0, bytes_accessed=moved),
    )(*operands)


def local(blocks, block_cols, product_cols):
    row_count = blocks.shape[0]
    block_edge = blocks.shape[2]
    fill_count = block_cols.shape[1]
    order_total = row_count * lax.axis_size(("row", "col"))
    row_place = lax.axis_index(("row", "col"))
    depth_index = lax.axis_index("depth")
    depth_count = lax.axis_size("depth")
    target_share = product_cols.shape[1] // depth_count

    full_rows = lax.all_gather(blocks, "depth", axis=1, tiled=True)
    near = {0: full_rows}
    near[1] = shifted(full_rows, ("row", "col"), 1)
    near[-1] = shifted(full_rows, ("row", "col"), -1)
    near[2] = shifted(near[1], ("row", "col"), 1)
    near[-2] = shifted(near[-1], ("row", "col"), -1)

    def halo_of(reach):
        return [near[offset] for offset in range(reach, -reach - 1, -1)]

    own_cols = lax.dynamic_slice_in_dim(block_cols, row_place * row_count, row_count, 0)
    own_targets = lax.dynamic_slice_in_dim(
        product_cols, depth_index * target_share, target_share, 1
    )

    halo_first = halo_of(1)
    table_first = block_table(
        block_cols, own_cols, own_targets, (row_place - 1) * row_count, order_total,
        fill_count, len(halo_first) * row_count * fill_count,
    )
    square, square_rows = square_products(table_first, full_rows, halo_first, depth_count)
    halo_second = halo_of(2)
    table_second = block_table(
        block_cols, product_cols, own_targets, (row_place - 2) * row_count, order_total,
        fill_count, len(halo_second) * row_count * fill_count,
    )
    return block_products(table_second, square_rows, halo_second, own=square)


def solution(mesh):
    placed = (P(("row", "col"), "depth", None, None), P(), P(("row", "col"), None))
    return jax.shard_map(
        local,
        mesh=mesh,
        in_specs=placed,
        out_specs=P(("row", "col"), "depth", None, None),
        check_vma=False,
    )
```

```python
import functools

import jax
import jax.numpy as jnp
from jax import lax
from jax.experimental import pallas as pl
from jax.experimental.pallas import tpu as pltpu
from jax.sharding import PartitionSpec as P


def shifted(value, axis, steps):
    count = lax.axis_size(axis)
    pairs = [(source, (source + steps) % count) for source in range(count)]
    return lax.ppermute(value, axis, pairs)


def block_table(block_cols, rows, targets, start_row, order_total, fill_count, miss):
    cols_of = block_cols[rows]
    matches = cols_of[:, None, :, :] == targets[:, :, None, None]
    has_match = jnp.any(matches, axis=3)
    slot_ids = jnp.arange(fill_count, dtype=jnp.int32)[None, None, None, :]
    position = jnp.sum(jnp.where(matches, slot_ids, 0), axis=3)
    local_rows = (rows - start_row) % order_total
    flat = local_rows[:, None, :] * fill_count + position
    flat = jnp.clip(flat, 0, miss)
    return jnp.where(has_match, flat, miss).astype(jnp.int32)


def product_kernel(n_out, n_inner, n_pieces, final, idx_ref, left_ref, *rest):
    pieces = rest[:n_pieces]
    rest = rest[n_pieces:]
    if final:
        own_ref, out_ref, halo, lcat, rcat, sems = rest
    else:
        out_ref, halo, lcat, rcat, sems = rest
    edge = left_ref.shape[-1]
    span = pieces[0].shape[0]
    copies = [
        pltpu.make_async_copy(piece, halo.at[pl.ds(k * span, span)], sems.at[k])
        for k, piece in enumerate(pieces)
    ]
    for copy in copies:
        copy.start()
    halo[n_pieces * span] = jnp.zeros((edge, edge), halo.dtype)
    for copy in copies:
        copy.wait()

    def row_body(row, carry):
        for inner in range(n_inner):
            lcat[:, inner * edge:(inner + 1) * edge] = left_ref[row, inner]

        def col_body(col, carry):
            item = row * n_out + col
            for inner in range(n_inner):
                pick = idx_ref[item * n_inner + inner]
                rcat[inner * edge:(inner + 1) * edge, :] = halo[pick]
            acc = jnp.dot(lcat[...], rcat[...], preferred_element_type=jnp.float32)
            if final:
                value = 3.0 * own_ref[row, col].astype(jnp.float32) - 2.0 * acc
            else:
                value = acc
            out_ref[row, col] = value.astype(out_ref.dtype)
            return carry

        return lax.fori_loop(0, n_out, col_body, carry)

    lax.fori_loop(0, left_ref.shape[0], row_body, 0)


def block_products(table, left, pieces, own=None):
    rows, n_inner, edge = left.shape[0], left.shape[1], left.shape[2]
    n_out = table.shape[1]
    final = own is not None
    flat_pieces = [piece.reshape(-1, edge, edge) for piece in pieces]
    span = flat_pieces[0].shape[0]
    operands = [table.reshape(-1), left] + flat_pieces + ([own] if final else [])
    vmem = pl.BlockSpec(memory_space=pltpu.VMEM)
    anywhere = pl.BlockSpec(memory_space=pl.ANY)
    in_specs = [pl.BlockSpec(memory_space=pltpu.SMEM), vmem] + [anywhere] * len(pieces)
    in_specs += [vmem] if final else []
    flops = 2 * rows * n_out * n_inner * edge ** 3
    moved = sum(int(x.size) * x.dtype.itemsize for x in operands) + rows * n_out * edge * edge * 2
    return pl.pallas_call(
        functools.partial(product_kernel, n_out, n_inner, len(pieces), final),
        out_shape=jax.ShapeDtypeStruct((rows, n_out, edge, edge), jnp.bfloat16),
        in_specs=in_specs,
        out_specs=vmem,
        scratch_shapes=[
            pltpu.VMEM((len(pieces) * span + 1, edge, edge), left.dtype),
            pltpu.VMEM((edge, n_inner * edge), left.dtype),
            pltpu.VMEM((n_inner * edge, edge), left.dtype),
            pltpu.SemaphoreType.DMA((len(pieces),)),
        ],
        compiler_params=pltpu.CompilerParams(vmem_limit_bytes=62 * 1024 * 1024),
        cost_estimate=pl.CostEstimate(flops=flops, transcendentals=0, bytes_accessed=moved),
    )(*operands)


MESH = pl.DeviceIdType.MESH


def square_kernel(n_own, n_inner, n_pieces, idx_ref, left_ref, *rest):
    pieces = rest[:n_pieces]
    out_ref, spread_ref, halo, lcat, rcat, sems, send_sems, recv_sems, keep_sems = rest[
        n_pieces:
    ]
    edge = left_ref.shape[-1]
    span = pieces[0].shape[0]
    row_count = left_ref.shape[0]
    row_at = lax.axis_index("row")
    col_at = lax.axis_index("col")
    depth_at = lax.axis_index("depth")
    depth_count = lax.axis_size("depth")
    ahead = lax.rem(depth_at + 1, depth_count)
    behind = lax.rem(depth_at + depth_count - 1, depth_count)
    across = lax.rem(depth_at + 2, depth_count)

    barrier = pltpu.get_barrier_semaphore()
    for peer in (ahead, behind):
        pl.semaphore_signal(
            barrier, inc=1, device_id=(row_at, col_at, peer), device_id_type=MESH
        )
    pl.semaphore_wait(barrier, 2)

    copies = [
        pltpu.make_async_copy(piece, halo.at[pl.ds(k * span, span)], sems.at[k])
        for k, piece in enumerate(pieces)
    ]
    for copy in copies:
        copy.start()
    halo[n_pieces * span] = jnp.zeros((edge, edge), halo.dtype)
    for copy in copies:
        copy.wait()

    def spread(row, k):
        source = out_ref.at[row, pl.ds(0, n_own)]
        target = spread_ref.at[row, pl.ds(depth_at * n_own, n_own)]
        if k == 0:
            return pltpu.make_async_copy(source, target, send_sems.at[row, 0])
        return pltpu.make_async_remote_copy(
            src_ref=source,
            dst_ref=target,
            send_sem=send_sems.at[row, k],
            recv_sem=recv_sems.at[row, k],
            device_id=(row_at, col_at, ahead if k == 1 else behind),
            device_id_type=MESH,
        )

    def keep(row):
        return pltpu.make_async_copy(
            out_ref.at[row, pl.ds(n_own, n_own)],
            spread_ref.at[row, pl.ds(across * n_own, n_own)],
            keep_sems.at[row],
        )

    def products(row, first):
        for inner in range(n_inner):
            lcat[:, inner * edge:(inner + 1) * edge] = left_ref[row, inner]

        def col_body(col, carry):
            item = row * 2 * n_own + col
            for inner in range(n_inner):
                pick = idx_ref[item * n_inner + inner]
                rcat[inner * edge:(inner + 1) * edge, :] = halo[pick]
            acc = jnp.dot(lcat[...], rcat[...], preferred_element_type=jnp.float32)
            out_ref[row, col] = acc.astype(out_ref.dtype)
            return carry

        lax.fori_loop(first, first + n_own, col_body, 0)

    def own_body(row, carry):
        products(row, 0)
        for k in range(3):
            spread(row, k).start()
        return carry

    def across_body(row, carry):
        products(row, n_own)
        keep(row).start()
        return carry

    lax.fori_loop(0, row_count, own_body, 0)
    lax.fori_loop(0, row_count, across_body, 0)
    for row in range(row_count):
        for k in range(3):
            spread(row, k).wait()
        keep(row).wait()


def square_products(table, left, pieces, depth_count):
    rows, n_inner, edge = left.shape[0], left.shape[1], left.shape[2]
    n_own = table.shape[1] // 2
    flat_pieces = [piece.reshape(-1, edge, edge) for piece in pieces]
    span = flat_pieces[0].shape[0]
    operands = [table.reshape(-1), left] + flat_pieces
    vmem = pl.BlockSpec(memory_space=pltpu.VMEM)
    anywhere = pl.BlockSpec(memory_space=pl.ANY)
    in_specs = [pl.BlockSpec(memory_space=pltpu.SMEM), vmem] + [anywhere] * len(pieces)
    flops = 2 * rows * 2 * n_own * n_inner * edge ** 3
    moved = sum(int(x.size) * x.dtype.itemsize for x in operands) + rows * n_own * edge * edge * 10
    return pl.pallas_call(
        functools.partial(square_kernel, n_own, n_inner, len(pieces)),
        out_shape=(
            jax.ShapeDtypeStruct((rows, 2 * n_own, edge, edge), jnp.bfloat16),
            jax.ShapeDtypeStruct((rows, depth_count * n_own, edge, edge), jnp.bfloat16),
        ),
        in_specs=in_specs,
        out_specs=(vmem, anywhere),
        scratch_shapes=[
            pltpu.VMEM((len(pieces) * span + 1, edge, edge), left.dtype),
            pltpu.VMEM((edge, n_inner * edge), left.dtype),
            pltpu.VMEM((n_inner * edge, edge), left.dtype),
            pltpu.SemaphoreType.DMA((len(pieces),)),
            pltpu.SemaphoreType.DMA((rows, 3)),
            pltpu.SemaphoreType.DMA((rows, 3)),
            pltpu.SemaphoreType.DMA((rows,)),
        ],
        compiler_params=pltpu.CompilerParams(
            vmem_limit_bytes=62 * 1024 * 1024, collective_id=0, has_side_effects=True
        ),
        cost_estimate=pl.CostEstimate(flops=flops, transcendentals=0, bytes_accessed=moved),
    )(*operands)


def local(blocks, block_cols, product_cols):
    row_count = blocks.shape[0]
    block_edge = blocks.shape[2]
    fill_count = block_cols.shape[1]
    order_total = row_count * lax.axis_size(("row", "col"))
    row_place = lax.axis_index(("row", "col"))
    depth_index = lax.axis_index("depth")
    depth_count = lax.axis_size("depth")
    target_share = product_cols.shape[1] // depth_count

    full_rows = lax.all_gather(blocks, "depth", axis=1, tiled=True)
    near = {0: full_rows}
    near[1] = shifted(full_rows, ("row", "col"), 1)
    near[-1] = shifted(full_rows, ("row", "col"), -1)
    near[2] = shifted(near[1], ("row", "col"), 1)
    near[-2] = shifted(near[-1], ("row", "col"), -1)

    def halo_of(reach):
        return [near[offset] for offset in range(reach, -reach - 1, -1)]

    own_cols = lax.dynamic_slice_in_dim(block_cols, row_place * row_count, row_count, 0)
    own_targets = lax.dynamic_slice_in_dim(
        product_cols, depth_index * target_share, target_share, 1
    )

    across_targets = lax.dynamic_slice_in_dim(
        product_cols, ((depth_index + 2) % depth_count) * target_share, target_share, 1
    )
    halo_first = halo_of(1)
    table_first = block_table(
        block_cols, own_cols, jnp.concatenate([own_targets, across_targets], axis=1), (row_place - 1) * row_count, order_total,
        fill_count, len(halo_first) * row_count * fill_count,
    )
    square, square_rows = square_products(table_first, full_rows, halo_first, depth_count)
    halo_second = halo_of(2)
    table_second = block_table(
        block_cols, product_cols, own_targets, (row_place - 2) * row_count, order_total,
        fill_count, len(halo_second) * row_count * fill_count,
    )
    return block_products(table_second, square_rows, halo_second, own=square)


def solution(mesh):
    placed = (P(("row", "col"), "depth", None, None), P(), P(("row", "col"), None))
    return jax.shard_map(
        local,
        mesh=mesh,
        in_specs=placed,
        out_specs=P(("row", "col"), "depth", None, None),
        check_vma=False,
    )
```

```python
import functools

import jax
import jax.numpy as jnp
from jax import lax
from jax.experimental import pallas as pl
from jax.experimental.pallas import tpu as pltpu
from jax.sharding import PartitionSpec as P


def shifted(value, axis, steps):
    count = lax.axis_size(axis)
    pairs = [(source, (source + steps) % count) for source in range(count)]
    return lax.ppermute(value, axis, pairs)


def block_table(block_cols, rows, targets, start_row, order_total, fill_count, miss):
    cols_of = block_cols[rows]
    matches = cols_of[:, None, :, :] == targets[:, :, None, None]
    has_match = jnp.any(matches, axis=3)
    slot_ids = jnp.arange(fill_count, dtype=jnp.int32)[None, None, None, :]
    position = jnp.sum(jnp.where(matches, slot_ids, 0), axis=3)
    local_rows = (rows - start_row) % order_total
    flat = local_rows[:, None, :] * fill_count + position
    flat = jnp.clip(flat, 0, miss)
    return jnp.where(has_match, flat, miss).astype(jnp.int32)


def product_kernel(n_out, n_inner, n_pieces, final, idx_ref, left_ref, *rest):
    pieces = rest[:n_pieces]
    rest = rest[n_pieces:]
    if final:
        own_ref, out_ref, halo, lcat, rcat, sems = rest
    else:
        out_ref, halo, lcat, rcat, sems = rest
    edge = left_ref.shape[-1]
    span = pieces[0].shape[0]
    copies = [
        pltpu.make_async_copy(piece, halo.at[pl.ds(k * span, span)], sems.at[k])
        for k, piece in enumerate(pieces)
    ]
    for copy in copies:
        copy.start()
    halo[n_pieces * span] = jnp.zeros((edge, edge), halo.dtype)
    for copy in copies:
        copy.wait()

    def row_body(row, carry):
        for inner in range(n_inner):
            lcat[:, inner * edge:(inner + 1) * edge] = left_ref[row, inner]

        def col_body(col, carry):
            item = row * n_out + col
            for inner in range(n_inner):
                pick = idx_ref[item * n_inner + inner]
                rcat[inner * edge:(inner + 1) * edge, :] = halo[pick]
            acc = jnp.dot(lcat[...], rcat[...], preferred_element_type=jnp.float32)
            if final:
                value = 3.0 * own_ref[row, col].astype(jnp.float32) - 2.0 * acc
            else:
                value = acc
            out_ref[row, col] = value.astype(out_ref.dtype)
            return carry

        return lax.fori_loop(0, n_out, col_body, carry)

    lax.fori_loop(0, left_ref.shape[0], row_body, 0)


def block_products(table, left, pieces, own=None):
    rows, n_inner, edge = left.shape[0], left.shape[1], left.shape[2]
    n_out = table.shape[1]
    final = own is not None
    flat_pieces = [piece.reshape(-1, edge, edge) for piece in pieces]
    span = flat_pieces[0].shape[0]
    operands = [table.reshape(-1), left] + flat_pieces + ([own] if final else [])
    vmem = pl.BlockSpec(memory_space=pltpu.VMEM)
    anywhere = pl.BlockSpec(memory_space=pl.ANY)
    in_specs = [pl.BlockSpec(memory_space=pltpu.SMEM), vmem] + [anywhere] * len(pieces)
    in_specs += [vmem] if final else []
    flops = 2 * rows * n_out * n_inner * edge ** 3
    moved = sum(int(x.size) * x.dtype.itemsize for x in operands) + rows * n_out * edge * edge * 2
    return pl.pallas_call(
        functools.partial(product_kernel, n_out, n_inner, len(pieces), final),
        out_shape=jax.ShapeDtypeStruct((rows, n_out, edge, edge), jnp.bfloat16),
        in_specs=in_specs,
        out_specs=vmem,
        scratch_shapes=[
            pltpu.VMEM((len(pieces) * span + 1, edge, edge), left.dtype),
            pltpu.VMEM((edge, n_inner * edge), left.dtype),
            pltpu.VMEM((n_inner * edge, edge), left.dtype),
            pltpu.SemaphoreType.DMA((len(pieces),)),
        ],
        compiler_params=pltpu.CompilerParams(vmem_limit_bytes=62 * 1024 * 1024),
        cost_estimate=pl.CostEstimate(flops=flops, transcendentals=0, bytes_accessed=moved),
    )(*operands)


MESH = pl.DeviceIdType.MESH


def square_kernel(n_own, n_inner, n_pieces, idx_ref, left_ref, *rest):
    pieces = rest[:n_pieces]
    out_ref, spread_ref, halo, lcat, rcat, sems, send_sems, recv_sems, keep_sems = rest[
        n_pieces:
    ]
    edge = left_ref.shape[-1]
    span = pieces[0].shape[0]
    row_count = left_ref.shape[0]
    row_at = lax.axis_index("row")
    col_at = lax.axis_index("col")
    depth_at = lax.axis_index("depth")
    depth_count = lax.axis_size("depth")
    ahead = lax.rem(depth_at + 1, depth_count)
    behind = lax.rem(depth_at + depth_count - 1, depth_count)
    across = lax.rem(depth_at + 2, depth_count)

    barrier = pltpu.get_barrier_semaphore()
    for peer in (ahead, behind):
        pl.semaphore_signal(
            barrier, inc=1, device_id=(row_at, col_at, peer), device_id_type=MESH
        )
    pl.semaphore_wait(barrier, 2)

    copies = [
        pltpu.make_async_copy(piece, halo.at[pl.ds(k * span, span)], sems.at[k])
        for k, piece in enumerate(pieces)
    ]
    for copy in copies:
        copy.start()
    halo[n_pieces * span] = jnp.zeros((edge, edge), halo.dtype)
    for copy in copies:
        copy.wait()

    def spread(row, k):
        source = out_ref.at[row, pl.ds(0, n_own)]
        target = spread_ref.at[row, pl.ds(depth_at * n_own, n_own)]
        if k == 0:
            return pltpu.make_async_copy(source, target, send_sems.at[row, 0])
        return pltpu.make_async_remote_copy(
            src_ref=source,
            dst_ref=target,
            send_sem=send_sems.at[row, k],
            recv_sem=recv_sems.at[row, k],
            device_id=(row_at, col_at, ahead if k == 1 else behind),
            device_id_type=MESH,
        )

    def keep(row):
        return pltpu.make_async_copy(
            out_ref.at[row, pl.ds(n_own, n_own)],
            spread_ref.at[row, pl.ds(across * n_own, n_own)],
            keep_sems.at[row],
        )

    def products(row, first):
        for inner in range(n_inner):
            lcat[:, inner * edge:(inner + 1) * edge] = left_ref[row, inner]

        def col_body(col, carry):
            item = row * 2 * n_own + col
            for inner in range(n_inner):
                pick = idx_ref[item * n_inner + inner]
                rcat[inner * edge:(inner + 1) * edge, :] = halo[pick]
            acc = jnp.dot(lcat[...], rcat[...], preferred_element_type=jnp.float32)
            out_ref[row, col] = acc.astype(out_ref.dtype)
            return carry

        lax.fori_loop(first, first + n_own, col_body, 0)

    def own_body(row, carry):
        products(row, 0)
        for k in range(3):
            spread(row, k).start()
        return carry

    def across_body(row, carry):
        products(row, n_own)
        keep(row).start()
        return carry

    lax.fori_loop(0, row_count, own_body, 0)
    lax.fori_loop(0, row_count, across_body, 0)
    for row in range(row_count):
        for k in range(3):
            spread(row, k).wait()
        keep(row).wait()


def square_products(table, left, pieces, depth_count):
    rows, n_inner, edge = left.shape[0], left.shape[1], left.shape[2]
    n_own = table.shape[1] // 2
    flat_pieces = [piece.reshape(-1, edge, edge) for piece in pieces]
    span = flat_pieces[0].shape[0]
    operands = [table.reshape(-1), left] + flat_pieces
    vmem = pl.BlockSpec(memory_space=pltpu.VMEM)
    anywhere = pl.BlockSpec(memory_space=pl.ANY)
    in_specs = [pl.BlockSpec(memory_space=pltpu.SMEM), vmem] + [anywhere] * len(pieces)
    flops = 2 * rows * 2 * n_own * n_inner * edge ** 3
    moved = sum(int(x.size) * x.dtype.itemsize for x in operands) + rows * n_own * edge * edge * 10
    return pl.pallas_call(
        functools.partial(square_kernel, n_own, n_inner, len(pieces)),
        out_shape=(
            jax.ShapeDtypeStruct((rows, 2 * n_own, edge, edge), jnp.bfloat16),
            jax.ShapeDtypeStruct((rows, depth_count * n_own, edge, edge), jnp.bfloat16),
        ),
        in_specs=in_specs,
        out_specs=(vmem, anywhere),
        scratch_shapes=[
            pltpu.VMEM((len(pieces) * span + 1, edge, edge), left.dtype),
            pltpu.VMEM((edge, n_inner * edge), left.dtype),
            pltpu.VMEM((n_inner * edge, edge), left.dtype),
            pltpu.SemaphoreType.DMA((len(pieces),)),
            pltpu.SemaphoreType.DMA((rows, 3)),
            pltpu.SemaphoreType.DMA((rows, 3)),
            pltpu.SemaphoreType.DMA((rows,)),
        ],
        compiler_params=pltpu.CompilerParams(
            vmem_limit_bytes=62 * 1024 * 1024, collective_id=0, has_side_effects=True
        ),
        cost_estimate=pl.CostEstimate(flops=flops, transcendentals=0, bytes_accessed=moved),
    )(*operands)


def halo_kernel(blocks_ref, full_ref, left_ref, right_ref, send_sems, recv_sems, side_send, side_recv):
    quarter = blocks_ref.shape[1]
    row_at = lax.axis_index("row")
    col_at = lax.axis_index("col")
    depth_at = lax.axis_index("depth")
    col_count = lax.axis_size("col")
    depth_count = lax.axis_size("depth")
    ring = lax.axis_size("row") * col_count
    place = row_at * col_count + col_at
    after = lax.rem(place + 1, ring)
    before = lax.rem(place + ring - 1, ring)
    after_id = (after // col_count, after % col_count, depth_at)
    before_id = (before // col_count, before % col_count, depth_at)
    peer_ids = [
        (row_at, col_at, lax.rem(depth_at + k, depth_count)) for k in range(1, depth_count)
    ]

    barrier = pltpu.get_barrier_semaphore()
    for device in peer_ids + [after_id, before_id]:
        pl.semaphore_signal(barrier, inc=1, device_id=device, device_id_type=MESH)
    pl.semaphore_wait(barrier, depth_count + 1)

    own = pl.ds(depth_at * quarter, quarter)
    local = pltpu.make_async_copy(blocks_ref, full_ref.at[:, own], send_sems.at[0])
    local.start()

    def to_peer(k):
        return pltpu.make_async_remote_copy(
            src_ref=blocks_ref,
            dst_ref=full_ref.at[:, own],
            send_sem=send_sems.at[k],
            recv_sem=recv_sems.at[k],
            device_id=peer_ids[k - 1],
            device_id_type=MESH,
        )

    def to_side(k, source, way):
        origin = lax.rem(depth_at + depth_count - k, depth_count)
        slot = pl.ds(origin * quarter, quarter)
        return pltpu.make_async_remote_copy(
            src_ref=source,
            dst_ref=(left_ref if way == 0 else right_ref).at[:, slot],
            send_sem=side_send.at[way, k],
            recv_sem=side_recv.at[way, k],
            device_id=after_id if way == 0 else before_id,
            device_id_type=MESH,
        )

    for way in range(2):
        to_side(0, blocks_ref, way).start()
    for k in range(1, depth_count):
        to_peer(k).start()
    for k in range(1, depth_count):
        to_peer(k).wait_recv()
        origin = lax.rem(depth_at + depth_count - k, depth_count)
        arrived = full_ref.at[:, pl.ds(origin * quarter, quarter)]
        for way in range(2):
            to_side(k, arrived, way).start()
    local.wait()
    for k in range(1, depth_count):
        to_peer(k).wait_send()
    for k in range(depth_count):
        for way in range(2):
            to_side(k, blocks_ref, way).wait()


def halo_exchange(blocks, depth_count):
    rows, quarter, edge = blocks.shape[0], blocks.shape[1], blocks.shape[2]
    whole = jax.ShapeDtypeStruct((rows, depth_count * quarter, edge, edge), blocks.dtype)
    anywhere = pl.BlockSpec(memory_space=pl.ANY)
    moved = int(blocks.size) * blocks.dtype.itemsize * (3 * depth_count + 3)
    return pl.pallas_call(
        halo_kernel,
        out_shape=(whole, whole, whole),
        in_specs=[anywhere],
        out_specs=(anywhere, anywhere, anywhere),
        scratch_shapes=[
            pltpu.SemaphoreType.DMA((depth_count,)),
            pltpu.SemaphoreType.DMA((depth_count,)),
            pltpu.SemaphoreType.DMA((2, depth_count)),
            pltpu.SemaphoreType.DMA((2, depth_count)),
        ],
        compiler_params=pltpu.CompilerParams(collective_id=1, has_side_effects=True),
        cost_estimate=pl.CostEstimate(flops=0, transcendentals=0, bytes_accessed=moved),
    )(blocks)


def local(blocks, block_cols, product_cols):
    row_count = blocks.shape[0]
    block_edge = blocks.shape[2]
    fill_count = block_cols.shape[1]
    order_total = row_count * lax.axis_size(("row", "col"))
    row_place = lax.axis_index(("row", "col"))
    depth_index = lax.axis_index("depth")
    depth_count = lax.axis_size("depth")
    target_share = product_cols.shape[1] // depth_count

    full_rows, from_before, from_after = halo_exchange(blocks, depth_count)
    near = {0: full_rows, 1: from_before, -1: from_after}
    near[2] = shifted(near[1], ("row", "col"), 1)
    near[-2] = shifted(near[-1], ("row", "col"), -1)

    def halo_of(reach):
        return [near[offset] for offset in range(reach, -reach - 1, -1)]

    own_cols = lax.dynamic_slice_in_dim(block_cols, row_place * row_count, row_count, 0)
    own_targets = lax.dynamic_slice_in_dim(
        product_cols, depth_index * target_share, target_share, 1
    )

    across_targets = lax.dynamic_slice_in_dim(
        product_cols, ((depth_index + 2) % depth_count) * target_share, target_share, 1
    )
    halo_first = halo_of(1)
    table_first = block_table(
        block_cols, own_cols, jnp.concatenate([own_targets, across_targets], axis=1), (row_place - 1) * row_count, order_total,
        fill_count, len(halo_first) * row_count * fill_count,
    )
    square, square_rows = square_products(table_first, full_rows, halo_first, depth_count)
    halo_second = halo_of(2)
    table_second = block_table(
        block_cols, product_cols, own_targets, (row_place - 2) * row_count, order_total,
        fill_count, len(halo_second) * row_count * fill_count,
    )
    return block_products(table_second, square_rows, halo_second, own=square)


def solution(mesh):
    placed = (P(("row", "col"), "depth", None, None), P(), P(("row", "col"), None))
    return jax.shard_map(
        local,
        mesh=mesh,
        in_specs=placed,
        out_specs=P(("row", "col"), "depth", None, None),
        check_vma=False,
    )
```

```python
import functools

import jax
import jax.numpy as jnp
from jax import lax
from jax.experimental import pallas as pl
from jax.experimental.pallas import tpu as pltpu
from jax.sharding import PartitionSpec as P


def shifted(value, axis, steps):
    count = lax.axis_size(axis)
    pairs = [(source, (source + steps) % count) for source in range(count)]
    return lax.ppermute(value, axis, pairs)


def block_table(block_cols, rows, targets, start_row, order_total, fill_count, miss):
    cols_of = block_cols[rows]
    matches = cols_of[:, None, :, :] == targets[:, :, None, None]
    has_match = jnp.any(matches, axis=3)
    slot_ids = jnp.arange(fill_count, dtype=jnp.int32)[None, None, None, :]
    position = jnp.sum(jnp.where(matches, slot_ids, 0), axis=3)
    local_rows = (rows - start_row) % order_total
    flat = local_rows[:, None, :] * fill_count + position
    flat = jnp.clip(flat, 0, miss)
    return jnp.where(has_match, flat, miss).astype(jnp.int32)


def product_kernel(n_out, n_inner, n_pieces, final, idx_ref, left_ref, *rest):
    pieces = rest[:n_pieces]
    rest = rest[n_pieces:]
    if final:
        own_ref, out_ref, halo, lcat, rcat, sems = rest
    else:
        out_ref, halo, lcat, rcat, sems = rest
    edge = left_ref.shape[-1]
    span = pieces[0].shape[0]
    copies = [
        pltpu.make_async_copy(piece, halo.at[pl.ds(k * span, span)], sems.at[k])
        for k, piece in enumerate(pieces)
    ]
    for copy in copies:
        copy.start()
    halo[n_pieces * span] = jnp.zeros((edge, edge), halo.dtype)
    for copy in copies:
        copy.wait()

    def row_body(row, carry):
        for inner in range(n_inner):
            lcat[:, inner * edge:(inner + 1) * edge] = left_ref[row, inner]

        def col_body(pair, carry):
            col = 2 * pair
            for half in range(2):
                item = row * n_out + col + half
                for inner in range(n_inner):
                    pick = idx_ref[item * n_inner + inner]
                    rcat[inner * edge:(inner + 1) * edge, half * edge:(half + 1) * edge] = halo[pick]
            acc = jnp.dot(lcat[...], rcat[...], preferred_element_type=jnp.float32)
            for half in range(2):
                part = acc[:, half * edge:(half + 1) * edge]
                if final:
                    value = 3.0 * own_ref[row, col + half].astype(jnp.float32) - 2.0 * part
                else:
                    value = part
                out_ref[row, col + half] = value.astype(out_ref.dtype)
            return carry

        return lax.fori_loop(0, n_out // 2, col_body, carry)

    lax.fori_loop(0, left_ref.shape[0], row_body, 0)


def block_products(table, left, pieces, own=None):
    rows, n_inner, edge = left.shape[0], left.shape[1], left.shape[2]
    n_out = table.shape[1]
    final = own is not None
    flat_pieces = [piece.reshape(-1, edge, edge) for piece in pieces]
    span = flat_pieces[0].shape[0]
    operands = [table.reshape(-1), left] + flat_pieces + ([own] if final else [])
    vmem = pl.BlockSpec(memory_space=pltpu.VMEM)
    anywhere = pl.BlockSpec(memory_space=pl.ANY)
    in_specs = [pl.BlockSpec(memory_space=pltpu.SMEM), vmem] + [anywhere] * len(pieces)
    in_specs += [vmem] if final else []
    flops = 2 * rows * n_out * n_inner * edge ** 3
    moved = sum(int(x.size) * x.dtype.itemsize for x in operands) + rows * n_out * edge * edge * 2
    return pl.pallas_call(
        functools.partial(product_kernel, n_out, n_inner, len(pieces), final),
        out_shape=jax.ShapeDtypeStruct((rows, n_out, edge, edge), jnp.bfloat16),
        in_specs=in_specs,
        out_specs=vmem,
        scratch_shapes=[
            pltpu.VMEM((len(pieces) * span + 1, edge, edge), left.dtype),
            pltpu.VMEM((edge, n_inner * edge), left.dtype),
            pltpu.VMEM((n_inner * edge, 2 * edge), left.dtype),
            pltpu.SemaphoreType.DMA((len(pieces),)),
        ],
        compiler_params=pltpu.CompilerParams(vmem_limit_bytes=62 * 1024 * 1024),
        cost_estimate=pl.CostEstimate(flops=flops, transcendentals=0, bytes_accessed=moved),
    )(*operands)


MESH = pl.DeviceIdType.MESH


def square_kernel(n_own, n_inner, n_pieces, idx_ref, left_ref, *rest):
    pieces = rest[:n_pieces]
    out_ref, spread_ref, halo, lcat, rcat, sems, send_sems, recv_sems, keep_sems = rest[
        n_pieces:
    ]
    edge = left_ref.shape[-1]
    span = pieces[0].shape[0]
    row_count = left_ref.shape[0]
    row_at = lax.axis_index("row")
    col_at = lax.axis_index("col")
    depth_at = lax.axis_index("depth")
    depth_count = lax.axis_size("depth")
    ahead = lax.rem(depth_at + 1, depth_count)
    behind = lax.rem(depth_at + depth_count - 1, depth_count)
    across = lax.rem(depth_at + 2, depth_count)

    barrier = pltpu.get_barrier_semaphore()
    for peer in (ahead, behind):
        pl.semaphore_signal(
            barrier, inc=1, device_id=(row_at, col_at, peer), device_id_type=MESH
        )
    pl.semaphore_wait(barrier, 2)

    copies = [
        pltpu.make_async_copy(piece, halo.at[pl.ds(k * span, span)], sems.at[k])
        for k, piece in enumerate(pieces)
    ]
    for copy in copies:
        copy.start()
    halo[n_pieces * span] = jnp.zeros((edge, edge), halo.dtype)
    for copy in copies:
        copy.wait()

    def spread(row, k):
        source = out_ref.at[row, pl.ds(0, n_own)]
        target = spread_ref.at[row, pl.ds(depth_at * n_own, n_own)]
        if k == 0:
            return pltpu.make_async_copy(source, target, send_sems.at[row, 0])
        return pltpu.make_async_remote_copy(
            src_ref=source,
            dst_ref=target,
            send_sem=send_sems.at[row, k],
            recv_sem=recv_sems.at[row, k],
            device_id=(row_at, col_at, ahead if k == 1 else behind),
            device_id_type=MESH,
        )

    def keep(row):
        return pltpu.make_async_copy(
            out_ref.at[row, pl.ds(n_own, n_own)],
            spread_ref.at[row, pl.ds(across * n_own, n_own)],
            keep_sems.at[row],
        )

    def products(row, first):
        for inner in range(n_inner):
            lcat[:, inner * edge:(inner + 1) * edge] = left_ref[row, inner]

        def col_body(pair, carry):
            col = first + 2 * pair
            for half in range(2):
                item = row * 2 * n_own + col + half
                for inner in range(n_inner):
                    pick = idx_ref[item * n_inner + inner]
                    rcat[inner * edge:(inner + 1) * edge, half * edge:(half + 1) * edge] = halo[pick]
            acc = jnp.dot(lcat[...], rcat[...], preferred_element_type=jnp.float32)
            for half in range(2):
                out_ref[row, col + half] = acc[:, half * edge:(half + 1) * edge].astype(out_ref.dtype)
            return carry

        lax.fori_loop(0, n_own // 2, col_body, 0)

    def own_body(row, carry):
        products(row, 0)
        for k in range(3):
            spread(row, k).start()
        return carry

    def across_body(row, carry):
        products(row, n_own)
        keep(row).start()
        return carry

    lax.fori_loop(0, row_count, own_body, 0)
    lax.fori_loop(0, row_count, across_body, 0)
    for row in range(row_count):
        for k in range(3):
            spread(row, k).wait()
        keep(row).wait()


def square_products(table, left, pieces, depth_count):
    rows, n_inner, edge = left.shape[0], left.shape[1], left.shape[2]
    n_own = table.shape[1] // 2
    flat_pieces = [piece.reshape(-1, edge, edge) for piece in pieces]
    span = flat_pieces[0].shape[0]
    operands = [table.reshape(-1), left] + flat_pieces
    vmem = pl.BlockSpec(memory_space=pltpu.VMEM)
    anywhere = pl.BlockSpec(memory_space=pl.ANY)
    in_specs = [pl.BlockSpec(memory_space=pltpu.SMEM), vmem] + [anywhere] * len(pieces)
    flops = 2 * rows * 2 * n_own * n_inner * edge ** 3
    moved = sum(int(x.size) * x.dtype.itemsize for x in operands) + rows * n_own * edge * edge * 10
    return pl.pallas_call(
        functools.partial(square_kernel, n_own, n_inner, len(pieces)),
        out_shape=(
            jax.ShapeDtypeStruct((rows, 2 * n_own, edge, edge), jnp.bfloat16),
            jax.ShapeDtypeStruct((rows, depth_count * n_own, edge, edge), jnp.bfloat16),
        ),
        in_specs=in_specs,
        out_specs=(vmem, anywhere),
        scratch_shapes=[
            pltpu.VMEM((len(pieces) * span + 1, edge, edge), left.dtype),
            pltpu.VMEM((edge, n_inner * edge), left.dtype),
            pltpu.VMEM((n_inner * edge, 2 * edge), left.dtype),
            pltpu.SemaphoreType.DMA((len(pieces),)),
            pltpu.SemaphoreType.DMA((rows, 3)),
            pltpu.SemaphoreType.DMA((rows, 3)),
            pltpu.SemaphoreType.DMA((rows,)),
        ],
        compiler_params=pltpu.CompilerParams(
            vmem_limit_bytes=62 * 1024 * 1024, collective_id=0, has_side_effects=True
        ),
        cost_estimate=pl.CostEstimate(flops=flops, transcendentals=0, bytes_accessed=moved),
    )(*operands)


def halo_kernel(blocks_ref, full_ref, left_ref, right_ref, send_sems, recv_sems, side_send, side_recv):
    quarter = blocks_ref.shape[1]
    row_at = lax.axis_index("row")
    col_at = lax.axis_index("col")
    depth_at = lax.axis_index("depth")
    col_count = lax.axis_size("col")
    depth_count = lax.axis_size("depth")
    ring = lax.axis_size("row") * col_count
    place = row_at * col_count + col_at
    after = lax.rem(place + 1, ring)
    before = lax.rem(place + ring - 1, ring)
    after_id = (after // col_count, after % col_count, depth_at)
    before_id = (before // col_count, before % col_count, depth_at)
    peer_ids = [
        (row_at, col_at, lax.rem(depth_at + k, depth_count)) for k in range(1, depth_count)
    ]

    barrier = pltpu.get_barrier_semaphore()
    for device in peer_ids + [after_id, before_id]:
        pl.semaphore_signal(barrier, inc=1, device_id=device, device_id_type=MESH)
    pl.semaphore_wait(barrier, depth_count + 1)

    own = pl.ds(depth_at * quarter, quarter)
    local = pltpu.make_async_copy(blocks_ref, full_ref.at[:, own], send_sems.at[0])
    local.start()

    def to_peer(k):
        return pltpu.make_async_remote_copy(
            src_ref=blocks_ref,
            dst_ref=full_ref.at[:, own],
            send_sem=send_sems.at[k],
            recv_sem=recv_sems.at[k],
            device_id=peer_ids[k - 1],
            device_id_type=MESH,
        )

    def to_side(k, source, way):
        origin = lax.rem(depth_at + depth_count - k, depth_count)
        slot = pl.ds(origin * quarter, quarter)
        return pltpu.make_async_remote_copy(
            src_ref=source,
            dst_ref=(left_ref if way == 0 else right_ref).at[:, slot],
            send_sem=side_send.at[way, k],
            recv_sem=side_recv.at[way, k],
            device_id=after_id if way == 0 else before_id,
            device_id_type=MESH,
        )

    for way in range(2):
        to_side(0, blocks_ref, way).start()
    for k in range(1, depth_count):
        to_peer(k).start()
    for k in range(1, depth_count):
        to_peer(k).wait_recv()
        origin = lax.rem(depth_at + depth_count - k, depth_count)
        arrived = full_ref.at[:, pl.ds(origin * quarter, quarter)]
        for way in range(2):
            to_side(k, arrived, way).start()
    local.wait()
    for k in range(1, depth_count):
        to_peer(k).wait_send()
    for k in range(depth_count):
        for way in range(2):
            to_side(k, blocks_ref, way).wait()


def halo_exchange(blocks, depth_count):
    rows, quarter, edge = blocks.shape[0], blocks.shape[1], blocks.shape[2]
    whole = jax.ShapeDtypeStruct((rows, depth_count * quarter, edge, edge), blocks.dtype)
    anywhere = pl.BlockSpec(memory_space=pl.ANY)
    moved = int(blocks.size) * blocks.dtype.itemsize * (3 * depth_count + 3)
    return pl.pallas_call(
        halo_kernel,
        out_shape=(whole, whole, whole),
        in_specs=[anywhere],
        out_specs=(anywhere, anywhere, anywhere),
        scratch_shapes=[
            pltpu.SemaphoreType.DMA((depth_count,)),
            pltpu.SemaphoreType.DMA((depth_count,)),
            pltpu.SemaphoreType.DMA((2, depth_count)),
            pltpu.SemaphoreType.DMA((2, depth_count)),
        ],
        compiler_params=pltpu.CompilerParams(collective_id=1, has_side_effects=True),
        cost_estimate=pl.CostEstimate(flops=0, transcendentals=0, bytes_accessed=moved),
    )(blocks)


def local(blocks, block_cols, product_cols):
    row_count = blocks.shape[0]
    block_edge = blocks.shape[2]
    fill_count = block_cols.shape[1]
    order_total = row_count * lax.axis_size(("row", "col"))
    row_place = lax.axis_index(("row", "col"))
    depth_index = lax.axis_index("depth")
    depth_count = lax.axis_size("depth")
    target_share = product_cols.shape[1] // depth_count

    full_rows, from_before, from_after = halo_exchange(blocks, depth_count)
    near = {0: full_rows, 1: from_before, -1: from_after}
    near[2] = shifted(near[1], ("row", "col"), 1)
    near[-2] = shifted(near[-1], ("row", "col"), -1)

    def halo_of(reach):
        return [near[offset] for offset in range(reach, -reach - 1, -1)]

    own_cols = lax.dynamic_slice_in_dim(block_cols, row_place * row_count, row_count, 0)
    own_targets = lax.dynamic_slice_in_dim(
        product_cols, depth_index * target_share, target_share, 1
    )

    across_targets = lax.dynamic_slice_in_dim(
        product_cols, ((depth_index + 2) % depth_count) * target_share, target_share, 1
    )
    halo_first = halo_of(1)
    table_first = block_table(
        block_cols, own_cols, jnp.concatenate([own_targets, across_targets], axis=1), (row_place - 1) * row_count, order_total,
        fill_count, len(halo_first) * row_count * fill_count,
    )
    square, square_rows = square_products(table_first, full_rows, halo_first, depth_count)
    halo_second = halo_of(2)
    table_second = block_table(
        block_cols, product_cols, own_targets, (row_place - 2) * row_count, order_total,
        fill_count, len(halo_second) * row_count * fill_count,
    )
    return block_products(table_second, square_rows, halo_second, own=square)


def solution(mesh):
    placed = (P(("row", "col"), "depth", None, None), P(), P(("row", "col"), None))
    return jax.shard_map(
        local,
        mesh=mesh,
        in_specs=placed,
        out_specs=P(("row", "col"), "depth", None, None),
        check_vma=False,
    )
```

```python
import functools

import jax
import jax.numpy as jnp
from jax import lax
from jax.experimental import pallas as pl
from jax.experimental.pallas import tpu as pltpu
from jax.sharding import PartitionSpec as P


def shifted(value, axis, steps):
    count = lax.axis_size(axis)
    pairs = [(source, (source + steps) % count) for source in range(count)]
    return lax.ppermute(value, axis, pairs)


def block_table(block_cols, rows, targets, start_row, order_total, fill_count, miss):
    cols_of = block_cols[rows]
    matches = cols_of[:, None, :, :] == targets[:, :, None, None]
    has_match = jnp.any(matches, axis=3)
    slot_ids = jnp.arange(fill_count, dtype=jnp.int32)[None, None, None, :]
    position = jnp.sum(jnp.where(matches, slot_ids, 0), axis=3)
    local_rows = (rows - start_row) % order_total
    flat = local_rows[:, None, :] * fill_count + position
    flat = jnp.clip(flat, 0, miss)
    return jnp.where(has_match, flat, miss).astype(jnp.int32)


def product_kernel(n_out, n_inner, n_pieces, final, idx_ref, left_ref, *rest):
    pieces = rest[:n_pieces]
    rest = rest[n_pieces:]
    if final:
        own_ref, out_ref, halo, lcat, rcat, sems = rest
    else:
        out_ref, halo, lcat, rcat, sems = rest
    edge = left_ref.shape[-1]
    span = pieces[0].shape[0]
    copies = [
        pltpu.make_async_copy(piece, halo.at[pl.ds(k * span, span)], sems.at[k])
        for k, piece in enumerate(pieces)
    ]
    for copy in copies:
        copy.start()
    halo[n_pieces * span] = jnp.zeros((edge, edge), halo.dtype)
    for copy in copies:
        copy.wait()

    def row_body(row, carry):
        for inner in range(n_inner):
            lcat[:, inner * edge:(inner + 1) * edge] = left_ref[row, inner]

        def col_body(pair, carry):
            col = 2 * pair
            for half in range(2):
                item = row * n_out + col + half
                for inner in range(n_inner):
                    pick = idx_ref[item * n_inner + inner]
                    rcat[inner * edge:(inner + 1) * edge, half * edge:(half + 1) * edge] = halo[pick]
            acc = jnp.dot(lcat[...], rcat[...], preferred_element_type=jnp.float32)
            for half in range(2):
                part = acc[:, half * edge:(half + 1) * edge]
                if final:
                    value = 3.0 * own_ref[row, col + half].astype(jnp.float32) - 2.0 * part
                else:
                    value = part
                out_ref[row, col + half] = value.astype(out_ref.dtype)
            return carry

        return lax.fori_loop(0, n_out // 2, col_body, carry)

    lax.fori_loop(0, left_ref.shape[0], row_body, 0)


def block_products(table, left, pieces, own=None):
    rows, n_inner, edge = left.shape[0], left.shape[1], left.shape[2]
    n_out = table.shape[1]
    final = own is not None
    flat_pieces = [piece.reshape(-1, edge, edge) for piece in pieces]
    span = flat_pieces[0].shape[0]
    operands = [table.reshape(-1), left] + flat_pieces + ([own] if final else [])
    vmem = pl.BlockSpec(memory_space=pltpu.VMEM)
    anywhere = pl.BlockSpec(memory_space=pl.ANY)
    in_specs = [pl.BlockSpec(memory_space=pltpu.SMEM), vmem] + [anywhere] * len(pieces)
    in_specs += [vmem] if final else []
    flops = 2 * rows * n_out * n_inner * edge ** 3
    moved = sum(int(x.size) * x.dtype.itemsize for x in operands) + rows * n_out * edge * edge * 2
    return pl.pallas_call(
        functools.partial(product_kernel, n_out, n_inner, len(pieces), final),
        out_shape=jax.ShapeDtypeStruct((rows, n_out, edge, edge), jnp.bfloat16),
        in_specs=in_specs,
        out_specs=vmem,
        scratch_shapes=[
            pltpu.VMEM((len(pieces) * span + 1, edge, edge), left.dtype),
            pltpu.VMEM((edge, n_inner * edge), left.dtype),
            pltpu.VMEM((n_inner * edge, 2 * edge), left.dtype),
            pltpu.SemaphoreType.DMA((len(pieces),)),
        ],
        compiler_params=pltpu.CompilerParams(vmem_limit_bytes=62 * 1024 * 1024),
        cost_estimate=pl.CostEstimate(flops=flops, transcendentals=0, bytes_accessed=moved),
    )(*operands)


MESH = pl.DeviceIdType.MESH


def square_kernel(n_own, n_inner, n_pieces, idx_ref, left_ref, *rest):
    pieces = rest[:n_pieces]
    (out_ref, spread_ref, far_before, far_after, halo, lcat, rcat, sems, send_sems,
     recv_sems, keep_sems, side_send, side_recv) = rest[n_pieces:]
    edge = left_ref.shape[-1]
    span = pieces[0].shape[0]
    row_count = left_ref.shape[0]
    row_at = lax.axis_index("row")
    col_at = lax.axis_index("col")
    depth_at = lax.axis_index("depth")
    depth_count = lax.axis_size("depth")
    ahead = lax.rem(depth_at + 1, depth_count)
    behind = lax.rem(depth_at + depth_count - 1, depth_count)
    across = lax.rem(depth_at + 2, depth_count)

    col_count = lax.axis_size("col")
    ring = lax.axis_size("row") * col_count
    place = row_at * col_count + col_at
    after = lax.rem(place + 1, ring)
    before = lax.rem(place + ring - 1, ring)
    after_id = (after // col_count, after % col_count, depth_at)
    before_id = (before // col_count, before % col_count, depth_at)

    barrier = pltpu.get_barrier_semaphore()
    for device in [(row_at, col_at, ahead), (row_at, col_at, behind), after_id, before_id]:
        pl.semaphore_signal(barrier, inc=1, device_id=device, device_id_type=MESH)
    pl.semaphore_wait(barrier, 4)

    sides = [
        pltpu.make_async_remote_copy(
            src_ref=pieces[0], dst_ref=far_before, send_sem=side_send.at[0],
            recv_sem=side_recv.at[0], device_id=after_id, device_id_type=MESH,
        ),
        pltpu.make_async_remote_copy(
            src_ref=pieces[n_pieces - 1], dst_ref=far_after, send_sem=side_send.at[1],
            recv_sem=side_recv.at[1], device_id=before_id, device_id_type=MESH,
        ),
    ]
    for side in sides:
        side.start()

    copies = [
        pltpu.make_async_copy(piece, halo.at[pl.ds(k * span, span)], sems.at[k])
        for k, piece in enumerate(pieces)
    ]
    for copy in copies:
        copy.start()
    halo[n_pieces * span] = jnp.zeros((edge, edge), halo.dtype)
    for copy in copies:
        copy.wait()

    def spread(row, k):
        source = out_ref.at[row, pl.ds(0, n_own)]
        target = spread_ref.at[row, pl.ds(depth_at * n_own, n_own)]
        if k == 0:
            return pltpu.make_async_copy(source, target, send_sems.at[row, 0])
        return pltpu.make_async_remote_copy(
            src_ref=source,
            dst_ref=target,
            send_sem=send_sems.at[row, k],
            recv_sem=recv_sems.at[row, k],
            device_id=(row_at, col_at, ahead if k == 1 else behind),
            device_id_type=MESH,
        )

    def keep(row):
        return pltpu.make_async_copy(
            out_ref.at[row, pl.ds(n_own, n_own)],
            spread_ref.at[row, pl.ds(across * n_own, n_own)],
            keep_sems.at[row],
        )

    def products(row, first):
        for inner in range(n_inner):
            lcat[:, inner * edge:(inner + 1) * edge] = left_ref[row, inner]

        def col_body(pair, carry):
            col = first + 2 * pair
            for half in range(2):
                item = row * 2 * n_own + col + half
                for inner in range(n_inner):
                    pick = idx_ref[item * n_inner + inner]
                    rcat[inner * edge:(inner + 1) * edge, half * edge:(half + 1) * edge] = halo[pick]
            acc = jnp.dot(lcat[...], rcat[...], preferred_element_type=jnp.float32)
            for half in range(2):
                out_ref[row, col + half] = acc[:, half * edge:(half + 1) * edge].astype(out_ref.dtype)
            return carry

        lax.fori_loop(0, n_own // 2, col_body, 0)

    def own_body(row, carry):
        products(row, 0)
        for k in range(3):
            spread(row, k).start()
        return carry

    def across_body(row, carry):
        products(row, n_own)
        keep(row).start()
        return carry

    lax.fori_loop(0, row_count, own_body, 0)
    lax.fori_loop(0, row_count, across_body, 0)
    for row in range(row_count):
        for k in range(3):
            spread(row, k).wait()
        keep(row).wait()
    for side in sides:
        side.wait()


def square_products(table, left, pieces, depth_count):
    rows, n_inner, edge = left.shape[0], left.shape[1], left.shape[2]
    n_own = table.shape[1] // 2
    flat_pieces = [piece.reshape(-1, edge, edge) for piece in pieces]
    span = flat_pieces[0].shape[0]
    operands = [table.reshape(-1), left] + flat_pieces
    vmem = pl.BlockSpec(memory_space=pltpu.VMEM)
    anywhere = pl.BlockSpec(memory_space=pl.ANY)
    in_specs = [pl.BlockSpec(memory_space=pltpu.SMEM), vmem] + [anywhere] * len(pieces)
    flops = 2 * rows * 2 * n_own * n_inner * edge ** 3
    moved = sum(int(x.size) * x.dtype.itemsize for x in operands) + rows * n_own * edge * edge * 10
    return pl.pallas_call(
        functools.partial(square_kernel, n_own, n_inner, len(pieces)),
        out_shape=(
            jax.ShapeDtypeStruct((rows, 2 * n_own, edge, edge), jnp.bfloat16),
            jax.ShapeDtypeStruct((rows, depth_count * n_own, edge, edge), jnp.bfloat16),
            jax.ShapeDtypeStruct(flat_pieces[0].shape, left.dtype),
            jax.ShapeDtypeStruct(flat_pieces[0].shape, left.dtype),
        ),
        in_specs=in_specs,
        out_specs=(vmem, anywhere, anywhere, anywhere),
        scratch_shapes=[
            pltpu.VMEM((len(pieces) * span + 1, edge, edge), left.dtype),
            pltpu.VMEM((edge, n_inner * edge), left.dtype),
            pltpu.VMEM((n_inner * edge, 2 * edge), left.dtype),
            pltpu.SemaphoreType.DMA((len(pieces),)),
            pltpu.SemaphoreType.DMA((rows, 3)),
            pltpu.SemaphoreType.DMA((rows, 3)),
            pltpu.SemaphoreType.DMA((rows,)),
            pltpu.SemaphoreType.DMA((2,)),
            pltpu.SemaphoreType.DMA((2,)),
        ],
        compiler_params=pltpu.CompilerParams(
            vmem_limit_bytes=62 * 1024 * 1024, collective_id=0, has_side_effects=True
        ),
        cost_estimate=pl.CostEstimate(flops=flops, transcendentals=0, bytes_accessed=moved),
    )(*operands)


def halo_kernel(blocks_ref, full_ref, left_ref, right_ref, send_sems, recv_sems, side_send, side_recv):
    quarter = blocks_ref.shape[1]
    row_at = lax.axis_index("row")
    col_at = lax.axis_index("col")
    depth_at = lax.axis_index("depth")
    col_count = lax.axis_size("col")
    depth_count = lax.axis_size("depth")
    ring = lax.axis_size("row") * col_count
    place = row_at * col_count + col_at
    after = lax.rem(place + 1, ring)
    before = lax.rem(place + ring - 1, ring)
    after_id = (after // col_count, after % col_count, depth_at)
    before_id = (before // col_count, before % col_count, depth_at)
    peer_ids = [
        (row_at, col_at, lax.rem(depth_at + k, depth_count)) for k in range(1, depth_count)
    ]

    barrier = pltpu.get_barrier_semaphore()
    for device in peer_ids + [after_id, before_id]:
        pl.semaphore_signal(barrier, inc=1, device_id=device, device_id_type=MESH)
    pl.semaphore_wait(barrier, depth_count + 1)

    own = pl.ds(depth_at * quarter, quarter)
    local = pltpu.make_async_copy(blocks_ref, full_ref.at[:, own], send_sems.at[0])
    local.start()

    def to_peer(k):
        return pltpu.make_async_remote_copy(
            src_ref=blocks_ref,
            dst_ref=full_ref.at[:, own],
            send_sem=send_sems.at[k],
            recv_sem=recv_sems.at[k],
            device_id=peer_ids[k - 1],
            device_id_type=MESH,
        )

    def to_side(k, source, way):
        origin = lax.rem(depth_at + depth_count - k, depth_count)
        slot = pl.ds(origin * quarter, quarter)
        return pltpu.make_async_remote_copy(
            src_ref=source,
            dst_ref=(left_ref if way == 0 else right_ref).at[:, slot],
            send_sem=side_send.at[way, k],
            recv_sem=side_recv.at[way, k],
            device_id=after_id if way == 0 else before_id,
            device_id_type=MESH,
        )

    for way in range(2):
        to_side(0, blocks_ref, way).start()
    for k in range(1, depth_count):
        to_peer(k).start()
    for k in sorted(range(1, depth_count), key=lambda k: min(k, depth_count - k)):
        to_peer(k).wait_recv()
        origin = lax.rem(depth_at + depth_count - k, depth_count)
        arrived = full_ref.at[:, pl.ds(origin * quarter, quarter)]
        for way in range(2):
            to_side(k, arrived, way).start()
    local.wait()
    for k in range(1, depth_count):
        to_peer(k).wait_send()
    for k in range(depth_count):
        for way in range(2):
            to_side(k, blocks_ref, way).wait()


def halo_exchange(blocks, depth_count):
    rows, quarter, edge = blocks.shape[0], blocks.shape[1], blocks.shape[2]
    whole = jax.ShapeDtypeStruct((rows, depth_count * quarter, edge, edge), blocks.dtype)
    anywhere = pl.BlockSpec(memory_space=pl.ANY)
    moved = int(blocks.size) * blocks.dtype.itemsize * (3 * depth_count + 3)
    return pl.pallas_call(
        halo_kernel,
        out_shape=(whole, whole, whole),
        in_specs=[anywhere],
        out_specs=(anywhere, anywhere, anywhere),
        scratch_shapes=[
            pltpu.SemaphoreType.DMA((depth_count,)),
            pltpu.SemaphoreType.DMA((depth_count,)),
            pltpu.SemaphoreType.DMA((2, depth_count)),
            pltpu.SemaphoreType.DMA((2, depth_count)),
        ],
        compiler_params=pltpu.CompilerParams(collective_id=1, has_side_effects=True),
        cost_estimate=pl.CostEstimate(flops=0, transcendentals=0, bytes_accessed=moved),
    )(blocks)


def local(blocks, block_cols, product_cols):
    row_count = blocks.shape[0]
    block_edge = blocks.shape[2]
    fill_count = block_cols.shape[1]
    order_total = row_count * lax.axis_size(("row", "col"))
    row_place = lax.axis_index(("row", "col"))
    depth_index = lax.axis_index("depth")
    depth_count = lax.axis_size("depth")
    target_share = product_cols.shape[1] // depth_count

    full_rows, from_before, from_after = halo_exchange(blocks, depth_count)
    near = {0: full_rows, 1: from_before, -1: from_after}

    def halo_of(reach):
        return [near[offset] for offset in range(reach, -reach - 1, -1)]

    own_cols = lax.dynamic_slice_in_dim(block_cols, row_place * row_count, row_count, 0)
    own_targets = lax.dynamic_slice_in_dim(
        product_cols, depth_index * target_share, target_share, 1
    )

    across_targets = lax.dynamic_slice_in_dim(
        product_cols, ((depth_index + 2) % depth_count) * target_share, target_share, 1
    )
    halo_first = halo_of(1)
    table_first = block_table(
        block_cols, own_cols, jnp.concatenate([own_targets, across_targets], axis=1), (row_place - 1) * row_count, order_total,
        fill_count, len(halo_first) * row_count * fill_count,
    )
    square, square_rows, near[2], near[-2] = square_products(
        table_first, full_rows, halo_first, depth_count
    )
    halo_second = halo_of(2)
    table_second = block_table(
        block_cols, product_cols, own_targets, (row_place - 2) * row_count, order_total,
        fill_count, len(halo_second) * row_count * fill_count,
    )
    return block_products(table_second, square_rows, halo_second, own=square)


def solution(mesh):
    placed = (P(("row", "col"), "depth", None, None), P(), P(("row", "col"), None))
    return jax.shard_map(
        local,
        mesh=mesh,
        in_specs=placed,
        out_specs=P(("row", "col"), "depth", None, None),
        check_vma=False,
    )
```

```python
import functools

import jax
import jax.numpy as jnp
from jax import lax
from jax.experimental import pallas as pl
from jax.experimental.pallas import tpu as pltpu
from jax.sharding import PartitionSpec as P


def shifted(value, axis, steps):
    count = lax.axis_size(axis)
    pairs = [(source, (source + steps) % count) for source in range(count)]
    return lax.ppermute(value, axis, pairs)


def block_table(block_cols, rows, targets, start_row, order_total, fill_count, miss):
    cols_of = block_cols[rows]
    matches = cols_of[:, None, :, :] == targets[:, :, None, None]
    has_match = jnp.any(matches, axis=3)
    slot_ids = jnp.arange(fill_count, dtype=jnp.int32)[None, None, None, :]
    position = jnp.sum(jnp.where(matches, slot_ids, 0), axis=3)
    local_rows = (rows - start_row) % order_total
    flat = local_rows[:, None, :] * fill_count + position
    flat = jnp.clip(flat, 0, miss)
    return jnp.where(has_match, flat, miss).astype(jnp.int32)


def product_kernel(n_out, n_inner, n_pieces, final, idx_ref, left_ref, *rest):
    pieces = rest[:n_pieces]
    rest = rest[n_pieces:]
    if final:
        own_ref, out_ref, halo, lcat, rcat, sems = rest
    else:
        out_ref, halo, lcat, rcat, sems = rest
    edge = left_ref.shape[-1]
    span = pieces[0].shape[0]
    copies = [
        pltpu.make_async_copy(piece, halo.at[pl.ds(k * span, span)], sems.at[k])
        for k, piece in enumerate(pieces)
    ]
    for copy in copies:
        copy.start()
    halo[n_pieces * span] = jnp.zeros((edge, edge), halo.dtype)
    for copy in copies:
        copy.wait()

    def row_body(row, carry):
        for inner in range(n_inner):
            lcat[:, inner * edge:(inner + 1) * edge] = left_ref[row, inner]

        def col_body(pair, carry):
            col = 2 * pair
            for half in range(2):
                item = row * n_out + col + half
                for inner in range(n_inner):
                    pick = idx_ref[item * n_inner + inner]
                    rcat[inner * edge:(inner + 1) * edge, half * edge:(half + 1) * edge] = halo[pick]
            acc = jnp.dot(lcat[...], rcat[...], preferred_element_type=jnp.float32)
            for half in range(2):
                part = acc[:, half * edge:(half + 1) * edge]
                if final:
                    value = 3.0 * own_ref[row, col + half].astype(jnp.float32) - 2.0 * part
                else:
                    value = part
                out_ref[row, col + half] = value.astype(out_ref.dtype)
            return carry

        return lax.fori_loop(0, n_out // 2, col_body, carry)

    lax.fori_loop(0, left_ref.shape[0], row_body, 0)


def block_products(table, left, pieces, own=None):
    rows, n_inner, edge = left.shape[0], left.shape[1], left.shape[2]
    n_out = table.shape[1]
    final = own is not None
    flat_pieces = [piece.reshape(-1, edge, edge) for piece in pieces]
    span = flat_pieces[0].shape[0]
    operands = [table.reshape(-1), left] + flat_pieces + ([own] if final else [])
    vmem = pl.BlockSpec(memory_space=pltpu.VMEM)
    anywhere = pl.BlockSpec(memory_space=pl.ANY)
    in_specs = [pl.BlockSpec(memory_space=pltpu.SMEM), vmem] + [anywhere] * len(pieces)
    in_specs += [vmem] if final else []
    flops = 2 * rows * n_out * n_inner * edge ** 3
    moved = sum(int(x.size) * x.dtype.itemsize for x in operands) + rows * n_out * edge * edge * 2
    return pl.pallas_call(
        functools.partial(product_kernel, n_out, n_inner, len(pieces), final),
        out_shape=jax.ShapeDtypeStruct((rows, n_out, edge, edge), jnp.bfloat16),
        in_specs=in_specs,
        out_specs=vmem,
        scratch_shapes=[
            pltpu.VMEM((len(pieces) * span + 1, edge, edge), left.dtype),
            pltpu.VMEM((edge, n_inner * edge), left.dtype),
            pltpu.VMEM((n_inner * edge, 2 * edge), left.dtype),
            pltpu.SemaphoreType.DMA((len(pieces),)),
        ],
        compiler_params=pltpu.CompilerParams(vmem_limit_bytes=62 * 1024 * 1024),
        cost_estimate=pl.CostEstimate(flops=flops, transcendentals=0, bytes_accessed=moved),
    )(*operands)


MESH = pl.DeviceIdType.MESH


def square_kernel(n_own, n_inner, n_pieces, idx_ref, left_ref, *rest):
    pieces = rest[:n_pieces]
    out_ref, spread_ref, halo, lcat, rcat, sems, send_sems, recv_sems, keep_sems = rest[
        n_pieces:
    ]
    edge = left_ref.shape[-1]
    span = pieces[0].shape[0]
    row_count = left_ref.shape[0]
    row_at = lax.axis_index("row")
    col_at = lax.axis_index("col")
    depth_at = lax.axis_index("depth")
    depth_count = lax.axis_size("depth")
    ahead = lax.rem(depth_at + 1, depth_count)
    behind = lax.rem(depth_at + depth_count - 1, depth_count)
    across = lax.rem(depth_at + 2, depth_count)

    barrier = pltpu.get_barrier_semaphore()
    for peer in (ahead, behind):
        pl.semaphore_signal(
            barrier, inc=1, device_id=(row_at, col_at, peer), device_id_type=MESH
        )
    pl.semaphore_wait(barrier, 2)

    copies = [
        pltpu.make_async_copy(piece, halo.at[pl.ds(k * span, span)], sems.at[k])
        for k, piece in enumerate(pieces)
    ]
    for copy in copies:
        copy.start()
    halo[n_pieces * span] = jnp.zeros((edge, edge), halo.dtype)
    for copy in copies:
        copy.wait()

    def spread(row, k):
        source = out_ref.at[row, pl.ds(0, n_own)]
        target = spread_ref.at[row, pl.ds(depth_at * n_own, n_own)]
        if k == 0:
            return pltpu.make_async_copy(source, target, send_sems.at[row, 0])
        return pltpu.make_async_remote_copy(
            src_ref=source,
            dst_ref=target,
            send_sem=send_sems.at[row, k],
            recv_sem=recv_sems.at[row, k],
            device_id=(row_at, col_at, ahead if k == 1 else behind),
            device_id_type=MESH,
        )

    def keep(row):
        return pltpu.make_async_copy(
            out_ref.at[row, pl.ds(n_own, n_own)],
            spread_ref.at[row, pl.ds(across * n_own, n_own)],
            keep_sems.at[row],
        )

    def products(row, first):
        for inner in range(n_inner):
            lcat[:, inner * edge:(inner + 1) * edge] = left_ref[row, inner]

        def col_body(pair, carry):
            col = first + 2 * pair
            for half in range(2):
                item = row * 2 * n_own + col + half
                for inner in range(n_inner):
                    pick = idx_ref[item * n_inner + inner]
                    rcat[inner * edge:(inner + 1) * edge, half * edge:(half + 1) * edge] = halo[pick]
            acc = jnp.dot(lcat[...], rcat[...], preferred_element_type=jnp.float32)
            for half in range(2):
                out_ref[row, col + half] = acc[:, half * edge:(half + 1) * edge].astype(out_ref.dtype)
            return carry

        lax.fori_loop(0, n_own // 2, col_body, 0)

    def own_body(row, carry):
        products(row, 0)
        for k in range(3):
            spread(row, k).start()
        return carry

    def across_body(row, carry):
        products(row, n_own)
        keep(row).start()
        return carry

    lax.fori_loop(0, row_count, own_body, 0)
    lax.fori_loop(0, row_count, across_body, 0)
    for row in range(row_count):
        for k in range(3):
            spread(row, k).wait()
        keep(row).wait()


def square_products(table, left, pieces, depth_count):
    rows, n_inner, edge = left.shape[0], left.shape[1], left.shape[2]
    n_own = table.shape[1] // 2
    flat_pieces = [piece.reshape(-1, edge, edge) for piece in pieces]
    span = flat_pieces[0].shape[0]
    operands = [table.reshape(-1), left] + flat_pieces
    vmem = pl.BlockSpec(memory_space=pltpu.VMEM)
    anywhere = pl.BlockSpec(memory_space=pl.ANY)
    in_specs = [pl.BlockSpec(memory_space=pltpu.SMEM), vmem] + [anywhere] * len(pieces)
    flops = 2 * rows * 2 * n_own * n_inner * edge ** 3
    moved = sum(int(x.size) * x.dtype.itemsize for x in operands) + rows * n_own * edge * edge * 10
    return pl.pallas_call(
        functools.partial(square_kernel, n_own, n_inner, len(pieces)),
        out_shape=(
            jax.ShapeDtypeStruct((rows, 2 * n_own, edge, edge), jnp.bfloat16),
            jax.ShapeDtypeStruct((rows, depth_count * n_own, edge, edge), jnp.bfloat16),
        ),
        in_specs=in_specs,
        out_specs=(vmem, anywhere),
        scratch_shapes=[
            pltpu.VMEM((len(pieces) * span + 1, edge, edge), left.dtype),
            pltpu.VMEM((edge, n_inner * edge), left.dtype),
            pltpu.VMEM((n_inner * edge, 2 * edge), left.dtype),
            pltpu.SemaphoreType.DMA((len(pieces),)),
            pltpu.SemaphoreType.DMA((rows, 3)),
            pltpu.SemaphoreType.DMA((rows, 3)),
            pltpu.SemaphoreType.DMA((rows,)),
        ],
        compiler_params=pltpu.CompilerParams(
            vmem_limit_bytes=62 * 1024 * 1024, collective_id=0, has_side_effects=True
        ),
        cost_estimate=pl.CostEstimate(flops=flops, transcendentals=0, bytes_accessed=moved),
    )(*operands)


def halo_kernel(blocks_ref, full_ref, left_ref, right_ref, send_sems, recv_sems, side_send, side_recv):
    quarter = blocks_ref.shape[1]
    row_at = lax.axis_index("row")
    col_at = lax.axis_index("col")
    depth_at = lax.axis_index("depth")
    col_count = lax.axis_size("col")
    depth_count = lax.axis_size("depth")
    ring = lax.axis_size("row") * col_count
    place = row_at * col_count + col_at
    after = lax.rem(place + 1, ring)
    before = lax.rem(place + ring - 1, ring)
    after_id = (after // col_count, after % col_count, depth_at)
    before_id = (before // col_count, before % col_count, depth_at)
    peer_ids = [
        (row_at, col_at, lax.rem(depth_at + k, depth_count)) for k in range(1, depth_count)
    ]

    barrier = pltpu.get_barrier_semaphore()
    for device in peer_ids + [after_id, before_id]:
        pl.semaphore_signal(barrier, inc=1, device_id=device, device_id_type=MESH)
    pl.semaphore_wait(barrier, depth_count + 1)

    own = pl.ds(depth_at * quarter, quarter)
    rows = blocks_ref.shape[0]
    local = pltpu.make_async_copy(blocks_ref, full_ref.at[:, own], side_send.at[2, 0, 0])
    local.start()

    def to_peer(k, row):
        return pltpu.make_async_remote_copy(
            src_ref=blocks_ref.at[row],
            dst_ref=full_ref.at[row, own],
            send_sem=send_sems.at[k, row],
            recv_sem=recv_sems.at[k, row],
            device_id=peer_ids[k - 1],
            device_id_type=MESH,
        )

    def to_side(k, row, way):
        origin = lax.rem(depth_at + depth_count - k, depth_count)
        slot = pl.ds(origin * quarter, quarter)
        source = blocks_ref.at[row] if k == 0 else full_ref.at[row, slot]
        return pltpu.make_async_remote_copy(
            src_ref=source,
            dst_ref=(left_ref if way == 0 else right_ref).at[row, slot],
            send_sem=side_send.at[way, k, row],
            recv_sem=side_recv.at[way, k, row],
            device_id=after_id if way == 0 else before_id,
            device_id_type=MESH,
        )

    for k in range(1, depth_count):
        for row in range(rows):
            to_peer(k, row).start()
    for row in range(rows):
        for way in range(2):
            to_side(0, row, way).start()
    for k in sorted(range(1, depth_count), key=lambda k: min(k, depth_count - k)):
        for row in range(rows):
            to_peer(k, row).wait_recv()
            for way in range(2):
                to_side(k, row, way).start()
    local.wait()
    for k in range(1, depth_count):
        for row in range(rows):
            to_peer(k, row).wait_send()
    for k in range(depth_count):
        for row in range(rows):
            for way in range(2):
                to_side(k, row, way).wait()


def halo_exchange(blocks, depth_count):
    rows, quarter, edge = blocks.shape[0], blocks.shape[1], blocks.shape[2]
    whole = jax.ShapeDtypeStruct((rows, depth_count * quarter, edge, edge), blocks.dtype)
    anywhere = pl.BlockSpec(memory_space=pl.ANY)
    moved = int(blocks.size) * blocks.dtype.itemsize * (3 * depth_count + 3)
    return pl.pallas_call(
        halo_kernel,
        out_shape=(whole, whole, whole),
        in_specs=[anywhere],
        out_specs=(anywhere, anywhere, anywhere),
        scratch_shapes=[
            pltpu.SemaphoreType.DMA((depth_count, rows)),
            pltpu.SemaphoreType.DMA((depth_count, rows)),
            pltpu.SemaphoreType.DMA((3, depth_count, rows)),
            pltpu.SemaphoreType.DMA((2, depth_count, rows)),
        ],
        compiler_params=pltpu.CompilerParams(collective_id=1, has_side_effects=True),
        cost_estimate=pl.CostEstimate(flops=0, transcendentals=0, bytes_accessed=moved),
    )(blocks)


def local(blocks, block_cols, product_cols):
    row_count = blocks.shape[0]
    block_edge = blocks.shape[2]
    fill_count = block_cols.shape[1]
    order_total = row_count * lax.axis_size(("row", "col"))
    row_place = lax.axis_index(("row", "col"))
    depth_index = lax.axis_index("depth")
    depth_count = lax.axis_size("depth")
    target_share = product_cols.shape[1] // depth_count

    full_rows, from_before, from_after = halo_exchange(blocks, depth_count)
    near = {0: full_rows, 1: from_before, -1: from_after}
    near[2] = shifted(near[1], ("row", "col"), 1)
    near[-2] = shifted(near[-1], ("row", "col"), -1)

    def halo_of(reach):
        return [near[offset] for offset in range(reach, -reach - 1, -1)]

    own_cols = lax.dynamic_slice_in_dim(block_cols, row_place * row_count, row_count, 0)
    own_targets = lax.dynamic_slice_in_dim(
        product_cols, depth_index * target_share, target_share, 1
    )

    across_targets = lax.dynamic_slice_in_dim(
        product_cols, ((depth_index + 2) % depth_count) * target_share, target_share, 1
    )
    halo_first = halo_of(1)
    table_first = block_table(
        block_cols, own_cols, jnp.concatenate([own_targets, across_targets], axis=1), (row_place - 1) * row_count, order_total,
        fill_count, len(halo_first) * row_count * fill_count,
    )
    square, square_rows = square_products(table_first, full_rows, halo_first, depth_count)
    halo_second = halo_of(2)
    table_second = block_table(
        block_cols, product_cols, own_targets, (row_place - 2) * row_count, order_total,
        fill_count, len(halo_second) * row_count * fill_count,
    )
    return block_products(table_second, square_rows, halo_second, own=square)


def solution(mesh):
    placed = (P(("row", "col"), "depth", None, None), P(), P(("row", "col"), None))
    return jax.shard_map(
        local,
        mesh=mesh,
        in_specs=placed,
        out_specs=P(("row", "col"), "depth", None, None),
        check_vma=False,
    )
```

```python
import functools

import jax
import jax.numpy as jnp
from jax import lax
from jax.experimental import pallas as pl
from jax.experimental.pallas import tpu as pltpu
from jax.sharding import PartitionSpec as P


def shifted(value, axis, steps):
    count = lax.axis_size(axis)
    pairs = [(source, (source + steps) % count) for source in range(count)]
    return lax.ppermute(value, axis, pairs)


def block_table(block_cols, rows, targets, start_row, order_total, fill_count, miss):
    cols_of = block_cols[rows]
    matches = cols_of[:, :, None, :] == targets[:, None, :, None]
    has_match = jnp.any(matches, axis=3)
    slot_ids = jnp.arange(fill_count, dtype=jnp.int32)[None, None, None, :]
    position = jnp.sum(jnp.where(matches, slot_ids, 0), axis=3)
    local_rows = (rows - start_row) % order_total
    flat = local_rows[:, :, None] * fill_count + position
    flat = jnp.clip(flat, 0, miss)
    return jnp.where(has_match, flat, miss).astype(jnp.int32)


def table_pick(idx_ref, view, row, inner, col):
    row_stride, first, inner_stride, shift, cap = view
    entry = idx_ref[row * row_stride + (first + inner) * inner_stride + col]
    return jnp.minimum(jnp.maximum(entry - shift, 0), cap)


def product_kernel(n_out, n_inner, n_pieces, final, view, idx_ref, left_ref, *rest):
    pieces = rest[:n_pieces]
    rest = rest[n_pieces:]
    if final:
        own_ref, out_ref, halo, lcat, rcat, sems = rest
    else:
        out_ref, halo, lcat, rcat, sems = rest
    edge = left_ref.shape[-1]
    span = pieces[0].shape[0]
    copies = [
        pltpu.make_async_copy(piece, halo.at[pl.ds(k * span, span)], sems.at[k])
        for k, piece in enumerate(pieces)
    ]
    for copy in copies:
        copy.start()
    halo[n_pieces * span] = jnp.zeros((edge, edge), halo.dtype)
    for copy in copies:
        copy.wait()

    def row_body(row, carry):
        for inner in range(n_inner):
            lcat[:, inner * edge:(inner + 1) * edge] = left_ref[row, inner]

        def col_body(pair, carry):
            col = 2 * pair
            for half in range(2):
                for inner in range(n_inner):
                    pick = table_pick(idx_ref, view, row, inner, col + half)
                    rcat[inner * edge:(inner + 1) * edge, half * edge:(half + 1) * edge] = halo[pick]
            acc = jnp.dot(lcat[...], rcat[...], preferred_element_type=jnp.float32)
            for half in range(2):
                part = acc[:, half * edge:(half + 1) * edge]
                if final:
                    value = 3.0 * own_ref[row, col + half].astype(jnp.float32) - 2.0 * part
                else:
                    value = part
                out_ref[row, col + half] = value.astype(out_ref.dtype)
            return carry

        return lax.fori_loop(0, n_out // 2, col_body, carry)

    lax.fori_loop(0, left_ref.shape[0], row_body, 0)


def block_products(table, left, pieces, n_out, view, own=None):
    rows, n_inner, edge = left.shape[0], left.shape[1], left.shape[2]
    final = own is not None
    flat_pieces = [piece.reshape(-1, edge, edge) for piece in pieces]
    span = flat_pieces[0].shape[0]
    operands = [table.reshape(-1), left] + flat_pieces + ([own] if final else [])
    vmem = pl.BlockSpec(memory_space=pltpu.VMEM)
    anywhere = pl.BlockSpec(memory_space=pl.ANY)
    in_specs = [pl.BlockSpec(memory_space=pltpu.SMEM), vmem] + [anywhere] * len(pieces)
    in_specs += [vmem] if final else []
    flops = 2 * rows * n_out * n_inner * edge ** 3
    moved = sum(int(x.size) * x.dtype.itemsize for x in operands) + rows * n_out * edge * edge * 2
    return pl.pallas_call(
        functools.partial(product_kernel, n_out, n_inner, len(pieces), final, view),
        out_shape=jax.ShapeDtypeStruct((rows, n_out, edge, edge), jnp.bfloat16),
        in_specs=in_specs,
        out_specs=vmem,
        scratch_shapes=[
            pltpu.VMEM((len(pieces) * span + 1, edge, edge), left.dtype),
            pltpu.VMEM((edge, n_inner * edge), left.dtype),
            pltpu.VMEM((n_inner * edge, 2 * edge), left.dtype),
            pltpu.SemaphoreType.DMA((len(pieces),)),
        ],
        compiler_params=pltpu.CompilerParams(vmem_limit_bytes=62 * 1024 * 1024),
        cost_estimate=pl.CostEstimate(flops=flops, transcendentals=0, bytes_accessed=moved),
    )(*operands)


MESH = pl.DeviceIdType.MESH


def square_kernel(n_own, n_inner, n_pieces, view, idx_ref, left_ref, *rest):
    pieces = rest[:n_pieces]
    out_ref, spread_ref, halo, lcat, rcat, sems, send_sems, recv_sems, keep_sems = rest[
        n_pieces:
    ]
    edge = left_ref.shape[-1]
    span = pieces[0].shape[0]
    row_count = left_ref.shape[0]
    row_at = lax.axis_index("row")
    col_at = lax.axis_index("col")
    depth_at = lax.axis_index("depth")
    depth_count = lax.axis_size("depth")
    ahead = lax.rem(depth_at + 1, depth_count)
    behind = lax.rem(depth_at + depth_count - 1, depth_count)
    across = lax.rem(depth_at + 2, depth_count)

    barrier = pltpu.get_barrier_semaphore()
    for peer in (ahead, behind):
        pl.semaphore_signal(
            barrier, inc=1, device_id=(row_at, col_at, peer), device_id_type=MESH
        )
    pl.semaphore_wait(barrier, 2)

    copies = [
        pltpu.make_async_copy(piece, halo.at[pl.ds(k * span, span)], sems.at[k])
        for k, piece in enumerate(pieces)
    ]
    for copy in copies:
        copy.start()
    halo[n_pieces * span] = jnp.zeros((edge, edge), halo.dtype)
    for copy in copies:
        copy.wait()

    def spread(row, k):
        source = out_ref.at[row, pl.ds(0, n_own)]
        target = spread_ref.at[row, pl.ds(depth_at * n_own, n_own)]
        if k == 0:
            return pltpu.make_async_copy(source, target, send_sems.at[row, 0])
        return pltpu.make_async_remote_copy(
            src_ref=source,
            dst_ref=target,
            send_sem=send_sems.at[row, k],
            recv_sem=recv_sems.at[row, k],
            device_id=(row_at, col_at, ahead if k == 1 else behind),
            device_id_type=MESH,
        )

    def keep(row):
        return pltpu.make_async_copy(
            out_ref.at[row, pl.ds(n_own, n_own)],
            spread_ref.at[row, pl.ds(across * n_own, n_own)],
            keep_sems.at[row],
        )

    def products(row, first):
        for inner in range(n_inner):
            lcat[:, inner * edge:(inner + 1) * edge] = left_ref[row, inner]

        def col_body(pair, carry):
            col = first + 2 * pair
            for half in range(2):
                for inner in range(n_inner):
                    pick = table_pick(idx_ref, view, row, inner, col + half)
                    rcat[inner * edge:(inner + 1) * edge, half * edge:(half + 1) * edge] = halo[pick]
            acc = jnp.dot(lcat[...], rcat[...], preferred_element_type=jnp.float32)
            for half in range(2):
                out_ref[row, col + half] = acc[:, half * edge:(half + 1) * edge].astype(out_ref.dtype)
            return carry

        lax.fori_loop(0, n_own // 2, col_body, 0)

    def own_body(row, carry):
        products(row, 0)
        for k in range(3):
            spread(row, k).start()
        return carry

    def across_body(row, carry):
        products(row, n_own)
        keep(row).start()
        return carry

    lax.fori_loop(0, row_count, own_body, 0)
    lax.fori_loop(0, row_count, across_body, 0)
    for row in range(row_count):
        for k in range(3):
            spread(row, k).wait()
        keep(row).wait()


def square_products(table, left, pieces, depth_count, n_own, view):
    rows, n_inner, edge = left.shape[0], left.shape[1], left.shape[2]
    flat_pieces = [piece.reshape(-1, edge, edge) for piece in pieces]
    span = flat_pieces[0].shape[0]
    operands = [table.reshape(-1), left] + flat_pieces
    vmem = pl.BlockSpec(memory_space=pltpu.VMEM)
    anywhere = pl.BlockSpec(memory_space=pl.ANY)
    in_specs = [pl.BlockSpec(memory_space=pltpu.SMEM), vmem] + [anywhere] * len(pieces)
    flops = 2 * rows * 2 * n_own * n_inner * edge ** 3
    moved = sum(int(x.size) * x.dtype.itemsize for x in operands) + rows * n_own * edge * edge * 10
    return pl.pallas_call(
        functools.partial(square_kernel, n_own, n_inner, len(pieces), view),
        out_shape=(
            jax.ShapeDtypeStruct((rows, 2 * n_own, edge, edge), jnp.bfloat16),
            jax.ShapeDtypeStruct((rows, depth_count * n_own, edge, edge), jnp.bfloat16),
        ),
        in_specs=in_specs,
        out_specs=(vmem, anywhere),
        scratch_shapes=[
            pltpu.VMEM((len(pieces) * span + 1, edge, edge), left.dtype),
            pltpu.VMEM((edge, n_inner * edge), left.dtype),
            pltpu.VMEM((n_inner * edge, 2 * edge), left.dtype),
            pltpu.SemaphoreType.DMA((len(pieces),)),
            pltpu.SemaphoreType.DMA((rows, 3)),
            pltpu.SemaphoreType.DMA((rows, 3)),
            pltpu.SemaphoreType.DMA((rows,)),
        ],
        compiler_params=pltpu.CompilerParams(
            vmem_limit_bytes=62 * 1024 * 1024, collective_id=0, has_side_effects=True
        ),
        cost_estimate=pl.CostEstimate(flops=flops, transcendentals=0, bytes_accessed=moved),
    )(*operands)


def halo_kernel(blocks_ref, full_ref, left_ref, right_ref, send_sems, recv_sems, side_send, side_recv):
    quarter = blocks_ref.shape[1]
    row_at = lax.axis_index("row")
    col_at = lax.axis_index("col")
    depth_at = lax.axis_index("depth")
    col_count = lax.axis_size("col")
    depth_count = lax.axis_size("depth")
    ring = lax.axis_size("row") * col_count
    place = row_at * col_count + col_at
    after = lax.rem(place + 1, ring)
    before = lax.rem(place + ring - 1, ring)
    after_id = (after // col_count, after % col_count, depth_at)
    before_id = (before // col_count, before % col_count, depth_at)
    peer_ids = [
        (row_at, col_at, lax.rem(depth_at + k, depth_count)) for k in range(1, depth_count)
    ]

    barrier = pltpu.get_barrier_semaphore()
    for device in peer_ids + [after_id, before_id]:
        pl.semaphore_signal(barrier, inc=1, device_id=device, device_id_type=MESH)
    pl.semaphore_wait(barrier, depth_count + 1)

    own = pl.ds(depth_at * quarter, quarter)
    rows = blocks_ref.shape[0]
    local = pltpu.make_async_copy(blocks_ref, full_ref.at[:, own], side_send.at[2, 0, 0])
    local.start()

    def to_peer(k, row):
        return pltpu.make_async_remote_copy(
            src_ref=blocks_ref.at[row],
            dst_ref=full_ref.at[row, own],
            send_sem=send_sems.at[k, row],
            recv_sem=recv_sems.at[k, row],
            device_id=peer_ids[k - 1],
            device_id_type=MESH,
        )

    def to_side(k, row, way):
        origin = lax.rem(depth_at + depth_count - k, depth_count)
        slot = pl.ds(origin * quarter, quarter)
        source = blocks_ref.at[row] if k == 0 else full_ref.at[row, slot]
        return pltpu.make_async_remote_copy(
            src_ref=source,
            dst_ref=(left_ref if way == 0 else right_ref).at[row, slot],
            send_sem=side_send.at[way, k, row],
            recv_sem=side_recv.at[way, k, row],
            device_id=after_id if way == 0 else before_id,
            device_id_type=MESH,
        )

    for k in range(1, depth_count):
        for row in range(rows):
            to_peer(k, row).start()
    for row in range(rows):
        for way in range(2):
            to_side(0, row, way).start()
    for k in sorted(range(1, depth_count), key=lambda k: min(k, depth_count - k)):
        for row in range(rows):
            to_peer(k, row).wait_recv()
            for way in range(2):
                to_side(k, row, way).start()
    local.wait()
    for k in range(1, depth_count):
        for row in range(rows):
            to_peer(k, row).wait_send()
    for k in range(depth_count):
        for row in range(rows):
            for way in range(2):
                to_side(k, row, way).wait()


def halo_exchange(blocks, depth_count):
    rows, quarter, edge = blocks.shape[0], blocks.shape[1], blocks.shape[2]
    whole = jax.ShapeDtypeStruct((rows, depth_count * quarter, edge, edge), blocks.dtype)
    anywhere = pl.BlockSpec(memory_space=pl.ANY)
    moved = int(blocks.size) * blocks.dtype.itemsize * (3 * depth_count + 3)
    return pl.pallas_call(
        halo_kernel,
        out_shape=(whole, whole, whole),
        in_specs=[anywhere],
        out_specs=(anywhere, anywhere, anywhere),
        scratch_shapes=[
            pltpu.SemaphoreType.DMA((depth_count, rows)),
            pltpu.SemaphoreType.DMA((depth_count, rows)),
            pltpu.SemaphoreType.DMA((3, depth_count, rows)),
            pltpu.SemaphoreType.DMA((2, depth_count, rows)),
        ],
        compiler_params=pltpu.CompilerParams(collective_id=1, has_side_effects=True),
        cost_estimate=pl.CostEstimate(flops=0, transcendentals=0, bytes_accessed=moved),
    )(blocks)


def local(blocks, block_cols, product_cols):
    row_count = blocks.shape[0]
    block_edge = blocks.shape[2]
    fill_count = block_cols.shape[1]
    order_total = row_count * lax.axis_size(("row", "col"))
    row_place = lax.axis_index(("row", "col"))
    depth_index = lax.axis_index("depth")
    depth_count = lax.axis_size("depth")
    target_share = product_cols.shape[1] // depth_count

    full_rows, from_before, from_after = halo_exchange(blocks, depth_count)
    near = {0: full_rows, 1: from_before, -1: from_after}
    near[2] = shifted(near[1], ("row", "col"), 1)
    near[-2] = shifted(near[-1], ("row", "col"), -1)

    def halo_of(reach):
        return [near[offset] for offset in range(reach, -reach - 1, -1)]

    own_cols = lax.dynamic_slice_in_dim(block_cols, row_place * row_count, row_count, 0)
    own_targets = lax.dynamic_slice_in_dim(
        product_cols, depth_index * target_share, target_share, 1
    )

    across_targets = lax.dynamic_slice_in_dim(
        product_cols, ((depth_index + 2) % depth_count) * target_share, target_share, 1
    )
    halo_first = halo_of(1)
    halo_second = halo_of(2)
    piece_blocks = row_count * fill_count
    inner_rows = jnp.concatenate([own_cols, product_cols], axis=1)
    targets = jnp.concatenate([own_targets, across_targets], axis=1)
    table = block_table(
        block_cols, inner_rows, targets, (row_place - 2) * row_count, order_total,
        fill_count, len(halo_second) * piece_blocks,
    )
    row_stride = inner_rows.shape[1] * targets.shape[1]
    first_view = (row_stride, 0, targets.shape[1], piece_blocks, len(halo_first) * piece_blocks)
    second_view = (row_stride, fill_count, targets.shape[1], 0, len(halo_second) * piece_blocks)
    square, square_rows = square_products(
        table, full_rows, halo_first, depth_count, target_share, first_view
    )
    return block_products(
        table, square_rows, halo_second, target_share, second_view, own=square
    )


def solution(mesh):
    placed = (P(("row", "col"), "depth", None, None), P(), P(("row", "col"), None))
    return jax.shard_map(
        local,
        mesh=mesh,
        in_specs=placed,
        out_specs=P(("row", "col"), "depth", None, None),
        check_vma=False,
    )
```

```python
import functools

import jax
import jax.numpy as jnp
from jax import lax
from jax.experimental import pallas as pl
from jax.experimental.pallas import tpu as pltpu
from jax.sharding import PartitionSpec as P


def shifted(value, axis, steps):
    count = lax.axis_size(axis)
    pairs = [(source, (source + steps) % count) for source in range(count)]
    return lax.ppermute(value, axis, pairs)


def block_table(block_cols, rows, targets, start_row, order_total, fill_count, miss):
    cols_of = block_cols[rows]
    matches = cols_of[:, :, None, :] == targets[:, None, :, None]
    has_match = jnp.any(matches, axis=3)
    slot_ids = jnp.arange(fill_count, dtype=jnp.int32)[None, None, None, :]
    position = jnp.sum(jnp.where(matches, slot_ids, 0), axis=3)
    local_rows = (rows - start_row) % order_total
    flat = local_rows[:, :, None] * fill_count + position
    flat = jnp.clip(flat, 0, miss)
    return jnp.where(has_match, flat, miss).astype(jnp.int32)


def table_pick(idx_ref, view, row, inner, col):
    row_stride, first, inner_stride, shift, cap = view
    entry = idx_ref[row * row_stride + (first + inner) * inner_stride + col]
    return jnp.minimum(jnp.maximum(entry - shift, 0), cap)


def product_kernel(n_out, n_inner, n_pieces, final, view, idx_ref, left_ref, *rest):
    pieces = rest[:n_pieces]
    rest = rest[n_pieces:]
    if final:
        own_ref, out_ref, halo, lcat, rcat, sems = rest
    else:
        out_ref, halo, lcat, rcat, sems = rest
    edge = left_ref.shape[-1]
    span = pieces[0].shape[0]
    copies = [
        pltpu.make_async_copy(piece, halo.at[pl.ds(k * span, span)], sems.at[k])
        for k, piece in enumerate(pieces)
    ]
    for copy in copies:
        copy.start()
    halo[n_pieces * span] = jnp.zeros((edge, edge), halo.dtype)
    for copy in copies:
        copy.wait()

    def row_body(row, carry):
        for inner in range(n_inner):
            lcat[:, inner * edge:(inner + 1) * edge] = left_ref[row, inner]

        for col in range(n_out):
            for inner in range(n_inner):
                pick = table_pick(idx_ref, view, row, inner, col)
                rcat[inner * edge:(inner + 1) * edge, col * edge:(col + 1) * edge] = halo[pick]
        acc = jnp.dot(lcat[...], rcat[...], preferred_element_type=jnp.float32)
        for col in range(n_out):
            part = acc[:, col * edge:(col + 1) * edge]
            if final:
                value = 3.0 * own_ref[row, col].astype(jnp.float32) - 2.0 * part
            else:
                value = part
            out_ref[row, col] = value.astype(out_ref.dtype)
        return carry

    lax.fori_loop(0, left_ref.shape[0], row_body, 0)


def block_products(table, left, pieces, n_out, view, own=None):
    rows, n_inner, edge = left.shape[0], left.shape[1], left.shape[2]
    final = own is not None
    flat_pieces = [piece.reshape(-1, edge, edge) for piece in pieces]
    span = flat_pieces[0].shape[0]
    operands = [table.reshape(-1), left] + flat_pieces + ([own] if final else [])
    vmem = pl.BlockSpec(memory_space=pltpu.VMEM)
    anywhere = pl.BlockSpec(memory_space=pl.ANY)
    in_specs = [pl.BlockSpec(memory_space=pltpu.SMEM), vmem] + [anywhere] * len(pieces)
    in_specs += [vmem] if final else []
    flops = 2 * rows * n_out * n_inner * edge ** 3
    moved = sum(int(x.size) * x.dtype.itemsize for x in operands) + rows * n_out * edge * edge * 2
    return pl.pallas_call(
        functools.partial(product_kernel, n_out, n_inner, len(pieces), final, view),
        out_shape=jax.ShapeDtypeStruct((rows, n_out, edge, edge), jnp.bfloat16),
        in_specs=in_specs,
        out_specs=vmem,
        scratch_shapes=[
            pltpu.VMEM((len(pieces) * span + 1, edge, edge), left.dtype),
            pltpu.VMEM((edge, n_inner * edge), left.dtype),
            pltpu.VMEM((n_inner * edge, n_out * edge), left.dtype),
            pltpu.SemaphoreType.DMA((len(pieces),)),
        ],
        compiler_params=pltpu.CompilerParams(vmem_limit_bytes=62 * 1024 * 1024),
        cost_estimate=pl.CostEstimate(flops=flops, transcendentals=0, bytes_accessed=moved),
    )(*operands)


MESH = pl.DeviceIdType.MESH


def square_kernel(n_own, n_inner, n_pieces, view, idx_ref, left_ref, *rest):
    pieces = rest[:n_pieces]
    out_ref, spread_ref, halo, lcat, rcat, sems, send_sems, recv_sems, keep_sems = rest[
        n_pieces:
    ]
    edge = left_ref.shape[-1]
    span = pieces[0].shape[0]
    row_count = left_ref.shape[0]
    row_at = lax.axis_index("row")
    col_at = lax.axis_index("col")
    depth_at = lax.axis_index("depth")
    depth_count = lax.axis_size("depth")
    ahead = lax.rem(depth_at + 1, depth_count)
    behind = lax.rem(depth_at + depth_count - 1, depth_count)
    across = lax.rem(depth_at + 2, depth_count)

    barrier = pltpu.get_barrier_semaphore()
    for peer in (ahead, behind):
        pl.semaphore_signal(
            barrier, inc=1, device_id=(row_at, col_at, peer), device_id_type=MESH
        )
    pl.semaphore_wait(barrier, 2)

    copies = [
        pltpu.make_async_copy(piece, halo.at[pl.ds(k * span, span)], sems.at[k])
        for k, piece in enumerate(pieces)
    ]
    for copy in copies:
        copy.start()
    halo[n_pieces * span] = jnp.zeros((edge, edge), halo.dtype)
    for copy in copies:
        copy.wait()

    def spread(row, k):
        source = out_ref.at[row, pl.ds(0, n_own)]
        target = spread_ref.at[row, pl.ds(depth_at * n_own, n_own)]
        if k == 0:
            return pltpu.make_async_copy(source, target, send_sems.at[row, 0])
        return pltpu.make_async_remote_copy(
            src_ref=source,
            dst_ref=target,
            send_sem=send_sems.at[row, k],
            recv_sem=recv_sems.at[row, k],
            device_id=(row_at, col_at, ahead if k == 1 else behind),
            device_id_type=MESH,
        )

    def keep(row):
        return pltpu.make_async_copy(
            out_ref.at[row, pl.ds(n_own, n_own)],
            spread_ref.at[row, pl.ds(across * n_own, n_own)],
            keep_sems.at[row],
        )

    def products(row, first):
        for inner in range(n_inner):
            lcat[:, inner * edge:(inner + 1) * edge] = left_ref[row, inner]

        for part in range(n_own):
            for inner in range(n_inner):
                pick = table_pick(idx_ref, view, row, inner, first + part)
                rcat[inner * edge:(inner + 1) * edge, part * edge:(part + 1) * edge] = halo[pick]
        acc = jnp.dot(lcat[...], rcat[...], preferred_element_type=jnp.float32)
        for part in range(n_own):
            out_ref[row, first + part] = acc[:, part * edge:(part + 1) * edge].astype(out_ref.dtype)

    def own_body(row, carry):
        products(row, 0)
        for k in range(3):
            spread(row, k).start()
        return carry

    def across_body(row, carry):
        products(row, n_own)
        keep(row).start()
        return carry

    lax.fori_loop(0, row_count, own_body, 0)
    lax.fori_loop(0, row_count, across_body, 0)
    for row in range(row_count):
        for k in range(3):
            spread(row, k).wait()
        keep(row).wait()


def square_products(table, left, pieces, depth_count, n_own, view):
    rows, n_inner, edge = left.shape[0], left.shape[1], left.shape[2]
    flat_pieces = [piece.reshape(-1, edge, edge) for piece in pieces]
    span = flat_pieces[0].shape[0]
    operands = [table.reshape(-1), left] + flat_pieces
    vmem = pl.BlockSpec(memory_space=pltpu.VMEM)
    anywhere = pl.BlockSpec(memory_space=pl.ANY)
    in_specs = [pl.BlockSpec(memory_space=pltpu.SMEM), vmem] + [anywhere] * len(pieces)
    flops = 2 * rows * 2 * n_own * n_inner * edge ** 3
    moved = sum(int(x.size) * x.dtype.itemsize for x in operands) + rows * n_own * edge * edge * 10
    return pl.pallas_call(
        functools.partial(square_kernel, n_own, n_inner, len(pieces), view),
        out_shape=(
            jax.ShapeDtypeStruct((rows, 2 * n_own, edge, edge), jnp.bfloat16),
            jax.ShapeDtypeStruct((rows, depth_count * n_own, edge, edge), jnp.bfloat16),
        ),
        in_specs=in_specs,
        out_specs=(vmem, anywhere),
        scratch_shapes=[
            pltpu.VMEM((len(pieces) * span + 1, edge, edge), left.dtype),
            pltpu.VMEM((edge, n_inner * edge), left.dtype),
            pltpu.VMEM((n_inner * edge, n_own * edge), left.dtype),
            pltpu.SemaphoreType.DMA((len(pieces),)),
            pltpu.SemaphoreType.DMA((rows, 3)),
            pltpu.SemaphoreType.DMA((rows, 3)),
            pltpu.SemaphoreType.DMA((rows,)),
        ],
        compiler_params=pltpu.CompilerParams(
            vmem_limit_bytes=62 * 1024 * 1024, collective_id=0, has_side_effects=True
        ),
        cost_estimate=pl.CostEstimate(flops=flops, transcendentals=0, bytes_accessed=moved),
    )(*operands)


def halo_kernel(blocks_ref, full_ref, left_ref, right_ref, send_sems, recv_sems, side_send, side_recv):
    quarter = blocks_ref.shape[1]
    row_at = lax.axis_index("row")
    col_at = lax.axis_index("col")
    depth_at = lax.axis_index("depth")
    col_count = lax.axis_size("col")
    depth_count = lax.axis_size("depth")
    ring = lax.axis_size("row") * col_count
    place = row_at * col_count + col_at
    after = lax.rem(place + 1, ring)
    before = lax.rem(place + ring - 1, ring)
    after_id = (after // col_count, after % col_count, depth_at)
    before_id = (before // col_count, before % col_count, depth_at)
    peer_ids = [
        (row_at, col_at, lax.rem(depth_at + k, depth_count)) for k in range(1, depth_count)
    ]

    barrier = pltpu.get_barrier_semaphore()
    for device in peer_ids + [after_id, before_id]:
        pl.semaphore_signal(barrier, inc=1, device_id=device, device_id_type=MESH)
    pl.semaphore_wait(barrier, depth_count + 1)

    own = pl.ds(depth_at * quarter, quarter)
    rows = blocks_ref.shape[0]
    local = pltpu.make_async_copy(blocks_ref, full_ref.at[:, own], side_send.at[2, 0, 0])
    local.start()

    def to_peer(k, row):
        return pltpu.make_async_remote_copy(
            src_ref=blocks_ref.at[row],
            dst_ref=full_ref.at[row, own],
            send_sem=send_sems.at[k, row],
            recv_sem=recv_sems.at[k, row],
            device_id=peer_ids[k - 1],
            device_id_type=MESH,
        )

    def to_side(k, row, way):
        origin = lax.rem(depth_at + depth_count - k, depth_count)
        slot = pl.ds(origin * quarter, quarter)
        source = blocks_ref.at[row] if k == 0 else full_ref.at[row, slot]
        return pltpu.make_async_remote_copy(
            src_ref=source,
            dst_ref=(left_ref if way == 0 else right_ref).at[row, slot],
            send_sem=side_send.at[way, k, row],
            recv_sem=side_recv.at[way, k, row],
            device_id=after_id if way == 0 else before_id,
            device_id_type=MESH,
        )

    for k in range(1, depth_count):
        for row in range(rows):
            to_peer(k, row).start()
    for row in range(rows):
        for way in range(2):
            to_side(0, row, way).start()
    for k in sorted(range(1, depth_count), key=lambda k: min(k, depth_count - k)):
        for row in range(rows):
            to_peer(k, row).wait_recv()
            for way in range(2):
                to_side(k, row, way).start()
    local.wait()
    for k in range(1, depth_count):
        for row in range(rows):
            to_peer(k, row).wait_send()
    for k in range(depth_count):
        for row in range(rows):
            for way in range(2):
                to_side(k, row, way).wait()


def halo_exchange(blocks, depth_count):
    rows, quarter, edge = blocks.shape[0], blocks.shape[1], blocks.shape[2]
    whole = jax.ShapeDtypeStruct((rows, depth_count * quarter, edge, edge), blocks.dtype)
    anywhere = pl.BlockSpec(memory_space=pl.ANY)
    moved = int(blocks.size) * blocks.dtype.itemsize * (3 * depth_count + 3)
    return pl.pallas_call(
        halo_kernel,
        out_shape=(whole, whole, whole),
        in_specs=[anywhere],
        out_specs=(anywhere, anywhere, anywhere),
        scratch_shapes=[
            pltpu.SemaphoreType.DMA((depth_count, rows)),
            pltpu.SemaphoreType.DMA((depth_count, rows)),
            pltpu.SemaphoreType.DMA((3, depth_count, rows)),
            pltpu.SemaphoreType.DMA((2, depth_count, rows)),
        ],
        compiler_params=pltpu.CompilerParams(collective_id=1, has_side_effects=True),
        cost_estimate=pl.CostEstimate(flops=0, transcendentals=0, bytes_accessed=moved),
    )(blocks)


def local(blocks, block_cols, product_cols):
    row_count = blocks.shape[0]
    block_edge = blocks.shape[2]
    fill_count = block_cols.shape[1]
    order_total = row_count * lax.axis_size(("row", "col"))
    row_place = lax.axis_index(("row", "col"))
    depth_index = lax.axis_index("depth")
    depth_count = lax.axis_size("depth")
    target_share = product_cols.shape[1] // depth_count

    full_rows, from_before, from_after = halo_exchange(blocks, depth_count)
    near = {0: full_rows, 1: from_before, -1: from_after}
    near[2] = shifted(near[1], ("row", "col"), 1)
    near[-2] = shifted(near[-1], ("row", "col"), -1)

    def halo_of(reach):
        return [near[offset] for offset in range(reach, -reach - 1, -1)]

    own_cols = lax.dynamic_slice_in_dim(block_cols, row_place * row_count, row_count, 0)
    own_targets = lax.dynamic_slice_in_dim(
        product_cols, depth_index * target_share, target_share, 1
    )

    across_targets = lax.dynamic_slice_in_dim(
        product_cols, ((depth_index + 2) % depth_count) * target_share, target_share, 1
    )
    halo_first = halo_of(1)
    halo_second = halo_of(2)
    piece_blocks = row_count * fill_count
    inner_rows = jnp.concatenate([own_cols, product_cols], axis=1)
    targets = jnp.concatenate([own_targets, across_targets], axis=1)
    table = block_table(
        block_cols, inner_rows, targets, (row_place - 2) * row_count, order_total,
        fill_count, len(halo_second) * piece_blocks,
    )
    row_stride = inner_rows.shape[1] * targets.shape[1]
    first_view = (row_stride, 0, targets.shape[1], piece_blocks, len(halo_first) * piece_blocks)
    second_view = (row_stride, fill_count, targets.shape[1], 0, len(halo_second) * piece_blocks)
    square, square_rows = square_products(
        table, full_rows, halo_first, depth_count, target_share, first_view
    )
    return block_products(
        table, square_rows, halo_second, target_share, second_view, own=square
    )


def solution(mesh):
    placed = (P(("row", "col"), "depth", None, None), P(), P(("row", "col"), None))
    return jax.shard_map(
        local,
        mesh=mesh,
        in_specs=placed,
        out_specs=P(("row", "col"), "depth", None, None),
        check_vma=False,
    )
```

```python
import functools

import jax
import jax.numpy as jnp
from jax import lax
from jax.experimental import pallas as pl
from jax.experimental.pallas import tpu as pltpu
from jax.sharding import PartitionSpec as P


def shifted(value, axis, steps):
    count = lax.axis_size(axis)
    pairs = [(source, (source + steps) % count) for source in range(count)]
    return lax.ppermute(value, axis, pairs)


def block_table(block_cols, rows, targets, start_row, order_total, fill_count, miss):
    cols_of = block_cols[rows]
    matches = cols_of[:, :, None, :] == targets[:, None, :, None]
    has_match = jnp.any(matches, axis=3)
    slot_ids = jnp.arange(fill_count, dtype=jnp.int32)[None, None, None, :]
    position = jnp.sum(jnp.where(matches, slot_ids, 0), axis=3)
    local_rows = (rows - start_row) % order_total
    flat = local_rows[:, :, None] * fill_count + position
    flat = jnp.clip(flat, 0, miss)
    return jnp.where(has_match, flat, miss).astype(jnp.int32)


def table_pick(idx_ref, view, row, inner, col):
    row_stride, first, inner_stride, shift, cap = view
    entry = idx_ref[row * row_stride + (first + inner) * inner_stride + col]
    return jnp.minimum(jnp.maximum(entry - shift, 0), cap)


def product_kernel(n_out, n_inner, n_pieces, final, view, idx_ref, left_ref, *rest):
    pieces = rest[:n_pieces]
    rest = rest[n_pieces:]
    if final:
        own_ref, out_ref, halo, lcat, rcat, sems = rest
    else:
        out_ref, halo, lcat, rcat, sems = rest
    edge = left_ref.shape[-1]
    span = pieces[0].shape[0]
    copies = [
        pltpu.make_async_copy(piece, halo.at[pl.ds(k * span, span)], sems.at[k])
        for k, piece in enumerate(pieces)
    ]
    for copy in copies:
        copy.start()
    halo[n_pieces * span] = jnp.zeros((edge, edge), halo.dtype)
    for copy in copies:
        copy.wait()

    def row_body(row, carry):
        for inner in range(n_inner):
            lcat[:, inner * edge:(inner + 1) * edge] = left_ref[row, inner]

        for col in range(n_out):
            for inner in range(n_inner):
                pick = table_pick(idx_ref, view, row, inner, col)
                rcat[inner * edge:(inner + 1) * edge, col * edge:(col + 1) * edge] = halo[pick]
        acc = jnp.dot(lcat[...], rcat[...], preferred_element_type=jnp.float32)
        for col in range(n_out):
            part = acc[:, col * edge:(col + 1) * edge]
            if final:
                value = 3.0 * own_ref[row, col].astype(jnp.float32) - 2.0 * part
            else:
                value = part
            out_ref[row, col] = value.astype(out_ref.dtype)
        return carry

    lax.fori_loop(0, left_ref.shape[0], row_body, 0)


def block_products(table, left, pieces, n_out, view, own=None):
    rows, n_inner, edge = left.shape[0], left.shape[1], left.shape[2]
    final = own is not None
    flat_pieces = [piece.reshape(-1, edge, edge) for piece in pieces]
    span = flat_pieces[0].shape[0]
    operands = [table.reshape(-1), left] + flat_pieces + ([own] if final else [])
    vmem = pl.BlockSpec(memory_space=pltpu.VMEM)
    anywhere = pl.BlockSpec(memory_space=pl.ANY)
    in_specs = [pl.BlockSpec(memory_space=pltpu.SMEM), vmem] + [anywhere] * len(pieces)
    in_specs += [vmem] if final else []
    flops = 2 * rows * n_out * n_inner * edge ** 3
    moved = sum(int(x.size) * x.dtype.itemsize for x in operands) + rows * n_out * edge * edge * 2
    return pl.pallas_call(
        functools.partial(product_kernel, n_out, n_inner, len(pieces), final, view),
        out_shape=jax.ShapeDtypeStruct((rows, n_out, edge, edge), jnp.bfloat16),
        in_specs=in_specs,
        out_specs=vmem,
        scratch_shapes=[
            pltpu.VMEM((len(pieces) * span + 1, edge, edge), left.dtype),
            pltpu.VMEM((edge, n_inner * edge), left.dtype),
            pltpu.VMEM((n_inner * edge, n_out * edge), left.dtype),
            pltpu.SemaphoreType.DMA((len(pieces),)),
        ],
        compiler_params=pltpu.CompilerParams(vmem_limit_bytes=62 * 1024 * 1024),
        cost_estimate=pl.CostEstimate(flops=flops, transcendentals=0, bytes_accessed=moved),
    )(*operands)


MESH = pl.DeviceIdType.MESH


def square_kernel(n_own, n_inner, n_pieces, view, idx_ref, left_ref, *rest):
    pieces = rest[:n_pieces]
    out_ref, spread_ref, halo, lcat, rcat, sems, send_sems, recv_sems, keep_sems = rest[
        n_pieces:
    ]
    edge = left_ref.shape[-1]
    span = pieces[0].shape[0]
    row_count = left_ref.shape[0]
    row_at = lax.axis_index("row")
    col_at = lax.axis_index("col")
    depth_at = lax.axis_index("depth")
    depth_count = lax.axis_size("depth")
    ahead = lax.rem(depth_at + 1, depth_count)
    behind = lax.rem(depth_at + depth_count - 1, depth_count)
    across = lax.rem(depth_at + 2, depth_count)

    barrier = pltpu.get_barrier_semaphore()
    for peer in (ahead, behind):
        pl.semaphore_signal(
            barrier, inc=1, device_id=(row_at, col_at, peer), device_id_type=MESH
        )
    pl.semaphore_wait(barrier, 2)

    copies = [
        pltpu.make_async_copy(piece, halo.at[pl.ds(k * span, span)], sems.at[k])
        for k, piece in enumerate(pieces)
    ]
    for copy in copies:
        copy.start()
    halo[n_pieces * span] = jnp.zeros((edge, edge), halo.dtype)
    for copy in copies:
        copy.wait()

    def spread(row, k):
        source = out_ref.at[row, pl.ds(0, n_own)]
        target = spread_ref.at[row, pl.ds(depth_at * n_own, n_own)]
        if k == 0:
            return pltpu.make_async_copy(source, target, send_sems.at[row, 0])
        return pltpu.make_async_remote_copy(
            src_ref=source,
            dst_ref=target,
            send_sem=send_sems.at[row, k],
            recv_sem=recv_sems.at[row, k],
            device_id=(row_at, col_at, ahead if k == 1 else behind),
            device_id_type=MESH,
        )

    def keep(row):
        return pltpu.make_async_copy(
            out_ref.at[row, pl.ds(n_own, n_own)],
            spread_ref.at[row, pl.ds(across * n_own, n_own)],
            keep_sems.at[row],
        )

    def products(row, first):
        for inner in range(n_inner):
            lcat[:, inner * edge:(inner + 1) * edge] = left_ref[row, inner]

        for part in range(n_own):
            for inner in range(n_inner):
                pick = table_pick(idx_ref, view, row, inner, first + part)
                rcat[inner * edge:(inner + 1) * edge, part * edge:(part + 1) * edge] = halo[pick]
        acc = jnp.dot(lcat[...], rcat[...], preferred_element_type=jnp.float32)
        for part in range(n_own):
            out_ref[row, first + part] = acc[:, part * edge:(part + 1) * edge].astype(out_ref.dtype)

    def own_body(row, carry):
        products(row, 0)
        for k in range(3):
            spread(row, k).start()
        return carry

    def across_body(row, carry):
        products(row, n_own)
        keep(row).start()
        return carry

    lax.fori_loop(0, row_count, own_body, 0)
    lax.fori_loop(0, row_count, across_body, 0)
    for row in range(row_count):
        for k in range(3):
            spread(row, k).wait()
        keep(row).wait()


def square_products(table, left, pieces, depth_count, n_own, view):
    rows, n_inner, edge = left.shape[0], left.shape[1], left.shape[2]
    flat_pieces = [piece.reshape(-1, edge, edge) for piece in pieces]
    span = flat_pieces[0].shape[0]
    operands = [table.reshape(-1), left] + flat_pieces
    vmem = pl.BlockSpec(memory_space=pltpu.VMEM)
    anywhere = pl.BlockSpec(memory_space=pl.ANY)
    in_specs = [pl.BlockSpec(memory_space=pltpu.SMEM), vmem] + [anywhere] * len(pieces)
    flops = 2 * rows * 2 * n_own * n_inner * edge ** 3
    moved = sum(int(x.size) * x.dtype.itemsize for x in operands) + rows * n_own * edge * edge * 10
    return pl.pallas_call(
        functools.partial(square_kernel, n_own, n_inner, len(pieces), view),
        out_shape=(
            jax.ShapeDtypeStruct((rows, 2 * n_own, edge, edge), jnp.bfloat16),
            jax.ShapeDtypeStruct((rows, depth_count * n_own, edge, edge), jnp.bfloat16),
        ),
        in_specs=in_specs,
        out_specs=(vmem, anywhere),
        scratch_shapes=[
            pltpu.VMEM((len(pieces) * span + 1, edge, edge), left.dtype),
            pltpu.VMEM((edge, n_inner * edge), left.dtype),
            pltpu.VMEM((n_inner * edge, n_own * edge), left.dtype),
            pltpu.SemaphoreType.DMA((len(pieces),)),
            pltpu.SemaphoreType.DMA((rows, 3)),
            pltpu.SemaphoreType.DMA((rows, 3)),
            pltpu.SemaphoreType.DMA((rows,)),
        ],
        compiler_params=pltpu.CompilerParams(
            vmem_limit_bytes=62 * 1024 * 1024, collective_id=0, has_side_effects=True
        ),
        cost_estimate=pl.CostEstimate(flops=flops, transcendentals=0, bytes_accessed=moved),
    )(*operands)


def halo_kernel(
    blocks_ref, full_ref, left_ref, right_ref, send_sems, recv_sems, side_send, side_recv,
    relay_sems,
):
    quarter = blocks_ref.shape[1]
    row_at = lax.axis_index("row")
    col_at = lax.axis_index("col")
    depth_at = lax.axis_index("depth")
    col_count = lax.axis_size("col")
    depth_count = lax.axis_size("depth")
    ring = lax.axis_size("row") * col_count
    place = row_at * col_count + col_at
    after = lax.rem(place + 1, ring)
    before = lax.rem(place + ring - 1, ring)
    after_id = (after // col_count, after % col_count, depth_at)
    before_id = (before // col_count, before % col_count, depth_at)
    peer_ids = [
        (row_at, col_at, lax.rem(depth_at + k, depth_count)) for k in range(1, depth_count)
    ]

    barrier = pltpu.get_barrier_semaphore()
    for device in peer_ids + [after_id, before_id]:
        pl.semaphore_signal(barrier, inc=1, device_id=device, device_id_type=MESH)
    pl.semaphore_wait(barrier, depth_count + 1)

    own = pl.ds(depth_at * quarter, quarter)
    rows = blocks_ref.shape[0]
    local = pltpu.make_async_copy(blocks_ref, full_ref.at[:, own], side_send.at[2, 0, 0])
    local.start()

    def to_peer(k, row):
        return pltpu.make_async_remote_copy(
            src_ref=blocks_ref.at[row],
            dst_ref=full_ref.at[row, own],
            send_sem=send_sems.at[k, row],
            recv_sem=recv_sems.at[k, row],
            device_id=peer_ids[k - 1],
            device_id_type=MESH,
        )

    def to_side(k, row, way):
        origin = lax.rem(depth_at + depth_count - k, depth_count)
        slot = pl.ds(origin * quarter, quarter)
        source = blocks_ref.at[row] if k == 0 else full_ref.at[row, slot]
        return pltpu.make_async_remote_copy(
            src_ref=source,
            dst_ref=(left_ref if way == 0 else right_ref).at[row, slot],
            send_sem=side_send.at[way, k, row],
            recv_sem=side_recv.at[way, k, row],
            device_id=after_id if way == 0 else before_id,
            device_id_type=MESH,
        )

    def slot_of(k):
        return pl.ds(lax.rem(depth_at + depth_count - k, depth_count) * quarter, quarter)

    def relay(row):
        k, target = (1, peer_ids[0]) if row < rows // 2 else (3, peer_ids[2])
        return pltpu.make_async_remote_copy(
            src_ref=full_ref.at[row, slot_of(k)],
            dst_ref=full_ref.at[row, slot_of(k)],
            send_sem=relay_sems.at[0, row],
            recv_sem=relay_sems.at[1, row],
            device_id=target,
            device_id_type=MESH,
        )

    for k in (1, 3):
        for row in range(rows):
            to_peer(k, row).start()
    for row in range(rows):
        for way in range(2):
            to_side(0, row, way).start()
    for row in range(rows):
        for k in (1, 3):
            to_peer(k, row).wait_recv()
            for way in range(2):
                to_side(k, row, way).start()
            if (k == 1) == (row < rows // 2):
                relay(row).start()
    for row in range(rows):
        relay(row).wait_recv()
        for way in range(2):
            to_side(2, row, way).start()
    local.wait()
    for row in range(rows):
        for k in (1, 3):
            to_peer(k, row).wait_send()
        relay(row).wait_send()
    for k in range(depth_count):
        for row in range(rows):
            for way in range(2):
                to_side(k, row, way).wait()


def halo_exchange(blocks, depth_count):
    rows, quarter, edge = blocks.shape[0], blocks.shape[1], blocks.shape[2]
    whole = jax.ShapeDtypeStruct((rows, depth_count * quarter, edge, edge), blocks.dtype)
    anywhere = pl.BlockSpec(memory_space=pl.ANY)
    moved = int(blocks.size) * blocks.dtype.itemsize * (3 * depth_count + 3)
    return pl.pallas_call(
        halo_kernel,
        out_shape=(whole, whole, whole),
        in_specs=[anywhere],
        out_specs=(anywhere, anywhere, anywhere),
        scratch_shapes=[
            pltpu.SemaphoreType.DMA((depth_count, rows)),
            pltpu.SemaphoreType.DMA((depth_count, rows)),
            pltpu.SemaphoreType.DMA((3, depth_count, rows)),
            pltpu.SemaphoreType.DMA((2, depth_count, rows)),
            pltpu.SemaphoreType.DMA((2, rows)),
        ],
        compiler_params=pltpu.CompilerParams(collective_id=1, has_side_effects=True),
        cost_estimate=pl.CostEstimate(flops=0, transcendentals=0, bytes_accessed=moved),
    )(blocks)


def local(blocks, block_cols, product_cols):
    row_count = blocks.shape[0]
    block_edge = blocks.shape[2]
    fill_count = block_cols.shape[1]
    order_total = row_count * lax.axis_size(("row", "col"))
    row_place = lax.axis_index(("row", "col"))
    depth_index = lax.axis_index("depth")
    depth_count = lax.axis_size("depth")
    target_share = product_cols.shape[1] // depth_count

    full_rows, from_before, from_after = halo_exchange(blocks, depth_count)
    near = {0: full_rows, 1: from_before, -1: from_after}
    near[2] = shifted(near[1], ("row", "col"), 1)
    near[-2] = shifted(near[-1], ("row", "col"), -1)

    def halo_of(reach):
        return [near[offset] for offset in range(reach, -reach - 1, -1)]

    own_cols = lax.dynamic_slice_in_dim(block_cols, row_place * row_count, row_count, 0)
    own_targets = lax.dynamic_slice_in_dim(
        product_cols, depth_index * target_share, target_share, 1
    )

    across_targets = lax.dynamic_slice_in_dim(
        product_cols, ((depth_index + 2) % depth_count) * target_share, target_share, 1
    )
    halo_first = halo_of(1)
    halo_second = halo_of(2)
    piece_blocks = row_count * fill_count
    inner_rows = jnp.concatenate([own_cols, product_cols], axis=1)
    targets = jnp.concatenate([own_targets, across_targets], axis=1)
    table = block_table(
        block_cols, inner_rows, targets, (row_place - 2) * row_count, order_total,
        fill_count, len(halo_second) * piece_blocks,
    )
    row_stride = inner_rows.shape[1] * targets.shape[1]
    first_view = (row_stride, 0, targets.shape[1], piece_blocks, len(halo_first) * piece_blocks)
    second_view = (row_stride, fill_count, targets.shape[1], 0, len(halo_second) * piece_blocks)
    square, square_rows = square_products(
        table, full_rows, halo_first, depth_count, target_share, first_view
    )
    return block_products(
        table, square_rows, halo_second, target_share, second_view, own=square
    )


def solution(mesh):
    placed = (P(("row", "col"), "depth", None, None), P(), P(("row", "col"), None))
    return jax.shard_map(
        local,
        mesh=mesh,
        in_specs=placed,
        out_specs=P(("row", "col"), "depth", None, None),
        check_vma=False,
    )
```

```python
import functools

import jax
import jax.numpy as jnp
from jax import lax
from jax.experimental import pallas as pl
from jax.experimental.pallas import tpu as pltpu
from jax.sharding import PartitionSpec as P


def shifted(value, axis, steps):
    count = lax.axis_size(axis)
    pairs = [(source, (source + steps) % count) for source in range(count)]
    return lax.ppermute(value, axis, pairs)


def block_table(block_cols, rows, targets, start_row, order_total, fill_count, miss):
    cols_of = block_cols[rows]
    matches = cols_of[:, :, None, :] == targets[:, None, :, None]
    has_match = jnp.any(matches, axis=3)
    slot_ids = jnp.arange(fill_count, dtype=jnp.int32)[None, None, None, :]
    position = jnp.sum(jnp.where(matches, slot_ids, 0), axis=3)
    local_rows = (rows - start_row) % order_total
    flat = local_rows[:, :, None] * fill_count + position
    flat = jnp.clip(flat, 0, miss)
    return jnp.where(has_match, flat, miss).astype(jnp.int32)


def table_pick(idx_ref, view, row, inner, col):
    row_stride, first, inner_stride, shift, cap = view
    entry = idx_ref[row * row_stride + (first + inner) * inner_stride + col]
    return jnp.minimum(jnp.maximum(entry - shift, 0), cap)


def product_kernel(n_out, n_inner, n_pieces, final, view, idx_ref, left_ref, *rest):
    pieces = rest[:n_pieces]
    rest = rest[n_pieces:]
    if final:
        own_ref, out_ref, halo, lcat, rcat, sems = rest
    else:
        out_ref, halo, lcat, rcat, sems = rest
    edge = left_ref.shape[-1]
    span = pieces[0].shape[0]
    copies = [
        pltpu.make_async_copy(piece, halo.at[pl.ds(k * span, span)], sems.at[k])
        for k, piece in enumerate(pieces)
    ]
    for copy in copies:
        copy.start()
    halo[n_pieces * span] = jnp.zeros((edge, edge), halo.dtype)
    for copy in copies:
        copy.wait()

    def row_body(row, carry):
        for inner in range(n_inner):
            lcat[:, inner * edge:(inner + 1) * edge] = left_ref[row, inner]

        for col in range(n_out):
            for inner in range(n_inner):
                pick = table_pick(idx_ref, view, row, inner, col)
                rcat[inner * edge:(inner + 1) * edge, col * edge:(col + 1) * edge] = halo[pick]
        acc = jnp.dot(lcat[...], rcat[...], preferred_element_type=jnp.float32)
        for col in range(n_out):
            part = acc[:, col * edge:(col + 1) * edge]
            if final:
                value = 3.0 * own_ref[row, col].astype(jnp.float32) - 2.0 * part
            else:
                value = part
            out_ref[row, col] = value.astype(out_ref.dtype)
        return carry

    lax.fori_loop(0, left_ref.shape[0], row_body, 0)


def block_products(table, left, pieces, n_out, view, own=None):
    rows, n_inner, edge = left.shape[0], left.shape[1], left.shape[2]
    final = own is not None
    flat_pieces = [piece.reshape(-1, edge, edge) for piece in pieces]
    span = flat_pieces[0].shape[0]
    operands = [table.reshape(-1), left] + flat_pieces + ([own] if final else [])
    vmem = pl.BlockSpec(memory_space=pltpu.VMEM)
    anywhere = pl.BlockSpec(memory_space=pl.ANY)
    in_specs = [pl.BlockSpec(memory_space=pltpu.SMEM), vmem] + [anywhere] * len(pieces)
    in_specs += [vmem] if final else []
    flops = 2 * rows * n_out * n_inner * edge ** 3
    moved = sum(int(x.size) * x.dtype.itemsize for x in operands) + rows * n_out * edge * edge * 2
    return pl.pallas_call(
        functools.partial(product_kernel, n_out, n_inner, len(pieces), final, view),
        out_shape=jax.ShapeDtypeStruct((rows, n_out, edge, edge), jnp.bfloat16),
        in_specs=in_specs,
        out_specs=vmem,
        scratch_shapes=[
            pltpu.VMEM((len(pieces) * span + 1, edge, edge), left.dtype),
            pltpu.VMEM((edge, n_inner * edge), left.dtype),
            pltpu.VMEM((n_inner * edge, n_out * edge), left.dtype),
            pltpu.SemaphoreType.DMA((len(pieces),)),
        ],
        compiler_params=pltpu.CompilerParams(vmem_limit_bytes=62 * 1024 * 1024),
        cost_estimate=pl.CostEstimate(flops=flops, transcendentals=0, bytes_accessed=moved),
    )(*operands)


MESH = pl.DeviceIdType.MESH


def square_kernel(n_own, n_inner, n_pieces, view, idx_ref, left_ref, *rest):
    pieces = rest[:n_pieces]
    out_ref, spread_ref, halo, lcat, rcat, sems, send_sems, recv_sems, keep_sems = rest[
        n_pieces:
    ]
    edge = left_ref.shape[-1]
    span = pieces[0].shape[0]
    row_count = left_ref.shape[0]
    row_at = lax.axis_index("row")
    col_at = lax.axis_index("col")
    depth_at = lax.axis_index("depth")
    depth_count = lax.axis_size("depth")
    ahead = lax.rem(depth_at + 1, depth_count)
    behind = lax.rem(depth_at + depth_count - 1, depth_count)
    across = lax.rem(depth_at + 2, depth_count)

    barrier = pltpu.get_barrier_semaphore()
    for peer in (ahead, behind):
        pl.semaphore_signal(
            barrier, inc=1, device_id=(row_at, col_at, peer), device_id_type=MESH
        )
    pl.semaphore_wait(barrier, 2)

    copies = [
        pltpu.make_async_copy(piece, halo.at[pl.ds(k * span, span)], sems.at[k])
        for k, piece in enumerate(pieces)
    ]
    for copy in copies:
        copy.start()
    halo[n_pieces * span] = jnp.zeros((edge, edge), halo.dtype)
    for copy in copies:
        copy.wait()

    def spread(row, k):
        source = out_ref.at[row, pl.ds(0, n_own)]
        target = spread_ref.at[row, pl.ds(depth_at * n_own, n_own)]
        if k == 0:
            return pltpu.make_async_copy(source, target, send_sems.at[row, 0])
        return pltpu.make_async_remote_copy(
            src_ref=source,
            dst_ref=target,
            send_sem=send_sems.at[row, k],
            recv_sem=recv_sems.at[row, k],
            device_id=(row_at, col_at, ahead if k == 1 else behind),
            device_id_type=MESH,
        )

    def keep(row):
        return pltpu.make_async_copy(
            out_ref.at[row, pl.ds(n_own, n_own)],
            spread_ref.at[row, pl.ds(across * n_own, n_own)],
            keep_sems.at[row],
        )

    def products(row, first):
        for inner in range(n_inner):
            lcat[:, inner * edge:(inner + 1) * edge] = left_ref[row, inner]

        for part in range(n_own):
            for inner in range(n_inner):
                pick = table_pick(idx_ref, view, row, inner, first + part)
                rcat[inner * edge:(inner + 1) * edge, part * edge:(part + 1) * edge] = halo[pick]
        acc = jnp.dot(lcat[...], rcat[...], preferred_element_type=jnp.float32)
        for part in range(n_own):
            out_ref[row, first + part] = acc[:, part * edge:(part + 1) * edge].astype(out_ref.dtype)

    def own_body(row, carry):
        products(row, 0)
        for k in range(3):
            spread(row, k).start()
        return carry

    def across_body(row, carry):
        products(row, n_own)
        keep(row).start()
        return carry

    lax.fori_loop(0, row_count, own_body, 0)
    lax.fori_loop(0, row_count, across_body, 0)
    for row in range(row_count):
        for k in range(3):
            spread(row, k).wait()
        keep(row).wait()


def square_products(table, left, pieces, depth_count, n_own, view):
    rows, n_inner, edge = left.shape[0], left.shape[1], left.shape[2]
    flat_pieces = [piece.reshape(-1, edge, edge) for piece in pieces]
    span = flat_pieces[0].shape[0]
    operands = [table.reshape(-1), left] + flat_pieces
    vmem = pl.BlockSpec(memory_space=pltpu.VMEM)
    anywhere = pl.BlockSpec(memory_space=pl.ANY)
    in_specs = [pl.BlockSpec(memory_space=pltpu.SMEM), vmem] + [anywhere] * len(pieces)
    flops = 2 * rows * 2 * n_own * n_inner * edge ** 3
    moved = sum(int(x.size) * x.dtype.itemsize for x in operands) + rows * n_own * edge * edge * 10
    return pl.pallas_call(
        functools.partial(square_kernel, n_own, n_inner, len(pieces), view),
        out_shape=(
            jax.ShapeDtypeStruct((rows, 2 * n_own, edge, edge), jnp.bfloat16),
            jax.ShapeDtypeStruct((rows, depth_count * n_own, edge, edge), jnp.bfloat16),
        ),
        in_specs=in_specs,
        out_specs=(vmem, anywhere),
        scratch_shapes=[
            pltpu.VMEM((len(pieces) * span + 1, edge, edge), left.dtype),
            pltpu.VMEM((edge, n_inner * edge), left.dtype),
            pltpu.VMEM((n_inner * edge, n_own * edge), left.dtype),
            pltpu.SemaphoreType.DMA((len(pieces),)),
            pltpu.SemaphoreType.DMA((rows, 3)),
            pltpu.SemaphoreType.DMA((rows, 3)),
            pltpu.SemaphoreType.DMA((rows,)),
        ],
        compiler_params=pltpu.CompilerParams(
            vmem_limit_bytes=62 * 1024 * 1024, collective_id=0, has_side_effects=True
        ),
        cost_estimate=pl.CostEstimate(flops=flops, transcendentals=0, bytes_accessed=moved),
    )(*operands)


def halo_kernel(
    blocks_ref, full_ref, left_ref, right_ref, send_sems, recv_sems, side_send, side_recv,
    relay_sems,
):
    quarter = blocks_ref.shape[1]
    row_at = lax.axis_index("row")
    col_at = lax.axis_index("col")
    depth_at = lax.axis_index("depth")
    col_count = lax.axis_size("col")
    depth_count = lax.axis_size("depth")
    ring = lax.axis_size("row") * col_count
    place = row_at * col_count + col_at
    after = lax.rem(place + 1, ring)
    before = lax.rem(place + ring - 1, ring)
    after_id = (after // col_count, after % col_count, depth_at)
    before_id = (before // col_count, before % col_count, depth_at)
    peer_ids = [
        (row_at, col_at, lax.rem(depth_at + k, depth_count)) for k in range(1, depth_count)
    ]

    barrier = pltpu.get_barrier_semaphore()
    for device in peer_ids + [after_id, before_id]:
        pl.semaphore_signal(barrier, inc=1, device_id=device, device_id_type=MESH)
    pl.semaphore_wait(barrier, depth_count + 1)

    own = pl.ds(depth_at * quarter, quarter)
    rows = blocks_ref.shape[0]
    local = pltpu.make_async_copy(blocks_ref, full_ref.at[:, own], side_send.at[2, 0, 0])
    local.start()

    def to_peer(k, row):
        return pltpu.make_async_remote_copy(
            src_ref=blocks_ref.at[row],
            dst_ref=full_ref.at[row, own],
            send_sem=send_sems.at[k, row],
            recv_sem=recv_sems.at[k, row],
            device_id=peer_ids[k - 1],
            device_id_type=MESH,
        )

    def to_side(k, row, way):
        origin = lax.rem(depth_at + depth_count - k, depth_count)
        slot = pl.ds(origin * quarter, quarter)
        source = blocks_ref.at[row] if k == 0 else full_ref.at[row, slot]
        return pltpu.make_async_remote_copy(
            src_ref=source,
            dst_ref=(left_ref if way == 0 else right_ref).at[row, slot],
            send_sem=side_send.at[way, k, row],
            recv_sem=side_recv.at[way, k, row],
            device_id=after_id if way == 0 else before_id,
            device_id_type=MESH,
        )

    def slot_of(k):
        return pl.ds(lax.rem(depth_at + depth_count - k, depth_count) * quarter, quarter)

    def relay(row):
        k, target = (1, peer_ids[0]) if row < rows // 2 else (3, peer_ids[2])
        return pltpu.make_async_remote_copy(
            src_ref=full_ref.at[row, slot_of(k)],
            dst_ref=full_ref.at[row, slot_of(k)],
            send_sem=relay_sems.at[0, row],
            recv_sem=relay_sems.at[1, row],
            device_id=target,
            device_id_type=MESH,
        )

    for k in (1, 3):
        for row in range(rows):
            to_peer(k, row).start()
    for row in range(rows):
        for way in range(2):
            to_side(0, row, way).start()
    for row in range(rows):
        for k in (1, 3):
            to_peer(k, row).wait_recv()
            for way in range(2):
                to_side(k, row, way).start()
            if (k == 1) == (row < rows // 2):
                relay(row).start()
    for row in range(rows):
        relay(row).wait_recv()
        for way in range(2):
            to_side(2, row, way).start()
    local.wait()
    for row in range(rows):
        for k in (1, 3):
            to_peer(k, row).wait_send()
        relay(row).wait_send()
    for k in range(depth_count):
        for row in range(rows):
            for way in range(2):
                to_side(k, row, way).wait()


def halo_exchange(blocks, depth_count):
    rows, quarter, edge = blocks.shape[0], blocks.shape[1], blocks.shape[2]
    whole = jax.ShapeDtypeStruct((rows, depth_count * quarter, edge, edge), blocks.dtype)
    anywhere = pl.BlockSpec(memory_space=pl.ANY)
    moved = int(blocks.size) * blocks.dtype.itemsize * (3 * depth_count + 3)
    return pl.pallas_call(
        halo_kernel,
        out_shape=(whole, whole, whole),
        in_specs=[anywhere],
        out_specs=(anywhere, anywhere, anywhere),
        scratch_shapes=[
            pltpu.SemaphoreType.DMA((depth_count, rows)),
            pltpu.SemaphoreType.DMA((depth_count, rows)),
            pltpu.SemaphoreType.DMA((3, depth_count, rows)),
            pltpu.SemaphoreType.DMA((2, depth_count, rows)),
            pltpu.SemaphoreType.DMA((2, rows)),
        ],
        compiler_params=pltpu.CompilerParams(collective_id=1, has_side_effects=True),
        cost_estimate=pl.CostEstimate(flops=0, transcendentals=0, bytes_accessed=moved),
    )(blocks)


def local(blocks, block_cols, product_cols):
    row_count = blocks.shape[0]
    block_edge = blocks.shape[2]
    fill_count = block_cols.shape[1]
    order_total = row_count * lax.axis_size(("row", "col"))
    row_place = lax.axis_index(("row", "col"))
    depth_index = lax.axis_index("depth")
    depth_count = lax.axis_size("depth")
    target_share = product_cols.shape[1] // depth_count

    full_rows, from_before, from_after = halo_exchange(blocks, depth_count)
    near = {0: full_rows, 1: from_before, -1: from_after}

    def halo_of(reach):
        return [near[offset] for offset in range(reach, -reach - 1, -1)]

    own_cols = lax.dynamic_slice_in_dim(block_cols, row_place * row_count, row_count, 0)
    own_targets = lax.dynamic_slice_in_dim(
        product_cols, depth_index * target_share, target_share, 1
    )

    across_targets = lax.dynamic_slice_in_dim(
        product_cols, ((depth_index + 2) % depth_count) * target_share, target_share, 1
    )
    piece_blocks = row_count * fill_count
    block_cols, product_cols, near[1] = lax.optimization_barrier(
        (block_cols, product_cols, near[1])
    )
    inner_rows = jnp.concatenate([own_cols, product_cols], axis=1)
    targets = jnp.concatenate([own_targets, across_targets], axis=1)
    table = block_table(
        block_cols, inner_rows, targets, (row_place - 2) * row_count, order_total,
        fill_count, 5 * piece_blocks,
    )
    table, near[1], near[-1] = lax.optimization_barrier((table, near[1], near[-1]))
    near[2] = shifted(near[1], ("row", "col"), 1)
    near[-2] = shifted(near[-1], ("row", "col"), -1)
    halo_first = halo_of(1)
    halo_second = halo_of(2)
    row_stride = inner_rows.shape[1] * targets.shape[1]
    first_view = (row_stride, 0, targets.shape[1], piece_blocks, len(halo_first) * piece_blocks)
    second_view = (row_stride, fill_count, targets.shape[1], 0, len(halo_second) * piece_blocks)
    square, square_rows = square_products(
        table, full_rows, halo_first, depth_count, target_share, first_view
    )
    return block_products(
        table, square_rows, halo_second, target_share, second_view, own=square
    )


def solution(mesh):
    placed = (P(("row", "col"), "depth", None, None), P(), P(("row", "col"), None))
    return jax.shard_map(
        local,
        mesh=mesh,
        in_specs=placed,
        out_specs=P(("row", "col"), "depth", None, None),
        check_vma=False,
    )
```

```python
import functools

import jax
import jax.numpy as jnp
from jax import lax
from jax.experimental import pallas as pl
from jax.experimental.pallas import tpu as pltpu
from jax.sharding import PartitionSpec as P


def shifted(value, axis, steps):
    count = lax.axis_size(axis)
    pairs = [(source, (source + steps) % count) for source in range(count)]
    return lax.ppermute(value, axis, pairs)


def block_table(block_cols, rows, targets, start_row, order_total, fill_count, miss):
    cols_of = block_cols[rows]
    matches = cols_of[:, :, None, :] == targets[:, None, :, None]
    has_match = jnp.any(matches, axis=3)
    slot_ids = jnp.arange(fill_count, dtype=jnp.int32)[None, None, None, :]
    position = jnp.sum(jnp.where(matches, slot_ids, 0), axis=3)
    local_rows = (rows - start_row) % order_total
    flat = local_rows[:, :, None] * fill_count + position
    flat = jnp.clip(flat, 0, miss)
    return jnp.where(has_match, flat, miss).astype(jnp.int32)


def table_pick(idx_ref, view, row, inner, col):
    row_stride, first, inner_stride, shift, cap = view
    entry = idx_ref[row * row_stride + (first + inner) * inner_stride + col]
    return jnp.minimum(jnp.maximum(entry - shift, 0), cap)


def product_kernel(n_out, n_inner, n_pieces, final, view, idx_ref, left_ref, *rest):
    pieces = rest[:n_pieces]
    rest = rest[n_pieces:]
    if final:
        own_ref, out_ref, halo, lcat, rcat, sems = rest
    else:
        out_ref, halo, lcat, rcat, sems = rest
    edge = left_ref.shape[-1]
    span = pieces[0].shape[0]
    copies = [
        pltpu.make_async_copy(piece, halo.at[pl.ds(k * span, span)], sems.at[k])
        for k, piece in enumerate(pieces)
    ]
    for copy in copies:
        copy.start()
    halo[n_pieces * span] = jnp.zeros((edge, edge), halo.dtype)
    for copy in copies:
        copy.wait()

    def row_body(row, carry):
        for inner in range(n_inner):
            lcat[:, inner * edge:(inner + 1) * edge] = left_ref[row, inner]

        for col in range(n_out):
            for inner in range(n_inner):
                pick = table_pick(idx_ref, view, row, inner, col)
                rcat[inner * edge:(inner + 1) * edge, col * edge:(col + 1) * edge] = halo[pick]
        acc = jnp.dot(lcat[...], rcat[...], preferred_element_type=jnp.float32)
        for col in range(n_out):
            part = acc[:, col * edge:(col + 1) * edge]
            if final:
                value = 3.0 * own_ref[row, col].astype(jnp.float32) - 2.0 * part
            else:
                value = part
            out_ref[row, col] = value.astype(out_ref.dtype)
        return carry

    lax.fori_loop(0, left_ref.shape[0], row_body, 0)


def block_products(table, left, pieces, n_out, view, own=None):
    rows, n_inner, edge = left.shape[0], left.shape[1], left.shape[2]
    final = own is not None
    flat_pieces = [piece.reshape(-1, edge, edge) for piece in pieces]
    span = flat_pieces[0].shape[0]
    operands = [table.reshape(-1), left] + flat_pieces + ([own] if final else [])
    vmem = pl.BlockSpec(memory_space=pltpu.VMEM)
    anywhere = pl.BlockSpec(memory_space=pl.ANY)
    in_specs = [pl.BlockSpec(memory_space=pltpu.SMEM), vmem] + [anywhere] * len(pieces)
    in_specs += [vmem] if final else []
    flops = 2 * rows * n_out * n_inner * edge ** 3
    moved = sum(int(x.size) * x.dtype.itemsize for x in operands) + rows * n_out * edge * edge * 2
    return pl.pallas_call(
        functools.partial(product_kernel, n_out, n_inner, len(pieces), final, view),
        out_shape=jax.ShapeDtypeStruct((rows, n_out, edge, edge), jnp.bfloat16),
        in_specs=in_specs,
        out_specs=vmem,
        scratch_shapes=[
            pltpu.VMEM((len(pieces) * span + 1, edge, edge), left.dtype),
            pltpu.VMEM((edge, n_inner * edge), left.dtype),
            pltpu.VMEM((n_inner * edge, n_out * edge), left.dtype),
            pltpu.SemaphoreType.DMA((len(pieces),)),
        ],
        compiler_params=pltpu.CompilerParams(vmem_limit_bytes=62 * 1024 * 1024),
        cost_estimate=pl.CostEstimate(flops=flops, transcendentals=0, bytes_accessed=moved),
    )(*operands)


MESH = pl.DeviceIdType.MESH


def square_kernel(n_own, n_inner, n_pieces, view, idx_ref, left_ref, *rest):
    pieces = rest[:n_pieces]
    out_ref, spread_ref, halo, lcat, rcat, sems, send_sems, recv_sems, keep_sems = rest[
        n_pieces:
    ]
    edge = left_ref.shape[-1]
    span = pieces[0].shape[0]
    row_count = left_ref.shape[0]
    row_at = lax.axis_index("row")
    col_at = lax.axis_index("col")
    depth_at = lax.axis_index("depth")
    depth_count = lax.axis_size("depth")
    ahead = lax.rem(depth_at + 1, depth_count)
    behind = lax.rem(depth_at + depth_count - 1, depth_count)
    across = lax.rem(depth_at + 2, depth_count)

    barrier = pltpu.get_barrier_semaphore()
    for peer in (ahead, behind):
        pl.semaphore_signal(
            barrier, inc=1, device_id=(row_at, col_at, peer), device_id_type=MESH
        )
    pl.semaphore_wait(barrier, 2)

    copies = [
        pltpu.make_async_copy(piece, halo.at[pl.ds(k * span, span)], sems.at[k])
        for k, piece in enumerate(pieces)
    ]
    for copy in copies:
        copy.start()
    halo[n_pieces * span] = jnp.zeros((edge, edge), halo.dtype)
    for copy in copies:
        copy.wait()

    def spread(row, k):
        source = out_ref.at[row, pl.ds(0, n_own)]
        target = spread_ref.at[row, pl.ds(depth_at * n_own, n_own)]
        if k == 0:
            return pltpu.make_async_copy(source, target, send_sems.at[row, 0])
        return pltpu.make_async_remote_copy(
            src_ref=source,
            dst_ref=target,
            send_sem=send_sems.at[row, k],
            recv_sem=recv_sems.at[row, k],
            device_id=(row_at, col_at, ahead if k == 1 else behind),
            device_id_type=MESH,
        )

    def keep(row):
        return pltpu.make_async_copy(
            out_ref.at[row, pl.ds(n_own, n_own)],
            spread_ref.at[row, pl.ds(across * n_own, n_own)],
            keep_sems.at[row],
        )

    def products(row, first):
        for inner in range(n_inner):
            lcat[:, inner * edge:(inner + 1) * edge] = left_ref[row, inner]

        for part in range(n_own):
            for inner in range(n_inner):
                pick = table_pick(idx_ref, view, row, inner, first + part)
                rcat[inner * edge:(inner + 1) * edge, part * edge:(part + 1) * edge] = halo[pick]
        acc = jnp.dot(lcat[...], rcat[...], preferred_element_type=jnp.float32)
        for part in range(n_own):
            out_ref[row, first + part] = acc[:, part * edge:(part + 1) * edge].astype(out_ref.dtype)

    def own_body(row, carry):
        products(row, 0)
        for k in range(3):
            spread(row, k).start()
        return carry

    def across_body(row, carry):
        products(row, n_own)
        keep(row).start()
        return carry

    lax.fori_loop(0, row_count, own_body, 0)
    lax.fori_loop(0, row_count, across_body, 0)
    for row in range(row_count):
        for k in range(3):
            spread(row, k).wait()
        keep(row).wait()


def square_products(table, left, pieces, depth_count, n_own, view):
    rows, n_inner, edge = left.shape[0], left.shape[1], left.shape[2]
    flat_pieces = [piece.reshape(-1, edge, edge) for piece in pieces]
    span = flat_pieces[0].shape[0]
    operands = [table.reshape(-1), left] + flat_pieces
    vmem = pl.BlockSpec(memory_space=pltpu.VMEM)
    anywhere = pl.BlockSpec(memory_space=pl.ANY)
    in_specs = [pl.BlockSpec(memory_space=pltpu.SMEM), vmem] + [anywhere] * len(pieces)
    flops = 2 * rows * 2 * n_own * n_inner * edge ** 3
    moved = sum(int(x.size) * x.dtype.itemsize for x in operands) + rows * n_own * edge * edge * 10
    return pl.pallas_call(
        functools.partial(square_kernel, n_own, n_inner, len(pieces), view),
        out_shape=(
            jax.ShapeDtypeStruct((rows, 2 * n_own, edge, edge), jnp.bfloat16),
            jax.ShapeDtypeStruct((rows, depth_count * n_own, edge, edge), jnp.bfloat16),
        ),
        in_specs=in_specs,
        out_specs=(vmem, anywhere),
        scratch_shapes=[
            pltpu.VMEM((len(pieces) * span + 1, edge, edge), left.dtype),
            pltpu.VMEM((edge, n_inner * edge), left.dtype),
            pltpu.VMEM((n_inner * edge, n_own * edge), left.dtype),
            pltpu.SemaphoreType.DMA((len(pieces),)),
            pltpu.SemaphoreType.DMA((rows, 3)),
            pltpu.SemaphoreType.DMA((rows, 3)),
            pltpu.SemaphoreType.DMA((rows,)),
        ],
        compiler_params=pltpu.CompilerParams(
            vmem_limit_bytes=62 * 1024 * 1024, collective_id=0, has_side_effects=True
        ),
        cost_estimate=pl.CostEstimate(flops=flops, transcendentals=0, bytes_accessed=moved),
    )(*operands)


def halo_kernel(
    blocks_ref, full_ref, left_ref, right_ref, send_sems, recv_sems, side_send, side_recv,
    relay_sems,
):
    quarter = blocks_ref.shape[1]
    row_at = lax.axis_index("row")
    col_at = lax.axis_index("col")
    depth_at = lax.axis_index("depth")
    col_count = lax.axis_size("col")
    depth_count = lax.axis_size("depth")
    ring = lax.axis_size("row") * col_count
    place = row_at * col_count + col_at
    after = lax.rem(place + 1, ring)
    before = lax.rem(place + ring - 1, ring)
    after_id = (after // col_count, after % col_count, depth_at)
    before_id = (before // col_count, before % col_count, depth_at)
    peer_ids = [
        (row_at, col_at, lax.rem(depth_at + k, depth_count)) for k in range(1, depth_count)
    ]

    barrier = pltpu.get_barrier_semaphore()
    for device in peer_ids + [after_id, before_id]:
        pl.semaphore_signal(barrier, inc=1, device_id=device, device_id_type=MESH)
    pl.semaphore_wait(barrier, depth_count + 1)

    own = pl.ds(depth_at * quarter, quarter)
    rows = blocks_ref.shape[0]
    local = pltpu.make_async_copy(blocks_ref, full_ref.at[:, own], side_send.at[2, 0, 0])
    local.start()

    def to_peer(k, row):
        return pltpu.make_async_remote_copy(
            src_ref=blocks_ref.at[row],
            dst_ref=full_ref.at[row, own],
            send_sem=send_sems.at[k, row],
            recv_sem=recv_sems.at[k, row],
            device_id=peer_ids[k - 1],
            device_id_type=MESH,
        )

    def to_side(k, row, way):
        origin = lax.rem(depth_at + depth_count - k, depth_count)
        slot = pl.ds(origin * quarter, quarter)
        source = blocks_ref.at[row] if k == 0 else full_ref.at[row, slot]
        return pltpu.make_async_remote_copy(
            src_ref=source,
            dst_ref=(left_ref if way == 0 else right_ref).at[row, slot],
            send_sem=side_send.at[way, k, row],
            recv_sem=side_recv.at[way, k, row],
            device_id=after_id if way == 0 else before_id,
            device_id_type=MESH,
        )

    def slot_of(k):
        return pl.ds(lax.rem(depth_at + depth_count - k, depth_count) * quarter, quarter)

    def relay(row):
        k, target = (1, peer_ids[0]) if row < rows // 2 else (3, peer_ids[2])
        return pltpu.make_async_remote_copy(
            src_ref=full_ref.at[row, slot_of(k)],
            dst_ref=full_ref.at[row, slot_of(k)],
            send_sem=relay_sems.at[0, row],
            recv_sem=relay_sems.at[1, row],
            device_id=target,
            device_id_type=MESH,
        )

    order = {1: list(range(rows)), 3: list(range(rows - 1, -1, -1))}
    for step in range(rows):
        for k in (1, 3):
            to_peer(k, order[k][step]).start()
    for row in range(rows):
        for way in range(2):
            to_side(0, row, way).start()
    for step in range(rows):
        for k in (1, 3):
            row = order[k][step]
            to_peer(k, row).wait_recv()
            if (k == 1) == (row < rows // 2):
                relay(row).start()
            for way in range(2):
                to_side(k, row, way).start()
    for step in range(rows // 2):
        for row in (step, rows - 1 - step):
            relay(row).wait_recv()
            for way in range(2):
                to_side(2, row, way).start()
    local.wait()
    for row in range(rows):
        for k in (1, 3):
            to_peer(k, row).wait_send()
        relay(row).wait_send()
    for k in range(depth_count):
        for row in range(rows):
            for way in range(2):
                to_side(k, row, way).wait()


def halo_exchange(blocks, depth_count):
    rows, quarter, edge = blocks.shape[0], blocks.shape[1], blocks.shape[2]
    whole = jax.ShapeDtypeStruct((rows, depth_count * quarter, edge, edge), blocks.dtype)
    anywhere = pl.BlockSpec(memory_space=pl.ANY)
    moved = int(blocks.size) * blocks.dtype.itemsize * (3 * depth_count + 3)
    return pl.pallas_call(
        halo_kernel,
        out_shape=(whole, whole, whole),
        in_specs=[anywhere],
        out_specs=(anywhere, anywhere, anywhere),
        scratch_shapes=[
            pltpu.SemaphoreType.DMA((depth_count, rows)),
            pltpu.SemaphoreType.DMA((depth_count, rows)),
            pltpu.SemaphoreType.DMA((3, depth_count, rows)),
            pltpu.SemaphoreType.DMA((2, depth_count, rows)),
            pltpu.SemaphoreType.DMA((2, rows)),
        ],
        compiler_params=pltpu.CompilerParams(collective_id=1, has_side_effects=True),
        cost_estimate=pl.CostEstimate(flops=0, transcendentals=0, bytes_accessed=moved),
    )(blocks)


def local(blocks, block_cols, product_cols):
    row_count = blocks.shape[0]
    block_edge = blocks.shape[2]
    fill_count = block_cols.shape[1]
    order_total = row_count * lax.axis_size(("row", "col"))
    row_place = lax.axis_index(("row", "col"))
    depth_index = lax.axis_index("depth")
    depth_count = lax.axis_size("depth")
    target_share = product_cols.shape[1] // depth_count

    full_rows, from_before, from_after = halo_exchange(blocks, depth_count)
    near = {0: full_rows, 1: from_before, -1: from_after}
    near[2] = shifted(near[1], ("row", "col"), 1)
    near[-2] = shifted(near[-1], ("row", "col"), -1)

    def halo_of(reach):
        return [near[offset] for offset in range(reach, -reach - 1, -1)]

    own_cols = lax.dynamic_slice_in_dim(block_cols, row_place * row_count, row_count, 0)
    own_targets = lax.dynamic_slice_in_dim(
        product_cols, depth_index * target_share, target_share, 1
    )

    across_targets = lax.dynamic_slice_in_dim(
        product_cols, ((depth_index + 2) % depth_count) * target_share, target_share, 1
    )
    halo_first = halo_of(1)
    halo_second = halo_of(2)
    piece_blocks = row_count * fill_count
    inner_rows = jnp.concatenate([own_cols, product_cols], axis=1)
    targets = jnp.concatenate([own_targets, across_targets], axis=1)
    table = block_table(
        block_cols, inner_rows, targets, (row_place - 2) * row_count, order_total,
        fill_count, len(halo_second) * piece_blocks,
    )
    row_stride = inner_rows.shape[1] * targets.shape[1]
    first_view = (row_stride, 0, targets.shape[1], piece_blocks, len(halo_first) * piece_blocks)
    second_view = (row_stride, fill_count, targets.shape[1], 0, len(halo_second) * piece_blocks)
    square, square_rows = square_products(
        table, full_rows, halo_first, depth_count, target_share, first_view
    )
    return block_products(
        table, square_rows, halo_second, target_share, second_view, own=square
    )


def solution(mesh):
    placed = (P(("row", "col"), "depth", None, None), P(), P(("row", "col"), None))
    return jax.shard_map(
        local,
        mesh=mesh,
        in_specs=placed,
        out_specs=P(("row", "col"), "depth", None, None),
        check_vma=False,
    )
```

```python
import functools

import jax
import jax.numpy as jnp
from jax import lax
from jax.experimental import pallas as pl
from jax.experimental.pallas import tpu as pltpu
from jax.sharding import PartitionSpec as P


def shifted(value, axis, steps):
    count = lax.axis_size(axis)
    pairs = [(source, (source + steps) % count) for source in range(count)]
    return lax.ppermute(value, axis, pairs)


def block_table(block_cols, rows, targets, start_row, order_total, fill_count, miss):
    cols_of = block_cols[rows]
    matches = cols_of[:, :, None, :] == targets[:, None, :, None]
    has_match = jnp.any(matches, axis=3)
    slot_ids = jnp.arange(fill_count, dtype=jnp.int32)[None, None, None, :]
    position = jnp.sum(jnp.where(matches, slot_ids, 0), axis=3)
    local_rows = (rows - start_row) % order_total
    flat = local_rows[:, :, None] * fill_count + position
    flat = jnp.clip(flat, 0, miss)
    return jnp.where(has_match, flat, miss).astype(jnp.int32)


def table_pick(idx_ref, view, row, inner, col):
    row_stride, first, inner_stride, shift, cap = view
    entry = idx_ref[row * row_stride + (first + inner) * inner_stride + col]
    return jnp.minimum(jnp.maximum(entry - shift, 0), cap)


def product_kernel(n_out, n_inner, n_pieces, final, view, idx_ref, left_hbm, *rest):
    pieces = rest[:n_pieces]
    rest = rest[n_pieces:]
    if final:
        own_ref, out_ref, halo, lcat, rcat, left_ref, sems = rest
    else:
        out_ref, halo, lcat, rcat, left_ref, sems = rest
    edge = left_ref.shape[-1]
    span = pieces[0].shape[0]
    copies = [pltpu.make_async_copy(left_hbm, left_ref, sems.at[n_pieces])] + [
        pltpu.make_async_copy(piece, halo.at[pl.ds(k * span, span)], sems.at[k])
        for k, piece in enumerate(pieces)
    ]
    for copy in copies:
        copy.start()
    halo[n_pieces * span] = jnp.zeros((edge, edge), halo.dtype)
    for copy in copies:
        copy.wait()

    def row_body(row, carry):
        for inner in range(n_inner):
            lcat[:, inner * edge:(inner + 1) * edge] = left_ref[row, inner]

        for col in range(n_out):
            for inner in range(n_inner):
                pick = table_pick(idx_ref, view, row, inner, col)
                rcat[inner * edge:(inner + 1) * edge, col * edge:(col + 1) * edge] = halo[pick]
        acc = jnp.dot(lcat[...], rcat[...], preferred_element_type=jnp.float32)
        for col in range(n_out):
            part = acc[:, col * edge:(col + 1) * edge]
            if final:
                value = 3.0 * own_ref[row, col].astype(jnp.float32) - 2.0 * part
            else:
                value = part
            out_ref[row, col] = value.astype(out_ref.dtype)
        return carry

    lax.fori_loop(0, left_ref.shape[0], row_body, 0)


def block_products(table, left, pieces, n_out, view, own=None):
    rows, n_inner, edge = left.shape[0], left.shape[1], left.shape[2]
    final = own is not None
    flat_pieces = [piece.reshape(-1, edge, edge) for piece in pieces]
    span = flat_pieces[0].shape[0]
    operands = [table.reshape(-1), left] + flat_pieces + ([own] if final else [])
    vmem = pl.BlockSpec(memory_space=pltpu.VMEM)
    anywhere = pl.BlockSpec(memory_space=pl.ANY)
    in_specs = [pl.BlockSpec(memory_space=pltpu.SMEM), anywhere] + [anywhere] * len(pieces)
    in_specs += [vmem] if final else []
    flops = 2 * rows * n_out * n_inner * edge ** 3
    moved = sum(int(x.size) * x.dtype.itemsize for x in operands) + rows * n_out * edge * edge * 2
    return pl.pallas_call(
        functools.partial(product_kernel, n_out, n_inner, len(pieces), final, view),
        out_shape=jax.ShapeDtypeStruct((rows, n_out, edge, edge), jnp.bfloat16),
        in_specs=in_specs,
        out_specs=vmem,
        scratch_shapes=[
            pltpu.VMEM((len(pieces) * span + 1, edge, edge), left.dtype),
            pltpu.VMEM((edge, n_inner * edge), left.dtype),
            pltpu.VMEM((n_inner * edge, n_out * edge), left.dtype),
            pltpu.VMEM(left.shape, left.dtype),
            pltpu.SemaphoreType.DMA((len(pieces) + 1,)),
        ],
        compiler_params=pltpu.CompilerParams(vmem_limit_bytes=62 * 1024 * 1024),
        cost_estimate=pl.CostEstimate(flops=flops, transcendentals=0, bytes_accessed=moved),
    )(*operands)


MESH = pl.DeviceIdType.MESH


def square_kernel(n_own, n_inner, n_pieces, view, idx_ref, left_ref, *rest):
    pieces = rest[:n_pieces]
    out_ref, spread_ref, halo, lcat, rcat, sems, send_sems, recv_sems, keep_sems = rest[
        n_pieces:
    ]
    edge = left_ref.shape[-1]
    span = pieces[0].shape[0]
    row_count = left_ref.shape[0]
    row_at = lax.axis_index("row")
    col_at = lax.axis_index("col")
    depth_at = lax.axis_index("depth")
    depth_count = lax.axis_size("depth")
    ahead = lax.rem(depth_at + 1, depth_count)
    behind = lax.rem(depth_at + depth_count - 1, depth_count)
    across = lax.rem(depth_at + 2, depth_count)

    barrier = pltpu.get_barrier_semaphore()
    for peer in (ahead, behind):
        pl.semaphore_signal(
            barrier, inc=1, device_id=(row_at, col_at, peer), device_id_type=MESH
        )
    pl.semaphore_wait(barrier, 2)

    copies = [
        pltpu.make_async_copy(piece, halo.at[pl.ds(k * span, span)], sems.at[k])
        for k, piece in enumerate(pieces)
    ]
    for copy in copies:
        copy.start()
    halo[n_pieces * span] = jnp.zeros((edge, edge), halo.dtype)
    for copy in copies:
        copy.wait()

    def spread(row, k):
        source = out_ref.at[row, pl.ds(0, n_own)]
        target = spread_ref.at[row, pl.ds(depth_at * n_own, n_own)]
        if k == 0:
            return pltpu.make_async_copy(source, target, send_sems.at[row, 0])
        return pltpu.make_async_remote_copy(
            src_ref=source,
            dst_ref=target,
            send_sem=send_sems.at[row, k],
            recv_sem=recv_sems.at[row, k],
            device_id=(row_at, col_at, ahead if k == 1 else behind),
            device_id_type=MESH,
        )

    def keep(row):
        return pltpu.make_async_copy(
            out_ref.at[row, pl.ds(n_own, n_own)],
            spread_ref.at[row, pl.ds(across * n_own, n_own)],
            keep_sems.at[row],
        )

    def products(row, first):
        for inner in range(n_inner):
            lcat[:, inner * edge:(inner + 1) * edge] = left_ref[row, inner]

        for part in range(n_own):
            for inner in range(n_inner):
                pick = table_pick(idx_ref, view, row, inner, first + part)
                rcat[inner * edge:(inner + 1) * edge, part * edge:(part + 1) * edge] = halo[pick]
        acc = jnp.dot(lcat[...], rcat[...], preferred_element_type=jnp.float32)
        for part in range(n_own):
            out_ref[row, first + part] = acc[:, part * edge:(part + 1) * edge].astype(out_ref.dtype)

    def own_body(row, carry):
        products(row, 0)
        for k in range(3):
            spread(row, k).start()
        return carry

    def across_body(row, carry):
        products(row, n_own)
        keep(row).start()
        return carry

    lax.fori_loop(0, row_count, own_body, 0)
    lax.fori_loop(0, row_count, across_body, 0)
    for row in range(row_count):
        for k in range(3):
            spread(row, k).wait()
        keep(row).wait()


def square_products(table, left, pieces, depth_count, n_own, view):
    rows, n_inner, edge = left.shape[0], left.shape[1], left.shape[2]
    flat_pieces = [piece.reshape(-1, edge, edge) for piece in pieces]
    span = flat_pieces[0].shape[0]
    operands = [table.reshape(-1), left] + flat_pieces
    vmem = pl.BlockSpec(memory_space=pltpu.VMEM)
    anywhere = pl.BlockSpec(memory_space=pl.ANY)
    in_specs = [pl.BlockSpec(memory_space=pltpu.SMEM), vmem] + [anywhere] * len(pieces)
    flops = 2 * rows * 2 * n_own * n_inner * edge ** 3
    moved = sum(int(x.size) * x.dtype.itemsize for x in operands) + rows * n_own * edge * edge * 10
    return pl.pallas_call(
        functools.partial(square_kernel, n_own, n_inner, len(pieces), view),
        out_shape=(
            jax.ShapeDtypeStruct((rows, 2 * n_own, edge, edge), jnp.bfloat16),
            jax.ShapeDtypeStruct((rows, depth_count * n_own, edge, edge), jnp.bfloat16),
        ),
        in_specs=in_specs,
        out_specs=(vmem, anywhere),
        scratch_shapes=[
            pltpu.VMEM((len(pieces) * span + 1, edge, edge), left.dtype),
            pltpu.VMEM((edge, n_inner * edge), left.dtype),
            pltpu.VMEM((n_inner * edge, n_own * edge), left.dtype),
            pltpu.SemaphoreType.DMA((len(pieces),)),
            pltpu.SemaphoreType.DMA((rows, 3)),
            pltpu.SemaphoreType.DMA((rows, 3)),
            pltpu.SemaphoreType.DMA((rows,)),
        ],
        compiler_params=pltpu.CompilerParams(
            vmem_limit_bytes=62 * 1024 * 1024, collective_id=0, has_side_effects=True
        ),
        cost_estimate=pl.CostEstimate(flops=flops, transcendentals=0, bytes_accessed=moved),
    )(*operands)


def halo_kernel(
    blocks_ref, full_ref, left_ref, right_ref, send_sems, recv_sems, side_send, side_recv,
    relay_sems,
):
    quarter = blocks_ref.shape[1]
    row_at = lax.axis_index("row")
    col_at = lax.axis_index("col")
    depth_at = lax.axis_index("depth")
    col_count = lax.axis_size("col")
    depth_count = lax.axis_size("depth")
    ring = lax.axis_size("row") * col_count
    place = row_at * col_count + col_at
    after = lax.rem(place + 1, ring)
    before = lax.rem(place + ring - 1, ring)
    after_id = (after // col_count, after % col_count, depth_at)
    before_id = (before // col_count, before % col_count, depth_at)
    peer_ids = [
        (row_at, col_at, lax.rem(depth_at + k, depth_count)) for k in range(1, depth_count)
    ]

    barrier = pltpu.get_barrier_semaphore()
    for device in peer_ids + [after_id, before_id]:
        pl.semaphore_signal(barrier, inc=1, device_id=device, device_id_type=MESH)
    pl.semaphore_wait(barrier, depth_count + 1)

    own = pl.ds(depth_at * quarter, quarter)
    rows = blocks_ref.shape[0]
    local = pltpu.make_async_copy(blocks_ref, full_ref.at[:, own], side_send.at[2, 0, 0])
    local.start()

    def to_peer(k, row):
        return pltpu.make_async_remote_copy(
            src_ref=blocks_ref.at[row],
            dst_ref=full_ref.at[row, own],
            send_sem=send_sems.at[k, row],
            recv_sem=recv_sems.at[k, row],
            device_id=peer_ids[k - 1],
            device_id_type=MESH,
        )

    def to_side(k, row, way):
        origin = lax.rem(depth_at + depth_count - k, depth_count)
        slot = pl.ds(origin * quarter, quarter)
        source = blocks_ref.at[row] if k == 0 else full_ref.at[row, slot]
        return pltpu.make_async_remote_copy(
            src_ref=source,
            dst_ref=(left_ref if way == 0 else right_ref).at[row, slot],
            send_sem=side_send.at[way, k, row],
            recv_sem=side_recv.at[way, k, row],
            device_id=after_id if way == 0 else before_id,
            device_id_type=MESH,
        )

    def slot_of(k):
        return pl.ds(lax.rem(depth_at + depth_count - k, depth_count) * quarter, quarter)

    def relay(row):
        k, target = (1, peer_ids[0]) if row < rows // 2 else (3, peer_ids[2])
        return pltpu.make_async_remote_copy(
            src_ref=full_ref.at[row, slot_of(k)],
            dst_ref=full_ref.at[row, slot_of(k)],
            send_sem=relay_sems.at[0, row],
            recv_sem=relay_sems.at[1, row],
            device_id=target,
            device_id_type=MESH,
        )

    order = {1: list(range(rows)), 3: list(range(rows - 1, -1, -1))}
    for step in range(rows):
        for k in (1, 3):
            to_peer(k, order[k][step]).start()
    for row in range(rows):
        for way in range(2):
            to_side(0, row, way).start()
    for step in range(rows):
        for k in (1, 3):
            row = order[k][step]
            to_peer(k, row).wait_recv()
            if (k == 1) == (row < rows // 2):
                relay(row).start()
            for way in range(2):
                to_side(k, row, way).start()
    for step in range(rows // 2):
        for row in (step, rows - 1 - step):
            relay(row).wait_recv()
            for way in range(2):
                to_side(2, row, way).start()
    local.wait()
    for row in range(rows):
        for k in (1, 3):
            to_peer(k, row).wait_send()
        relay(row).wait_send()
    for k in range(depth_count):
        for row in range(rows):
            for way in range(2):
                to_side(k, row, way).wait()


def halo_exchange(blocks, depth_count):
    rows, quarter, edge = blocks.shape[0], blocks.shape[1], blocks.shape[2]
    whole = jax.ShapeDtypeStruct((rows, depth_count * quarter, edge, edge), blocks.dtype)
    anywhere = pl.BlockSpec(memory_space=pl.ANY)
    moved = int(blocks.size) * blocks.dtype.itemsize * (3 * depth_count + 3)
    return pl.pallas_call(
        halo_kernel,
        out_shape=(whole, whole, whole),
        in_specs=[anywhere],
        out_specs=(anywhere, anywhere, anywhere),
        scratch_shapes=[
            pltpu.SemaphoreType.DMA((depth_count, rows)),
            pltpu.SemaphoreType.DMA((depth_count, rows)),
            pltpu.SemaphoreType.DMA((3, depth_count, rows)),
            pltpu.SemaphoreType.DMA((2, depth_count, rows)),
            pltpu.SemaphoreType.DMA((2, rows)),
        ],
        compiler_params=pltpu.CompilerParams(collective_id=1, has_side_effects=True),
        cost_estimate=pl.CostEstimate(flops=0, transcendentals=0, bytes_accessed=moved),
    )(blocks)


def local(blocks, block_cols, product_cols):
    row_count = blocks.shape[0]
    block_edge = blocks.shape[2]
    fill_count = block_cols.shape[1]
    order_total = row_count * lax.axis_size(("row", "col"))
    row_place = lax.axis_index(("row", "col"))
    depth_index = lax.axis_index("depth")
    depth_count = lax.axis_size("depth")
    target_share = product_cols.shape[1] // depth_count

    full_rows, from_before, from_after = halo_exchange(blocks, depth_count)
    near = {0: full_rows, 1: from_before, -1: from_after}
    near[2] = shifted(near[1], ("row", "col"), 1)
    near[-2] = shifted(near[-1], ("row", "col"), -1)

    def halo_of(reach):
        return [near[offset] for offset in range(reach, -reach - 1, -1)]

    own_cols = lax.dynamic_slice_in_dim(block_cols, row_place * row_count, row_count, 0)
    own_targets = lax.dynamic_slice_in_dim(
        product_cols, depth_index * target_share, target_share, 1
    )

    across_targets = lax.dynamic_slice_in_dim(
        product_cols, ((depth_index + 2) % depth_count) * target_share, target_share, 1
    )
    halo_first = halo_of(1)
    halo_second = halo_of(2)
    piece_blocks = row_count * fill_count
    inner_rows = jnp.concatenate([own_cols, product_cols], axis=1)
    targets = jnp.concatenate([own_targets, across_targets], axis=1)
    table = block_table(
        block_cols, inner_rows, targets, (row_place - 2) * row_count, order_total,
        fill_count, len(halo_second) * piece_blocks,
    )
    row_stride = inner_rows.shape[1] * targets.shape[1]
    first_view = (row_stride, 0, targets.shape[1], piece_blocks, len(halo_first) * piece_blocks)
    second_view = (row_stride, fill_count, targets.shape[1], 0, len(halo_second) * piece_blocks)
    square, square_rows = square_products(
        table, full_rows, halo_first, depth_count, target_share, first_view
    )
    return block_products(
        table, square_rows, halo_second, target_share, second_view, own=square
    )


def solution(mesh):
    placed = (P(("row", "col"), "depth", None, None), P(), P(("row", "col"), None))
    return jax.shard_map(
        local,
        mesh=mesh,
        in_specs=placed,
        out_specs=P(("row", "col"), "depth", None, None),
        check_vma=False,
    )
```

```python
import functools

import jax
import jax.numpy as jnp
from jax import lax
from jax.experimental import pallas as pl
from jax.experimental.pallas import tpu as pltpu
from jax.sharding import PartitionSpec as P


def shifted(value, axis, steps):
    count = lax.axis_size(axis)
    pairs = [(source, (source + steps) % count) for source in range(count)]
    return lax.ppermute(value, axis, pairs)


def block_table(block_cols, rows, targets, start_row, order_total, fill_count, miss):
    cols_of = block_cols[rows]
    matches = cols_of[:, :, None, :] == targets[:, None, :, None]
    has_match = jnp.any(matches, axis=3)
    slot_ids = jnp.arange(fill_count, dtype=jnp.int32)[None, None, None, :]
    position = jnp.sum(jnp.where(matches, slot_ids, 0), axis=3)
    local_rows = (rows - start_row) % order_total
    flat = local_rows[:, :, None] * fill_count + position
    flat = jnp.clip(flat, 0, miss)
    return jnp.where(has_match, flat, miss).astype(jnp.int32)


def table_pick(idx_ref, view, row, inner, col):
    row_stride, first, inner_stride, shift, cap = view
    entry = idx_ref[row * row_stride + (first + inner) * inner_stride + col]
    return jnp.minimum(jnp.maximum(entry - shift, 0), cap)


def product_kernel(n_out, n_inner, n_pieces, final, view, idx_ref, left_hbm, *rest):
    pieces = rest[:n_pieces]
    rest = rest[n_pieces:]
    if final:
        own_ref, out_ref, halo, lcat, rcat, left_ref, sems = rest
    else:
        out_ref, halo, lcat, rcat, left_ref, sems = rest
    edge = left_ref.shape[-1]
    span = pieces[0].shape[0]
    copies = [pltpu.make_async_copy(left_hbm, left_ref, sems.at[n_pieces])] + [
        pltpu.make_async_copy(piece, halo.at[pl.ds(k * span, span)], sems.at[k])
        for k, piece in enumerate(pieces)
    ]
    for copy in copies:
        copy.start()
    halo[n_pieces * span] = jnp.zeros((edge, edge), halo.dtype)
    for copy in copies:
        copy.wait()

    def row_body(row, carry):
        for inner in range(n_inner):
            lcat[:, inner * edge:(inner + 1) * edge] = left_ref[row, inner]

        for col in range(n_out):
            for inner in range(n_inner):
                pick = table_pick(idx_ref, view, row, inner, col)
                rcat[inner * edge:(inner + 1) * edge, col * edge:(col + 1) * edge] = halo[pick]
        acc = jnp.dot(lcat[...], rcat[...], preferred_element_type=jnp.float32)
        for col in range(n_out):
            part = acc[:, col * edge:(col + 1) * edge]
            if final:
                value = 3.0 * own_ref[row, col].astype(jnp.float32) - 2.0 * part
            else:
                value = part
            out_ref[row, col] = value.astype(out_ref.dtype)
        return carry

    lax.fori_loop(0, left_ref.shape[0], row_body, 0)


def block_products(table, left, pieces, n_out, view, own=None):
    rows, n_inner, edge = left.shape[0], left.shape[1], left.shape[2]
    final = own is not None
    flat_pieces = [piece.reshape(-1, edge, edge) for piece in pieces]
    span = flat_pieces[0].shape[0]
    operands = [table.reshape(-1), left] + flat_pieces + ([own] if final else [])
    vmem = pl.BlockSpec(memory_space=pltpu.VMEM)
    anywhere = pl.BlockSpec(memory_space=pl.ANY)
    in_specs = [pl.BlockSpec(memory_space=pltpu.SMEM), anywhere] + [anywhere] * len(pieces)
    in_specs += [vmem] if final else []
    flops = 2 * rows * n_out * n_inner * edge ** 3
    moved = sum(int(x.size) * x.dtype.itemsize for x in operands) + rows * n_out * edge * edge * 2
    return pl.pallas_call(
        functools.partial(product_kernel, n_out, n_inner, len(pieces), final, view),
        out_shape=jax.ShapeDtypeStruct((rows, n_out, edge, edge), jnp.bfloat16),
        in_specs=in_specs,
        out_specs=vmem,
        scratch_shapes=[
            pltpu.VMEM((len(pieces) * span + 1, edge, edge), left.dtype),
            pltpu.VMEM((edge, n_inner * edge), left.dtype),
            pltpu.VMEM((n_inner * edge, n_out * edge), left.dtype),
            pltpu.VMEM(left.shape, left.dtype),
            pltpu.SemaphoreType.DMA((len(pieces) + 1,)),
        ],
        compiler_params=pltpu.CompilerParams(vmem_limit_bytes=62 * 1024 * 1024),
        cost_estimate=pl.CostEstimate(flops=flops, transcendentals=0, bytes_accessed=moved),
    )(*operands)


MESH = pl.DeviceIdType.MESH


def square_kernel(n_own, n_inner, n_pieces, view, idx_ref, left_ref, *rest):
    pieces = rest[:n_pieces]
    out_ref, spread_ref, halo, lcat, rcat, sems, send_sems, recv_sems, keep_sems = rest[
        n_pieces:
    ]
    edge = left_ref.shape[-1]
    span = pieces[0].shape[0]
    row_count = left_ref.shape[0]
    row_at = lax.axis_index("row")
    col_at = lax.axis_index("col")
    depth_at = lax.axis_index("depth")
    depth_count = lax.axis_size("depth")
    ahead = lax.rem(depth_at + 1, depth_count)
    behind = lax.rem(depth_at + depth_count - 1, depth_count)
    across = lax.rem(depth_at + 2, depth_count)

    barrier = pltpu.get_barrier_semaphore()
    for peer in (ahead, behind):
        pl.semaphore_signal(
            barrier, inc=1, device_id=(row_at, col_at, peer), device_id_type=MESH
        )
    pl.semaphore_wait(barrier, 2)

    copies = [
        pltpu.make_async_copy(piece, halo.at[pl.ds(k * span, span)], sems.at[k])
        for k, piece in enumerate(pieces)
    ]
    for copy in copies:
        copy.start()
    halo[n_pieces * span] = jnp.zeros((edge, edge), halo.dtype)
    for copy in copies:
        copy.wait()

    def spread(row, k):
        width = n_own if k == 0 else n_own - 1
        source = out_ref.at[row, pl.ds(0, width)]
        target = spread_ref.at[row, pl.ds(depth_at * n_own, width)]
        if k == 0:
            return pltpu.make_async_copy(source, target, send_sems.at[row, 0])
        return pltpu.make_async_remote_copy(
            src_ref=source,
            dst_ref=target,
            send_sem=send_sems.at[row, k],
            recv_sem=recv_sems.at[row, k],
            device_id=(row_at, col_at, ahead if k == 1 else behind),
            device_id_type=MESH,
        )

    def keep(row, j):
        last = n_own - 1
        start, width, slot = [
            (n_own, n_own, across * n_own),
            (2 * n_own, 1, ahead * n_own + last),
            (2 * n_own + 1, 1, behind * n_own + last),
        ][j]
        return pltpu.make_async_copy(
            out_ref.at[row, pl.ds(start, width)],
            spread_ref.at[row, pl.ds(slot, width)],
            keep_sems.at[row, j],
        )

    def products(row, first, count):
        for inner in range(n_inner):
            lcat[:, inner * edge:(inner + 1) * edge] = left_ref[row, inner]

        for part in range(count):
            for inner in range(n_inner):
                pick = table_pick(idx_ref, view, row, inner, first + part)
                rcat[inner * edge:(inner + 1) * edge, part * edge:(part + 1) * edge] = halo[pick]
        acc = jnp.dot(
            lcat[...], rcat[:, : count * edge], preferred_element_type=jnp.float32
        )
        for part in range(count):
            out_ref[row, first + part] = acc[:, part * edge:(part + 1) * edge].astype(out_ref.dtype)

    def own_body(row, carry):
        products(row, 0, n_own)
        for k in range(3):
            spread(row, k).start()
        return carry

    def across_body(row, carry):
        products(row, n_own, n_own + 2)
        for j in range(3):
            keep(row, j).start()
        return carry

    lax.fori_loop(0, row_count, own_body, 0)
    lax.fori_loop(0, row_count, across_body, 0)
    for row in range(row_count):
        for k in range(3):
            spread(row, k).wait()
        for j in range(3):
            keep(row, j).wait()


def square_products(table, left, pieces, depth_count, n_own, view):
    rows, n_inner, edge = left.shape[0], left.shape[1], left.shape[2]
    flat_pieces = [piece.reshape(-1, edge, edge) for piece in pieces]
    span = flat_pieces[0].shape[0]
    operands = [table.reshape(-1), left] + flat_pieces
    vmem = pl.BlockSpec(memory_space=pltpu.VMEM)
    anywhere = pl.BlockSpec(memory_space=pl.ANY)
    in_specs = [pl.BlockSpec(memory_space=pltpu.SMEM), vmem] + [anywhere] * len(pieces)
    flops = 2 * rows * (2 * n_own + 2) * n_inner * edge ** 3
    moved = sum(int(x.size) * x.dtype.itemsize for x in operands) + rows * n_own * edge * edge * 10
    return pl.pallas_call(
        functools.partial(square_kernel, n_own, n_inner, len(pieces), view),
        out_shape=(
            jax.ShapeDtypeStruct((rows, 2 * n_own + 2, edge, edge), jnp.bfloat16),
            jax.ShapeDtypeStruct((rows, depth_count * n_own, edge, edge), jnp.bfloat16),
        ),
        in_specs=in_specs,
        out_specs=(vmem, anywhere),
        scratch_shapes=[
            pltpu.VMEM((len(pieces) * span + 1, edge, edge), left.dtype),
            pltpu.VMEM((edge, n_inner * edge), left.dtype),
            pltpu.VMEM((n_inner * edge, (n_own + 2) * edge), left.dtype),
            pltpu.SemaphoreType.DMA((len(pieces),)),
            pltpu.SemaphoreType.DMA((rows, 3)),
            pltpu.SemaphoreType.DMA((rows, 3)),
            pltpu.SemaphoreType.DMA((rows, 3)),
        ],
        compiler_params=pltpu.CompilerParams(
            vmem_limit_bytes=62 * 1024 * 1024, collective_id=0, has_side_effects=True
        ),
        cost_estimate=pl.CostEstimate(flops=flops, transcendentals=0, bytes_accessed=moved),
    )(*operands)


def halo_kernel(
    blocks_ref, full_ref, left_ref, right_ref, send_sems, recv_sems, side_send, side_recv,
    relay_sems,
):
    quarter = blocks_ref.shape[1]
    row_at = lax.axis_index("row")
    col_at = lax.axis_index("col")
    depth_at = lax.axis_index("depth")
    col_count = lax.axis_size("col")
    depth_count = lax.axis_size("depth")
    ring = lax.axis_size("row") * col_count
    place = row_at * col_count + col_at
    after = lax.rem(place + 1, ring)
    before = lax.rem(place + ring - 1, ring)
    after_id = (after // col_count, after % col_count, depth_at)
    before_id = (before // col_count, before % col_count, depth_at)
    peer_ids = [
        (row_at, col_at, lax.rem(depth_at + k, depth_count)) for k in range(1, depth_count)
    ]

    barrier = pltpu.get_barrier_semaphore()
    for device in peer_ids + [after_id, before_id]:
        pl.semaphore_signal(barrier, inc=1, device_id=device, device_id_type=MESH)
    pl.semaphore_wait(barrier, depth_count + 1)

    own = pl.ds(depth_at * quarter, quarter)
    rows = blocks_ref.shape[0]
    local = pltpu.make_async_copy(blocks_ref, full_ref.at[:, own], side_send.at[2, 0, 0])
    local.start()

    def to_peer(k, row):
        return pltpu.make_async_remote_copy(
            src_ref=blocks_ref.at[row],
            dst_ref=full_ref.at[row, own],
            send_sem=send_sems.at[k, row],
            recv_sem=recv_sems.at[k, row],
            device_id=peer_ids[k - 1],
            device_id_type=MESH,
        )

    def to_side(k, row, way):
        origin = lax.rem(depth_at + depth_count - k, depth_count)
        slot = pl.ds(origin * quarter, quarter)
        source = blocks_ref.at[row] if k == 0 else full_ref.at[row, slot]
        return pltpu.make_async_remote_copy(
            src_ref=source,
            dst_ref=(left_ref if way == 0 else right_ref).at[row, slot],
            send_sem=side_send.at[way, k, row],
            recv_sem=side_recv.at[way, k, row],
            device_id=after_id if way == 0 else before_id,
            device_id_type=MESH,
        )

    def slot_of(k):
        return pl.ds(lax.rem(depth_at + depth_count - k, depth_count) * quarter, quarter)

    def relay(row):
        k, target = (1, peer_ids[0]) if row < rows // 2 else (3, peer_ids[2])
        return pltpu.make_async_remote_copy(
            src_ref=full_ref.at[row, slot_of(k)],
            dst_ref=full_ref.at[row, slot_of(k)],
            send_sem=relay_sems.at[0, row],
            recv_sem=relay_sems.at[1, row],
            device_id=target,
            device_id_type=MESH,
        )

    order = {1: list(range(rows)), 3: list(range(rows - 1, -1, -1))}
    for step in range(rows):
        for k in (1, 3):
            to_peer(k, order[k][step]).start()
    for row in range(rows):
        for way in range(2):
            to_side(0, row, way).start()
    for step in range(rows):
        for k in (1, 3):
            row = order[k][step]
            to_peer(k, row).wait_recv()
            if (k == 1) == (row < rows // 2):
                relay(row).start()
            for way in range(2):
                to_side(k, row, way).start()
    for step in range(rows // 2):
        for row in (step, rows - 1 - step):
            relay(row).wait_recv()
            for way in range(2):
                to_side(2, row, way).start()
    local.wait()
    for row in range(rows):
        for k in (1, 3):
            to_peer(k, row).wait_send()
        relay(row).wait_send()
    for k in range(depth_count):
        for row in range(rows):
            for way in range(2):
                to_side(k, row, way).wait()


def halo_exchange(blocks, depth_count):
    rows, quarter, edge = blocks.shape[0], blocks.shape[1], blocks.shape[2]
    whole = jax.ShapeDtypeStruct((rows, depth_count * quarter, edge, edge), blocks.dtype)
    anywhere = pl.BlockSpec(memory_space=pl.ANY)
    moved = int(blocks.size) * blocks.dtype.itemsize * (3 * depth_count + 3)
    return pl.pallas_call(
        halo_kernel,
        out_shape=(whole, whole, whole),
        in_specs=[anywhere],
        out_specs=(anywhere, anywhere, anywhere),
        scratch_shapes=[
            pltpu.SemaphoreType.DMA((depth_count, rows)),
            pltpu.SemaphoreType.DMA((depth_count, rows)),
            pltpu.SemaphoreType.DMA((3, depth_count, rows)),
            pltpu.SemaphoreType.DMA((2, depth_count, rows)),
            pltpu.SemaphoreType.DMA((2, rows)),
        ],
        compiler_params=pltpu.CompilerParams(collective_id=1, has_side_effects=True),
        cost_estimate=pl.CostEstimate(flops=0, transcendentals=0, bytes_accessed=moved),
    )(blocks)


def local(blocks, block_cols, product_cols):
    row_count = blocks.shape[0]
    block_edge = blocks.shape[2]
    fill_count = block_cols.shape[1]
    order_total = row_count * lax.axis_size(("row", "col"))
    row_place = lax.axis_index(("row", "col"))
    depth_index = lax.axis_index("depth")
    depth_count = lax.axis_size("depth")
    target_share = product_cols.shape[1] // depth_count

    full_rows, from_before, from_after = halo_exchange(blocks, depth_count)
    near = {0: full_rows, 1: from_before, -1: from_after}
    near[2] = shifted(near[1], ("row", "col"), 1)
    near[-2] = shifted(near[-1], ("row", "col"), -1)

    def halo_of(reach):
        return [near[offset] for offset in range(reach, -reach - 1, -1)]

    own_cols = lax.dynamic_slice_in_dim(block_cols, row_place * row_count, row_count, 0)
    own_targets = lax.dynamic_slice_in_dim(
        product_cols, depth_index * target_share, target_share, 1
    )

    across_targets = lax.dynamic_slice_in_dim(
        product_cols, ((depth_index + 2) % depth_count) * target_share, target_share, 1
    )
    halo_first = halo_of(1)
    halo_second = halo_of(2)
    piece_blocks = row_count * fill_count
    inner_rows = jnp.concatenate([own_cols, product_cols], axis=1)
    ahead_last = lax.dynamic_slice_in_dim(
        product_cols, ((depth_index + 1) % depth_count) * target_share + target_share - 1, 1, 1
    )
    behind_last = lax.dynamic_slice_in_dim(
        product_cols,
        ((depth_index + depth_count - 1) % depth_count) * target_share + target_share - 1, 1, 1,
    )
    targets = jnp.concatenate([own_targets, across_targets, ahead_last, behind_last], axis=1)
    table = block_table(
        block_cols, inner_rows, targets, (row_place - 2) * row_count, order_total,
        fill_count, len(halo_second) * piece_blocks,
    )
    row_stride = inner_rows.shape[1] * targets.shape[1]
    first_view = (row_stride, 0, targets.shape[1], piece_blocks, len(halo_first) * piece_blocks)
    second_view = (row_stride, fill_count, targets.shape[1], 0, len(halo_second) * piece_blocks)
    square, square_rows = square_products(
        table, full_rows, halo_first, depth_count, target_share, first_view
    )
    return block_products(
        table, square_rows, halo_second, target_share, second_view, own=square
    )


def solution(mesh):
    placed = (P(("row", "col"), "depth", None, None), P(), P(("row", "col"), None))
    return jax.shard_map(
        local,
        mesh=mesh,
        in_specs=placed,
        out_specs=P(("row", "col"), "depth", None, None),
        check_vma=False,
    )
```

```python
import functools

import jax
import jax.numpy as jnp
from jax import lax
from jax.experimental import pallas as pl
from jax.experimental.pallas import tpu as pltpu
from jax.sharding import PartitionSpec as P


def shifted(value, axis, steps):
    count = lax.axis_size(axis)
    pairs = [(source, (source + steps) % count) for source in range(count)]
    return lax.ppermute(value, axis, pairs)


def block_table(block_cols, rows, targets, start_row, order_total, fill_count, miss):
    cols_of = block_cols[rows]
    matches = cols_of[:, :, None, :] == targets[:, None, :, None]
    has_match = jnp.any(matches, axis=3)
    slot_ids = jnp.arange(fill_count, dtype=jnp.int32)[None, None, None, :]
    position = jnp.sum(jnp.where(matches, slot_ids, 0), axis=3)
    local_rows = (rows - start_row) % order_total
    flat = local_rows[:, :, None] * fill_count + position
    flat = jnp.clip(flat, 0, miss)
    return jnp.where(has_match, flat, miss).astype(jnp.int32)


def table_pick(idx_ref, view, row, inner, col):
    row_stride, first, inner_stride, shift, cap = view
    entry = idx_ref[row * row_stride + (first + inner) * inner_stride + col]
    return jnp.minimum(jnp.maximum(entry - shift, 0), cap)


def product_kernel(n_out, n_inner, n_pieces, final, view, idx_ref, left_hbm, *rest):
    pieces = rest[:n_pieces]
    rest = rest[n_pieces:]
    if final:
        own_ref, out_ref, halo, lcat, rcat, left_ref, sems = rest
    else:
        out_ref, halo, lcat, rcat, left_ref, sems = rest
    edge = left_ref.shape[-1]
    span = pieces[0].shape[0]
    copies = [pltpu.make_async_copy(left_hbm, left_ref, sems.at[n_pieces])] + [
        pltpu.make_async_copy(piece, halo.at[pl.ds(k * span, span)], sems.at[k])
        for k, piece in enumerate(pieces)
    ]
    for copy in copies:
        copy.start()
    halo[n_pieces * span] = jnp.zeros((edge, edge), halo.dtype)
    for copy in copies:
        copy.wait()

    for row in range(left_ref.shape[0]):
        lbuf, rbuf = lcat.at[row % 2], rcat.at[row % 2]
        for inner in range(n_inner):
            lbuf[:, inner * edge:(inner + 1) * edge] = left_ref[row, inner]

        for col in range(n_out):
            for inner in range(n_inner):
                pick = table_pick(idx_ref, view, row, inner, col)
                rbuf[inner * edge:(inner + 1) * edge, col * edge:(col + 1) * edge] = halo[pick]
        acc = jnp.dot(lbuf[...], rbuf[...], preferred_element_type=jnp.float32)
        for col in range(n_out):
            part = acc[:, col * edge:(col + 1) * edge]
            if final:
                value = 3.0 * own_ref[row, col].astype(jnp.float32) - 2.0 * part
            else:
                value = part
            out_ref[row, col] = value.astype(out_ref.dtype)


def block_products(table, left, pieces, n_out, view, own=None):
    rows, n_inner, edge = left.shape[0], left.shape[1], left.shape[2]
    final = own is not None
    flat_pieces = [piece.reshape(-1, edge, edge) for piece in pieces]
    span = flat_pieces[0].shape[0]
    operands = [table.reshape(-1), left] + flat_pieces + ([own] if final else [])
    vmem = pl.BlockSpec(memory_space=pltpu.VMEM)
    anywhere = pl.BlockSpec(memory_space=pl.ANY)
    in_specs = [pl.BlockSpec(memory_space=pltpu.SMEM), anywhere] + [anywhere] * len(pieces)
    in_specs += [vmem] if final else []
    flops = 2 * rows * n_out * n_inner * edge ** 3
    moved = sum(int(x.size) * x.dtype.itemsize for x in operands) + rows * n_out * edge * edge * 2
    return pl.pallas_call(
        functools.partial(product_kernel, n_out, n_inner, len(pieces), final, view),
        out_shape=jax.ShapeDtypeStruct((rows, n_out, edge, edge), jnp.bfloat16),
        in_specs=in_specs,
        out_specs=vmem,
        scratch_shapes=[
            pltpu.VMEM((len(pieces) * span + 1, edge, edge), left.dtype),
            pltpu.VMEM((2, edge, n_inner * edge), left.dtype),
            pltpu.VMEM((2, n_inner * edge, n_out * edge), left.dtype),
            pltpu.VMEM(left.shape, left.dtype),
            pltpu.SemaphoreType.DMA((len(pieces) + 1,)),
        ],
        compiler_params=pltpu.CompilerParams(vmem_limit_bytes=62 * 1024 * 1024),
        cost_estimate=pl.CostEstimate(flops=flops, transcendentals=0, bytes_accessed=moved),
    )(*operands)


MESH = pl.DeviceIdType.MESH


def square_kernel(n_own, n_inner, n_pieces, view, idx_ref, left_ref, *rest):
    pieces = rest[:n_pieces]
    out_ref, spread_ref, halo, lcat, rcat, sems, send_sems, recv_sems, keep_sems = rest[
        n_pieces:
    ]
    edge = left_ref.shape[-1]
    span = pieces[0].shape[0]
    row_count = left_ref.shape[0]
    row_at = lax.axis_index("row")
    col_at = lax.axis_index("col")
    depth_at = lax.axis_index("depth")
    depth_count = lax.axis_size("depth")
    ahead = lax.rem(depth_at + 1, depth_count)
    behind = lax.rem(depth_at + depth_count - 1, depth_count)
    across = lax.rem(depth_at + 2, depth_count)

    barrier = pltpu.get_barrier_semaphore()
    for peer in (ahead, behind):
        pl.semaphore_signal(
            barrier, inc=1, device_id=(row_at, col_at, peer), device_id_type=MESH
        )
    pl.semaphore_wait(barrier, 2)

    copies = [
        pltpu.make_async_copy(piece, halo.at[pl.ds(k * span, span)], sems.at[k])
        for k, piece in enumerate(pieces)
    ]
    for copy in copies:
        copy.start()
    halo[n_pieces * span] = jnp.zeros((edge, edge), halo.dtype)
    for copy in copies:
        copy.wait()

    def spread(row, k):
        width = n_own if k == 0 else n_own - 1
        source = out_ref.at[row, pl.ds(0, width)]
        target = spread_ref.at[row, pl.ds(depth_at * n_own, width)]
        if k == 0:
            return pltpu.make_async_copy(source, target, send_sems.at[row, 0])
        return pltpu.make_async_remote_copy(
            src_ref=source,
            dst_ref=target,
            send_sem=send_sems.at[row, k],
            recv_sem=recv_sems.at[row, k],
            device_id=(row_at, col_at, ahead if k == 1 else behind),
            device_id_type=MESH,
        )

    def keep(row, j):
        last = n_own - 1
        start, width, slot = [
            (n_own, n_own, across * n_own),
            (2 * n_own, 1, ahead * n_own + last),
            (2 * n_own + 1, 1, behind * n_own + last),
        ][j]
        return pltpu.make_async_copy(
            out_ref.at[row, pl.ds(start, width)],
            spread_ref.at[row, pl.ds(slot, width)],
            keep_sems.at[row, j],
        )

    def products(row, first, count):
        for inner in range(n_inner):
            lcat[:, inner * edge:(inner + 1) * edge] = left_ref[row, inner]

        for part in range(count):
            for inner in range(n_inner):
                pick = table_pick(idx_ref, view, row, inner, first + part)
                rcat[inner * edge:(inner + 1) * edge, part * edge:(part + 1) * edge] = halo[pick]
        acc = jnp.dot(
            lcat[...], rcat[:, : count * edge], preferred_element_type=jnp.float32
        )
        for part in range(count):
            out_ref[row, first + part] = acc[:, part * edge:(part + 1) * edge].astype(out_ref.dtype)

    def own_body(row, carry):
        products(row, 0, n_own)
        for k in range(3):
            spread(row, k).start()
        return carry

    def across_body(row, carry):
        products(row, n_own, n_own + 2)
        for j in range(3):
            keep(row, j).start()
        return carry

    lax.fori_loop(0, row_count, own_body, 0)
    lax.fori_loop(0, row_count, across_body, 0)
    for row in range(row_count):
        for k in range(3):
            spread(row, k).wait()
        for j in range(3):
            keep(row, j).wait()


def square_products(table, left, pieces, depth_count, n_own, view):
    rows, n_inner, edge = left.shape[0], left.shape[1], left.shape[2]
    flat_pieces = [piece.reshape(-1, edge, edge) for piece in pieces]
    span = flat_pieces[0].shape[0]
    operands = [table.reshape(-1), left] + flat_pieces
    vmem = pl.BlockSpec(memory_space=pltpu.VMEM)
    anywhere = pl.BlockSpec(memory_space=pl.ANY)
    in_specs = [pl.BlockSpec(memory_space=pltpu.SMEM), vmem] + [anywhere] * len(pieces)
    flops = 2 * rows * (2 * n_own + 2) * n_inner * edge ** 3
    moved = sum(int(x.size) * x.dtype.itemsize for x in operands) + rows * n_own * edge * edge * 10
    return pl.pallas_call(
        functools.partial(square_kernel, n_own, n_inner, len(pieces), view),
        out_shape=(
            jax.ShapeDtypeStruct((rows, 2 * n_own + 2, edge, edge), jnp.bfloat16),
            jax.ShapeDtypeStruct((rows, depth_count * n_own, edge, edge), jnp.bfloat16),
        ),
        in_specs=in_specs,
        out_specs=(vmem, anywhere),
        scratch_shapes=[
            pltpu.VMEM((len(pieces) * span + 1, edge, edge), left.dtype),
            pltpu.VMEM((edge, n_inner * edge), left.dtype),
            pltpu.VMEM((n_inner * edge, (n_own + 2) * edge), left.dtype),
            pltpu.SemaphoreType.DMA((len(pieces),)),
            pltpu.SemaphoreType.DMA((rows, 3)),
            pltpu.SemaphoreType.DMA((rows, 3)),
            pltpu.SemaphoreType.DMA((rows, 3)),
        ],
        compiler_params=pltpu.CompilerParams(
            vmem_limit_bytes=62 * 1024 * 1024, collective_id=0, has_side_effects=True
        ),
        cost_estimate=pl.CostEstimate(flops=flops, transcendentals=0, bytes_accessed=moved),
    )(*operands)


def halo_kernel(
    blocks_ref, full_ref, left_ref, right_ref, send_sems, recv_sems, side_send, side_recv,
    relay_sems,
):
    quarter = blocks_ref.shape[1]
    row_at = lax.axis_index("row")
    col_at = lax.axis_index("col")
    depth_at = lax.axis_index("depth")
    col_count = lax.axis_size("col")
    depth_count = lax.axis_size("depth")
    ring = lax.axis_size("row") * col_count
    place = row_at * col_count + col_at
    after = lax.rem(place + 1, ring)
    before = lax.rem(place + ring - 1, ring)
    after_id = (after // col_count, after % col_count, depth_at)
    before_id = (before // col_count, before % col_count, depth_at)
    peer_ids = [
        (row_at, col_at, lax.rem(depth_at + k, depth_count)) for k in range(1, depth_count)
    ]

    barrier = pltpu.get_barrier_semaphore()
    for device in peer_ids + [after_id, before_id]:
        pl.semaphore_signal(barrier, inc=1, device_id=device, device_id_type=MESH)
    pl.semaphore_wait(barrier, depth_count + 1)

    own = pl.ds(depth_at * quarter, quarter)
    rows = blocks_ref.shape[0]
    local = pltpu.make_async_copy(blocks_ref, full_ref.at[:, own], side_send.at[2, 0, 0])
    local.start()

    def to_peer(k, row):
        return pltpu.make_async_remote_copy(
            src_ref=blocks_ref.at[row],
            dst_ref=full_ref.at[row, own],
            send_sem=send_sems.at[k, row],
            recv_sem=recv_sems.at[k, row],
            device_id=peer_ids[k - 1],
            device_id_type=MESH,
        )

    def to_side(k, row, way):
        origin = lax.rem(depth_at + depth_count - k, depth_count)
        slot = pl.ds(origin * quarter, quarter)
        source = blocks_ref.at[row] if k == 0 else full_ref.at[row, slot]
        return pltpu.make_async_remote_copy(
            src_ref=source,
            dst_ref=(left_ref if way == 0 else right_ref).at[row, slot],
            send_sem=side_send.at[way, k, row],
            recv_sem=side_recv.at[way, k, row],
            device_id=after_id if way == 0 else before_id,
            device_id_type=MESH,
        )

    def slot_of(k):
        return pl.ds(lax.rem(depth_at + depth_count - k, depth_count) * quarter, quarter)

    def relay(row):
        k, target = (1, peer_ids[0]) if row < rows // 2 else (3, peer_ids[2])
        return pltpu.make_async_remote_copy(
            src_ref=full_ref.at[row, slot_of(k)],
            dst_ref=full_ref.at[row, slot_of(k)],
            send_sem=relay_sems.at[0, row],
            recv_sem=relay_sems.at[1, row],
            device_id=target,
            device_id_type=MESH,
        )

    order = {1: list(range(rows)), 3: list(range(rows - 1, -1, -1))}
    for step in range(rows):
        for k in (1, 3):
            to_peer(k, order[k][step]).start()
    for row in range(rows):
        for way in range(2):
            to_side(0, row, way).start()
    for step in range(rows):
        for k in (1, 3):
            row = order[k][step]
            to_peer(k, row).wait_recv()
            if (k == 1) == (row < rows // 2):
                relay(row).start()
            for way in range(2):
                to_side(k, row, way).start()
    for step in range(rows // 2):
        for row in (step, rows - 1 - step):
            relay(row).wait_recv()
            for way in range(2):
                to_side(2, row, way).start()
    local.wait()
    for row in range(rows):
        for k in (1, 3):
            to_peer(k, row).wait_send()
        relay(row).wait_send()
    for k in range(depth_count):
        for row in range(rows):
            for way in range(2):
                to_side(k, row, way).wait()


def halo_exchange(blocks, depth_count):
    rows, quarter, edge = blocks.shape[0], blocks.shape[1], blocks.shape[2]
    whole = jax.ShapeDtypeStruct((rows, depth_count * quarter, edge, edge), blocks.dtype)
    anywhere = pl.BlockSpec(memory_space=pl.ANY)
    moved = int(blocks.size) * blocks.dtype.itemsize * (3 * depth_count + 3)
    return pl.pallas_call(
        halo_kernel,
        out_shape=(whole, whole, whole),
        in_specs=[anywhere],
        out_specs=(anywhere, anywhere, anywhere),
        scratch_shapes=[
            pltpu.SemaphoreType.DMA((depth_count, rows)),
            pltpu.SemaphoreType.DMA((depth_count, rows)),
            pltpu.SemaphoreType.DMA((3, depth_count, rows)),
            pltpu.SemaphoreType.DMA((2, depth_count, rows)),
            pltpu.SemaphoreType.DMA((2, rows)),
        ],
        compiler_params=pltpu.CompilerParams(collective_id=1, has_side_effects=True),
        cost_estimate=pl.CostEstimate(flops=0, transcendentals=0, bytes_accessed=moved),
    )(blocks)


def local(blocks, block_cols, product_cols):
    row_count = blocks.shape[0]
    block_edge = blocks.shape[2]
    fill_count = block_cols.shape[1]
    order_total = row_count * lax.axis_size(("row", "col"))
    row_place = lax.axis_index(("row", "col"))
    depth_index = lax.axis_index("depth")
    depth_count = lax.axis_size("depth")
    target_share = product_cols.shape[1] // depth_count

    full_rows, from_before, from_after = halo_exchange(blocks, depth_count)
    near = {0: full_rows, 1: from_before, -1: from_after}
    near[2] = shifted(near[1], ("row", "col"), 1)
    near[-2] = shifted(near[-1], ("row", "col"), -1)

    def halo_of(reach):
        return [near[offset] for offset in range(reach, -reach - 1, -1)]

    own_cols = lax.dynamic_slice_in_dim(block_cols, row_place * row_count, row_count, 0)
    own_targets = lax.dynamic_slice_in_dim(
        product_cols, depth_index * target_share, target_share, 1
    )

    across_targets = lax.dynamic_slice_in_dim(
        product_cols, ((depth_index + 2) % depth_count) * target_share, target_share, 1
    )
    halo_first = halo_of(1)
    halo_second = halo_of(2)
    piece_blocks = row_count * fill_count
    inner_rows = jnp.concatenate([own_cols, product_cols], axis=1)
    ahead_last = lax.dynamic_slice_in_dim(
        product_cols, ((depth_index + 1) % depth_count) * target_share + target_share - 1, 1, 1
    )
    behind_last = lax.dynamic_slice_in_dim(
        product_cols,
        ((depth_index + depth_count - 1) % depth_count) * target_share + target_share - 1, 1, 1,
    )
    targets = jnp.concatenate([own_targets, across_targets, ahead_last, behind_last], axis=1)
    table = block_table(
        block_cols, inner_rows, targets, (row_place - 2) * row_count, order_total,
        fill_count, len(halo_second) * piece_blocks,
    )
    row_stride = inner_rows.shape[1] * targets.shape[1]
    first_view = (row_stride, 0, targets.shape[1], piece_blocks, len(halo_first) * piece_blocks)
    second_view = (row_stride, fill_count, targets.shape[1], 0, len(halo_second) * piece_blocks)
    square, square_rows = square_products(
        table, full_rows, halo_first, depth_count, target_share, first_view
    )
    return block_products(
        table, square_rows, halo_second, target_share, second_view, own=square
    )


def solution(mesh):
    placed = (P(("row", "col"), "depth", None, None), P(), P(("row", "col"), None))
    return jax.shard_map(
        local,
        mesh=mesh,
        in_specs=placed,
        out_specs=P(("row", "col"), "depth", None, None),
        check_vma=False,
    )
```

```python
import functools

import jax
import jax.numpy as jnp
from jax import lax
from jax.experimental import pallas as pl
from jax.experimental.pallas import tpu as pltpu
from jax.sharding import PartitionSpec as P


def shifted(value, axis, steps):
    count = lax.axis_size(axis)
    pairs = [(source, (source + steps) % count) for source in range(count)]
    return lax.ppermute(value, axis, pairs)


def block_table(block_cols, rows, targets, start_row, order_total, fill_count, miss):
    cols_of = block_cols[rows]
    matches = cols_of[:, :, None, :] == targets[:, None, :, None]
    has_match = jnp.any(matches, axis=3)
    slot_ids = jnp.arange(fill_count, dtype=jnp.int32)[None, None, None, :]
    position = jnp.sum(jnp.where(matches, slot_ids, 0), axis=3)
    local_rows = (rows - start_row) % order_total
    flat = local_rows[:, :, None] * fill_count + position
    flat = jnp.clip(flat, 0, miss)
    return jnp.where(has_match, flat, miss).astype(jnp.int32)


def table_pick(idx_ref, view, row, inner, col):
    row_stride, first, inner_stride, shift, cap = view
    entry = idx_ref[row * row_stride + (first + inner) * inner_stride + col]
    return jnp.minimum(jnp.maximum(entry - shift, 0), cap)


def product_kernel(n_out, n_inner, n_pieces, final, view, idx_ref, left_hbm, *rest):
    pieces = rest[:n_pieces]
    rest = rest[n_pieces:]
    if final:
        own_ref, out_ref, halo, lcat, rcat, left_ref, sems = rest
    else:
        out_ref, halo, lcat, rcat, left_ref, sems = rest
    edge = left_ref.shape[-1]
    span = pieces[0].shape[0]
    rows = left_ref.shape[0]
    per_row = span // rows
    halo_rows = n_pieces * rows
    reach = (n_pieces - 1) * rows

    def halo_copy(h):
        piece = pieces[h // rows]
        return pltpu.make_async_copy(
            piece.at[pl.ds((h % rows) * per_row, per_row)],
            halo.at[pl.ds(h * per_row, per_row)],
            sems.at[h],
        )

    def left_copy(row):
        return pltpu.make_async_copy(left_hbm.at[row], left_ref.at[row], sems.at[halo_rows + row])

    def needed(row):
        first = 0 if row == 0 else min(reach + row, halo_rows)
        return range(first, min(reach + row + 1, halo_rows))

    for row in range(rows):
        for h in needed(row):
            halo_copy(h).start()
        left_copy(row).start()
    halo[n_pieces * span] = jnp.zeros((edge, edge), halo.dtype)

    for row in range(left_ref.shape[0]):
        for h in needed(row):
            halo_copy(h).wait()
        left_copy(row).wait()
        lbuf, rbuf = lcat.at[row % 2], rcat.at[row % 2]
        for inner in range(n_inner):
            lbuf[:, inner * edge:(inner + 1) * edge] = left_ref[row, inner]

        for col in range(n_out):
            for inner in range(n_inner):
                pick = table_pick(idx_ref, view, row, inner, col)
                rbuf[inner * edge:(inner + 1) * edge, col * edge:(col + 1) * edge] = halo[pick]
        acc = jnp.dot(lbuf[...], rbuf[...], preferred_element_type=jnp.float32)
        for col in range(n_out):
            part = acc[:, col * edge:(col + 1) * edge]
            if final:
                value = 3.0 * own_ref[row, col].astype(jnp.float32) - 2.0 * part
            else:
                value = part
            out_ref[row, col] = value.astype(out_ref.dtype)


def block_products(table, left, pieces, n_out, view, own=None):
    rows, n_inner, edge = left.shape[0], left.shape[1], left.shape[2]
    final = own is not None
    flat_pieces = [piece.reshape(-1, edge, edge) for piece in pieces]
    span = flat_pieces[0].shape[0]
    operands = [table.reshape(-1), left] + flat_pieces + ([own] if final else [])
    vmem = pl.BlockSpec(memory_space=pltpu.VMEM)
    anywhere = pl.BlockSpec(memory_space=pl.ANY)
    in_specs = [pl.BlockSpec(memory_space=pltpu.SMEM), anywhere] + [anywhere] * len(pieces)
    in_specs += [vmem] if final else []
    flops = 2 * rows * n_out * n_inner * edge ** 3
    moved = sum(int(x.size) * x.dtype.itemsize for x in operands) + rows * n_out * edge * edge * 2
    return pl.pallas_call(
        functools.partial(product_kernel, n_out, n_inner, len(pieces), final, view),
        out_shape=jax.ShapeDtypeStruct((rows, n_out, edge, edge), jnp.bfloat16),
        in_specs=in_specs,
        out_specs=vmem,
        scratch_shapes=[
            pltpu.VMEM((len(pieces) * span + 1, edge, edge), left.dtype),
            pltpu.VMEM((2, edge, n_inner * edge), left.dtype),
            pltpu.VMEM((2, n_inner * edge, n_out * edge), left.dtype),
            pltpu.VMEM(left.shape, left.dtype),
            pltpu.SemaphoreType.DMA((len(pieces) * rows + rows,)),
        ],
        compiler_params=pltpu.CompilerParams(vmem_limit_bytes=62 * 1024 * 1024),
        cost_estimate=pl.CostEstimate(flops=flops, transcendentals=0, bytes_accessed=moved),
    )(*operands)


MESH = pl.DeviceIdType.MESH


def square_kernel(n_own, n_inner, n_pieces, view, idx_ref, left_ref, *rest):
    pieces = rest[:n_pieces]
    out_ref, spread_ref, halo, lcat, rcat, sems, send_sems, recv_sems, keep_sems = rest[
        n_pieces:
    ]
    edge = left_ref.shape[-1]
    span = pieces[0].shape[0]
    row_count = left_ref.shape[0]
    row_at = lax.axis_index("row")
    col_at = lax.axis_index("col")
    depth_at = lax.axis_index("depth")
    depth_count = lax.axis_size("depth")
    ahead = lax.rem(depth_at + 1, depth_count)
    behind = lax.rem(depth_at + depth_count - 1, depth_count)
    across = lax.rem(depth_at + 2, depth_count)

    barrier = pltpu.get_barrier_semaphore()
    for peer in (ahead, behind):
        pl.semaphore_signal(
            barrier, inc=1, device_id=(row_at, col_at, peer), device_id_type=MESH
        )
    pl.semaphore_wait(barrier, 2)

    copies = [
        pltpu.make_async_copy(piece, halo.at[pl.ds(k * span, span)], sems.at[k])
        for k, piece in enumerate(pieces)
    ]
    for copy in copies:
        copy.start()
    halo[n_pieces * span] = jnp.zeros((edge, edge), halo.dtype)
    for copy in copies:
        copy.wait()

    def spread(row, k):
        width = n_own if k == 0 else n_own - 1
        source = out_ref.at[row, pl.ds(0, width)]
        target = spread_ref.at[row, pl.ds(depth_at * n_own, width)]
        if k == 0:
            return pltpu.make_async_copy(source, target, send_sems.at[row, 0])
        return pltpu.make_async_remote_copy(
            src_ref=source,
            dst_ref=target,
            send_sem=send_sems.at[row, k],
            recv_sem=recv_sems.at[row, k],
            device_id=(row_at, col_at, ahead if k == 1 else behind),
            device_id_type=MESH,
        )

    def keep(row, j):
        last = n_own - 1
        start, width, slot = [
            (n_own, n_own, across * n_own),
            (2 * n_own, 1, ahead * n_own + last),
            (2 * n_own + 1, 1, behind * n_own + last),
        ][j]
        return pltpu.make_async_copy(
            out_ref.at[row, pl.ds(start, width)],
            spread_ref.at[row, pl.ds(slot, width)],
            keep_sems.at[row, j],
        )

    def products(row, first, count):
        for inner in range(n_inner):
            lcat[:, inner * edge:(inner + 1) * edge] = left_ref[row, inner]

        for part in range(count):
            for inner in range(n_inner):
                pick = table_pick(idx_ref, view, row, inner, first + part)
                rcat[inner * edge:(inner + 1) * edge, part * edge:(part + 1) * edge] = halo[pick]
        acc = jnp.dot(
            lcat[...], rcat[:, : count * edge], preferred_element_type=jnp.float32
        )
        for part in range(count):
            out_ref[row, first + part] = acc[:, part * edge:(part + 1) * edge].astype(out_ref.dtype)

    def own_body(row, carry):
        products(row, 0, n_own)
        for k in range(3):
            spread(row, k).start()
        return carry

    def across_body(row, carry):
        products(row, n_own, n_own + 2)
        for j in range(3):
            keep(row, j).start()
        return carry

    lax.fori_loop(0, row_count, own_body, 0)
    lax.fori_loop(0, row_count, across_body, 0)
    for row in range(row_count):
        for k in range(3):
            spread(row, k).wait()
        for j in range(3):
            keep(row, j).wait()


def square_products(table, left, pieces, depth_count, n_own, view):
    rows, n_inner, edge = left.shape[0], left.shape[1], left.shape[2]
    flat_pieces = [piece.reshape(-1, edge, edge) for piece in pieces]
    span = flat_pieces[0].shape[0]
    operands = [table.reshape(-1), left] + flat_pieces
    vmem = pl.BlockSpec(memory_space=pltpu.VMEM)
    anywhere = pl.BlockSpec(memory_space=pl.ANY)
    in_specs = [pl.BlockSpec(memory_space=pltpu.SMEM), vmem] + [anywhere] * len(pieces)
    flops = 2 * rows * (2 * n_own + 2) * n_inner * edge ** 3
    moved = sum(int(x.size) * x.dtype.itemsize for x in operands) + rows * n_own * edge * edge * 10
    return pl.pallas_call(
        functools.partial(square_kernel, n_own, n_inner, len(pieces), view),
        out_shape=(
            jax.ShapeDtypeStruct((rows, 2 * n_own + 2, edge, edge), jnp.bfloat16),
            jax.ShapeDtypeStruct((rows, depth_count * n_own, edge, edge), jnp.bfloat16),
        ),
        in_specs=in_specs,
        out_specs=(vmem, anywhere),
        scratch_shapes=[
            pltpu.VMEM((len(pieces) * span + 1, edge, edge), left.dtype),
            pltpu.VMEM((edge, n_inner * edge), left.dtype),
            pltpu.VMEM((n_inner * edge, (n_own + 2) * edge), left.dtype),
            pltpu.SemaphoreType.DMA((len(pieces),)),
            pltpu.SemaphoreType.DMA((rows, 3)),
            pltpu.SemaphoreType.DMA((rows, 3)),
            pltpu.SemaphoreType.DMA((rows, 3)),
        ],
        compiler_params=pltpu.CompilerParams(
            vmem_limit_bytes=62 * 1024 * 1024, collective_id=0, has_side_effects=True
        ),
        cost_estimate=pl.CostEstimate(flops=flops, transcendentals=0, bytes_accessed=moved),
    )(*operands)


def halo_kernel(
    blocks_ref, full_ref, left_ref, right_ref, send_sems, recv_sems, side_send, side_recv,
    relay_sems,
):
    quarter = blocks_ref.shape[1]
    row_at = lax.axis_index("row")
    col_at = lax.axis_index("col")
    depth_at = lax.axis_index("depth")
    col_count = lax.axis_size("col")
    depth_count = lax.axis_size("depth")
    ring = lax.axis_size("row") * col_count
    place = row_at * col_count + col_at
    after = lax.rem(place + 1, ring)
    before = lax.rem(place + ring - 1, ring)
    after_id = (after // col_count, after % col_count, depth_at)
    before_id = (before // col_count, before % col_count, depth_at)
    peer_ids = [
        (row_at, col_at, lax.rem(depth_at + k, depth_count)) for k in range(1, depth_count)
    ]

    barrier = pltpu.get_barrier_semaphore()
    for device in peer_ids + [after_id, before_id]:
        pl.semaphore_signal(barrier, inc=1, device_id=device, device_id_type=MESH)
    pl.semaphore_wait(barrier, depth_count + 1)

    own = pl.ds(depth_at * quarter, quarter)
    rows = blocks_ref.shape[0]
    local = pltpu.make_async_copy(blocks_ref, full_ref.at[:, own], side_send.at[2, 0, 0])
    local.start()

    def to_peer(k, row):
        return pltpu.make_async_remote_copy(
            src_ref=blocks_ref.at[row],
            dst_ref=full_ref.at[row, own],
            send_sem=send_sems.at[k, row],
            recv_sem=recv_sems.at[k, row],
            device_id=peer_ids[k - 1],
            device_id_type=MESH,
        )

    def to_side(k, row, way):
        origin = lax.rem(depth_at + depth_count - k, depth_count)
        slot = pl.ds(origin * quarter, quarter)
        source = blocks_ref.at[row] if k == 0 else full_ref.at[row, slot]
        return pltpu.make_async_remote_copy(
            src_ref=source,
            dst_ref=(left_ref if way == 0 else right_ref).at[row, slot],
            send_sem=side_send.at[way, k, row],
            recv_sem=side_recv.at[way, k, row],
            device_id=after_id if way == 0 else before_id,
            device_id_type=MESH,
        )

    def slot_of(k):
        return pl.ds(lax.rem(depth_at + depth_count - k, depth_count) * quarter, quarter)

    def relay(row):
        k, target = (1, peer_ids[0]) if row < rows // 2 else (3, peer_ids[2])
        return pltpu.make_async_remote_copy(
            src_ref=full_ref.at[row, slot_of(k)],
            dst_ref=full_ref.at[row, slot_of(k)],
            send_sem=relay_sems.at[0, row],
            recv_sem=relay_sems.at[1, row],
            device_id=target,
            device_id_type=MESH,
        )

    order = {1: list(range(rows)), 3: list(range(rows - 1, -1, -1))}
    for step in range(rows):
        for k in (1, 3):
            to_peer(k, order[k][step]).start()
    for row in range(rows):
        for way in range(2):
            to_side(0, row, way).start()
    for step in range(rows):
        for k in (1, 3):
            row = order[k][step]
            to_peer(k, row).wait_recv()
            if (k == 1) == (row < rows // 2):
                relay(row).start()
            for way in range(2):
                to_side(k, row, way).start()
    for step in range(rows // 2):
        for row in (step, rows - 1 - step):
            relay(row).wait_recv()
            for way in range(2):
                to_side(2, row, way).start()
    local.wait()
    for row in range(rows):
        for k in (1, 3):
            to_peer(k, row).wait_send()
        relay(row).wait_send()
    for k in range(depth_count):
        for row in range(rows):
            for way in range(2):
                to_side(k, row, way).wait()


def halo_exchange(blocks, depth_count):
    rows, quarter, edge = blocks.shape[0], blocks.shape[1], blocks.shape[2]
    whole = jax.ShapeDtypeStruct((rows, depth_count * quarter, edge, edge), blocks.dtype)
    anywhere = pl.BlockSpec(memory_space=pl.ANY)
    moved = int(blocks.size) * blocks.dtype.itemsize * (3 * depth_count + 3)
    return pl.pallas_call(
        halo_kernel,
        out_shape=(whole, whole, whole),
        in_specs=[anywhere],
        out_specs=(anywhere, anywhere, anywhere),
        scratch_shapes=[
            pltpu.SemaphoreType.DMA((depth_count, rows)),
            pltpu.SemaphoreType.DMA((depth_count, rows)),
            pltpu.SemaphoreType.DMA((3, depth_count, rows)),
            pltpu.SemaphoreType.DMA((2, depth_count, rows)),
            pltpu.SemaphoreType.DMA((2, rows)),
        ],
        compiler_params=pltpu.CompilerParams(collective_id=1, has_side_effects=True),
        cost_estimate=pl.CostEstimate(flops=0, transcendentals=0, bytes_accessed=moved),
    )(blocks)


def local(blocks, block_cols, product_cols):
    row_count = blocks.shape[0]
    block_edge = blocks.shape[2]
    fill_count = block_cols.shape[1]
    order_total = row_count * lax.axis_size(("row", "col"))
    row_place = lax.axis_index(("row", "col"))
    depth_index = lax.axis_index("depth")
    depth_count = lax.axis_size("depth")
    target_share = product_cols.shape[1] // depth_count

    full_rows, from_before, from_after = halo_exchange(blocks, depth_count)
    near = {0: full_rows, 1: from_before, -1: from_after}
    near[2] = shifted(near[1], ("row", "col"), 1)
    near[-2] = shifted(near[-1], ("row", "col"), -1)

    def halo_of(reach):
        return [near[offset] for offset in range(reach, -reach - 1, -1)]

    own_cols = lax.dynamic_slice_in_dim(block_cols, row_place * row_count, row_count, 0)
    own_targets = lax.dynamic_slice_in_dim(
        product_cols, depth_index * target_share, target_share, 1
    )

    across_targets = lax.dynamic_slice_in_dim(
        product_cols, ((depth_index + 2) % depth_count) * target_share, target_share, 1
    )
    halo_first = halo_of(1)
    halo_second = halo_of(2)
    piece_blocks = row_count * fill_count
    inner_rows = jnp.concatenate([own_cols, product_cols], axis=1)
    ahead_last = lax.dynamic_slice_in_dim(
        product_cols, ((depth_index + 1) % depth_count) * target_share + target_share - 1, 1, 1
    )
    behind_last = lax.dynamic_slice_in_dim(
        product_cols,
        ((depth_index + depth_count - 1) % depth_count) * target_share + target_share - 1, 1, 1,
    )
    targets = jnp.concatenate([own_targets, across_targets, ahead_last, behind_last], axis=1)
    table = block_table(
        block_cols, inner_rows, targets, (row_place - 2) * row_count, order_total,
        fill_count, len(halo_second) * piece_blocks,
    )
    row_stride = inner_rows.shape[1] * targets.shape[1]
    first_view = (row_stride, 0, targets.shape[1], piece_blocks, len(halo_first) * piece_blocks)
    second_view = (row_stride, fill_count, targets.shape[1], 0, len(halo_second) * piece_blocks)
    square, square_rows = square_products(
        table, full_rows, halo_first, depth_count, target_share, first_view
    )
    return block_products(
        table, square_rows, halo_second, target_share, second_view, own=square
    )


def solution(mesh):
    placed = (P(("row", "col"), "depth", None, None), P(), P(("row", "col"), None))
    return jax.shard_map(
        local,
        mesh=mesh,
        in_specs=placed,
        out_specs=P(("row", "col"), "depth", None, None),
        check_vma=False,
    )
```

```python
import functools

import jax
import jax.numpy as jnp
from jax import lax
from jax.experimental import pallas as pl
from jax.experimental.pallas import tpu as pltpu
from jax.sharding import PartitionSpec as P


def shifted(value, axis, steps):
    count = lax.axis_size(axis)
    pairs = [(source, (source + steps) % count) for source in range(count)]
    return lax.ppermute(value, axis, pairs)


def block_table(block_cols, rows, targets, start_row, order_total, fill_count, miss):
    cols_of = block_cols[rows]
    matches = cols_of[:, :, None, :] == targets[:, None, :, None]
    has_match = jnp.any(matches, axis=3)
    slot_ids = jnp.arange(fill_count, dtype=jnp.int32)[None, None, None, :]
    position = jnp.sum(jnp.where(matches, slot_ids, 0), axis=3)
    local_rows = (rows - start_row) % order_total
    flat = local_rows[:, :, None] * fill_count + position
    flat = jnp.clip(flat, 0, miss)
    return jnp.where(has_match, flat, miss).astype(jnp.int32)


def table_pick(idx_ref, view, row, inner, col):
    row_stride, first, inner_stride, shift, cap = view
    entry = idx_ref[row * row_stride + (first + inner) * inner_stride + col]
    return jnp.minimum(jnp.maximum(entry - shift, 0), cap)


def product_kernel(n_out, n_inner, n_pieces, final, view, idx_ref, left_hbm, *rest):
    pieces = rest[:n_pieces]
    rest = rest[n_pieces:]
    if final:
        own_ref, out_ref, halo, lcat, rcat, left_ref, sems = rest
    else:
        out_ref, halo, lcat, rcat, left_ref, sems = rest
    edge = left_hbm.shape[-1]
    span = pieces[0].shape[0]
    rows = left_hbm.shape[0]
    per_row = span // rows
    halo_rows = n_pieces * rows
    reach = (n_pieces - 1) * rows

    def halo_copy(h):
        piece = pieces[h // rows]
        return pltpu.make_async_copy(
            piece.at[pl.ds((h % rows) * per_row, per_row)],
            halo.at[pl.ds(h * per_row, per_row)],
            sems.at[h],
        )

    def left_copy(row, inner):
        return pltpu.make_async_copy(
            left_hbm.at[row, inner],
            left_ref.at[row, :, pl.ds(inner * edge, edge)],
            sems.at[halo_rows + row * n_inner + inner],
        )

    def needed(row):
        first = 0 if row == 0 else min(reach + row, halo_rows)
        return range(first, min(reach + row + 1, halo_rows))

    for row in range(rows):
        for inner in range(n_inner):
            left_copy(row, inner).start()
        for h in needed(row):
            halo_copy(h).start()
    halo[n_pieces * span] = jnp.zeros((edge, edge), halo.dtype)

    for row in range(rows):
        for h in needed(row):
            halo_copy(h).wait()
        for inner in range(n_inner):
            left_copy(row, inner).wait()
        lbuf, rbuf = left_ref.at[row], rcat.at[row % 2]

        for col in range(n_out):
            for inner in range(n_inner):
                pick = table_pick(idx_ref, view, row, inner, col)
                rbuf[inner * edge:(inner + 1) * edge, col * edge:(col + 1) * edge] = halo[pick]
        acc = jnp.dot(lbuf[...], rbuf[...], preferred_element_type=jnp.float32)
        for col in range(n_out):
            part = acc[:, col * edge:(col + 1) * edge]
            if final:
                value = 3.0 * own_ref[row, col].astype(jnp.float32) - 2.0 * part
            else:
                value = part
            out_ref[row, col] = value.astype(out_ref.dtype)


def block_products(table, left, pieces, n_out, view, own=None):
    rows, n_inner, edge = left.shape[0], left.shape[1], left.shape[2]
    final = own is not None
    flat_pieces = [piece.reshape(-1, edge, edge) for piece in pieces]
    span = flat_pieces[0].shape[0]
    operands = [table.reshape(-1), left] + flat_pieces + ([own] if final else [])
    vmem = pl.BlockSpec(memory_space=pltpu.VMEM)
    anywhere = pl.BlockSpec(memory_space=pl.ANY)
    in_specs = [pl.BlockSpec(memory_space=pltpu.SMEM), anywhere] + [anywhere] * len(pieces)
    in_specs += [vmem] if final else []
    flops = 2 * rows * n_out * n_inner * edge ** 3
    moved = sum(int(x.size) * x.dtype.itemsize for x in operands) + rows * n_out * edge * edge * 2
    return pl.pallas_call(
        functools.partial(product_kernel, n_out, n_inner, len(pieces), final, view),
        out_shape=jax.ShapeDtypeStruct((rows, n_out, edge, edge), jnp.bfloat16),
        in_specs=in_specs,
        out_specs=vmem,
        scratch_shapes=[
            pltpu.VMEM((len(pieces) * span + 1, edge, edge), left.dtype),
            pltpu.VMEM((1, 1), left.dtype),
            pltpu.VMEM((2, n_inner * edge, n_out * edge), left.dtype),
            pltpu.VMEM((rows, edge, n_inner * edge), left.dtype),
            pltpu.SemaphoreType.DMA((len(pieces) * rows + rows * n_inner,)),
        ],
        compiler_params=pltpu.CompilerParams(vmem_limit_bytes=62 * 1024 * 1024),
        cost_estimate=pl.CostEstimate(flops=flops, transcendentals=0, bytes_accessed=moved),
    )(*operands)


MESH = pl.DeviceIdType.MESH


def square_kernel(n_own, n_inner, n_pieces, view, idx_ref, left_ref, *rest):
    pieces = rest[:n_pieces]
    out_ref, spread_ref, halo, lcat, rcat, sems, send_sems, recv_sems, keep_sems = rest[
        n_pieces:
    ]
    edge = left_ref.shape[-1]
    span = pieces[0].shape[0]
    row_count = left_ref.shape[0]
    row_at = lax.axis_index("row")
    col_at = lax.axis_index("col")
    depth_at = lax.axis_index("depth")
    depth_count = lax.axis_size("depth")
    ahead = lax.rem(depth_at + 1, depth_count)
    behind = lax.rem(depth_at + depth_count - 1, depth_count)
    across = lax.rem(depth_at + 2, depth_count)

    barrier = pltpu.get_barrier_semaphore()
    for peer in (ahead, behind):
        pl.semaphore_signal(
            barrier, inc=1, device_id=(row_at, col_at, peer), device_id_type=MESH
        )
    pl.semaphore_wait(barrier, 2)

    copies = [
        pltpu.make_async_copy(piece, halo.at[pl.ds(k * span, span)], sems.at[k])
        for k, piece in enumerate(pieces)
    ]
    for copy in copies:
        copy.start()
    halo[n_pieces * span] = jnp.zeros((edge, edge), halo.dtype)
    for copy in copies:
        copy.wait()

    def spread(row, k):
        width = n_own if k == 0 else n_own - 1
        source = out_ref.at[row, pl.ds(0, width)]
        target = spread_ref.at[row, pl.ds(depth_at * n_own, width)]
        if k == 0:
            return pltpu.make_async_copy(source, target, send_sems.at[row, 0])
        return pltpu.make_async_remote_copy(
            src_ref=source,
            dst_ref=target,
            send_sem=send_sems.at[row, k],
            recv_sem=recv_sems.at[row, k],
            device_id=(row_at, col_at, ahead if k == 1 else behind),
            device_id_type=MESH,
        )

    def keep(row, j):
        last = n_own - 1
        start, width, slot = [
            (n_own, n_own, across * n_own),
            (2 * n_own, 1, ahead * n_own + last),
            (2 * n_own + 1, 1, behind * n_own + last),
        ][j]
        return pltpu.make_async_copy(
            out_ref.at[row, pl.ds(start, width)],
            spread_ref.at[row, pl.ds(slot, width)],
            keep_sems.at[row, j],
        )

    def products(row, first, count):
        for inner in range(n_inner):
            lcat[:, inner * edge:(inner + 1) * edge] = left_ref[row, inner]

        for part in range(count):
            for inner in range(n_inner):
                pick = table_pick(idx_ref, view, row, inner, first + part)
                rcat[inner * edge:(inner + 1) * edge, part * edge:(part + 1) * edge] = halo[pick]
        acc = jnp.dot(
            lcat[...], rcat[:, : count * edge], preferred_element_type=jnp.float32
        )
        for part in range(count):
            out_ref[row, first + part] = acc[:, part * edge:(part + 1) * edge].astype(out_ref.dtype)

    def own_body(row, carry):
        products(row, 0, n_own)
        for k in range(3):
            spread(row, k).start()
        return carry

    def across_body(row, carry):
        products(row, n_own, n_own + 2)
        for j in range(3):
            keep(row, j).start()
        return carry

    lax.fori_loop(0, row_count, own_body, 0)
    lax.fori_loop(0, row_count, across_body, 0)
    for row in range(row_count):
        for k in range(3):
            spread(row, k).wait()
        for j in range(3):
            keep(row, j).wait()


def square_products(table, left, pieces, depth_count, n_own, view):
    rows, n_inner, edge = left.shape[0], left.shape[1], left.shape[2]
    flat_pieces = [piece.reshape(-1, edge, edge) for piece in pieces]
    span = flat_pieces[0].shape[0]
    operands = [table.reshape(-1), left] + flat_pieces
    vmem = pl.BlockSpec(memory_space=pltpu.VMEM)
    anywhere = pl.BlockSpec(memory_space=pl.ANY)
    in_specs = [pl.BlockSpec(memory_space=pltpu.SMEM), vmem] + [anywhere] * len(pieces)
    flops = 2 * rows * (2 * n_own + 2) * n_inner * edge ** 3
    moved = sum(int(x.size) * x.dtype.itemsize for x in operands) + rows * n_own * edge * edge * 10
    return pl.pallas_call(
        functools.partial(square_kernel, n_own, n_inner, len(pieces), view),
        out_shape=(
            jax.ShapeDtypeStruct((rows, 2 * n_own + 2, edge, edge), jnp.bfloat16),
            jax.ShapeDtypeStruct((rows, depth_count * n_own, edge, edge), jnp.bfloat16),
        ),
        in_specs=in_specs,
        out_specs=(vmem, anywhere),
        scratch_shapes=[
            pltpu.VMEM((len(pieces) * span + 1, edge, edge), left.dtype),
            pltpu.VMEM((edge, n_inner * edge), left.dtype),
            pltpu.VMEM((n_inner * edge, (n_own + 2) * edge), left.dtype),
            pltpu.SemaphoreType.DMA((len(pieces),)),
            pltpu.SemaphoreType.DMA((rows, 3)),
            pltpu.SemaphoreType.DMA((rows, 3)),
            pltpu.SemaphoreType.DMA((rows, 3)),
        ],
        compiler_params=pltpu.CompilerParams(
            vmem_limit_bytes=62 * 1024 * 1024, collective_id=0, has_side_effects=True
        ),
        cost_estimate=pl.CostEstimate(flops=flops, transcendentals=0, bytes_accessed=moved),
    )(*operands)


def halo_kernel(
    blocks_ref, full_ref, left_ref, right_ref, send_sems, recv_sems, side_send, side_recv,
    relay_sems,
):
    quarter = blocks_ref.shape[1]
    row_at = lax.axis_index("row")
    col_at = lax.axis_index("col")
    depth_at = lax.axis_index("depth")
    col_count = lax.axis_size("col")
    depth_count = lax.axis_size("depth")
    ring = lax.axis_size("row") * col_count
    place = row_at * col_count + col_at
    after = lax.rem(place + 1, ring)
    before = lax.rem(place + ring - 1, ring)
    after_id = (after // col_count, after % col_count, depth_at)
    before_id = (before // col_count, before % col_count, depth_at)
    peer_ids = [
        (row_at, col_at, lax.rem(depth_at + k, depth_count)) for k in range(1, depth_count)
    ]

    barrier = pltpu.get_barrier_semaphore()
    for device in peer_ids + [after_id, before_id]:
        pl.semaphore_signal(barrier, inc=1, device_id=device, device_id_type=MESH)
    pl.semaphore_wait(barrier, depth_count + 1)

    own = pl.ds(depth_at * quarter, quarter)
    rows = blocks_ref.shape[0]
    local = pltpu.make_async_copy(blocks_ref, full_ref.at[:, own], side_send.at[2, 0, 0])
    local.start()

    def to_peer(k, row):
        return pltpu.make_async_remote_copy(
            src_ref=blocks_ref.at[row],
            dst_ref=full_ref.at[row, own],
            send_sem=send_sems.at[k, row],
            recv_sem=recv_sems.at[k, row],
            device_id=peer_ids[k - 1],
            device_id_type=MESH,
        )

    def to_side(k, row, way):
        origin = lax.rem(depth_at + depth_count - k, depth_count)
        slot = pl.ds(origin * quarter, quarter)
        source = blocks_ref.at[row] if k == 0 else full_ref.at[row, slot]
        return pltpu.make_async_remote_copy(
            src_ref=source,
            dst_ref=(left_ref if way == 0 else right_ref).at[row, slot],
            send_sem=side_send.at[way, k, row],
            recv_sem=side_recv.at[way, k, row],
            device_id=after_id if way == 0 else before_id,
            device_id_type=MESH,
        )

    def slot_of(k):
        return pl.ds(lax.rem(depth_at + depth_count - k, depth_count) * quarter, quarter)

    def relay(row):
        k, target = (1, peer_ids[0]) if row < rows // 2 else (3, peer_ids[2])
        return pltpu.make_async_remote_copy(
            src_ref=full_ref.at[row, slot_of(k)],
            dst_ref=full_ref.at[row, slot_of(k)],
            send_sem=relay_sems.at[0, row],
            recv_sem=relay_sems.at[1, row],
            device_id=target,
            device_id_type=MESH,
        )

    order = {1: list(range(rows)), 3: list(range(rows - 1, -1, -1))}
    for step in range(rows):
        for k in (1, 3):
            to_peer(k, order[k][step]).start()
    for row in range(rows):
        for way in range(2):
            to_side(0, row, way).start()
    for step in range(rows):
        for k in (1, 3):
            row = order[k][step]
            to_peer(k, row).wait_recv()
            if (k == 1) == (row < rows // 2):
                relay(row).start()
            for way in range(2):
                to_side(k, row, way).start()
    for step in range(rows // 2):
        for row in (step, rows - 1 - step):
            relay(row).wait_recv()
            for way in range(2):
                to_side(2, row, way).start()
    local.wait()
    for row in range(rows):
        for k in (1, 3):
            to_peer(k, row).wait_send()
        relay(row).wait_send()
    for k in range(depth_count):
        for row in range(rows):
            for way in range(2):
                to_side(k, row, way).wait()


def halo_exchange(blocks, depth_count):
    rows, quarter, edge = blocks.shape[0], blocks.shape[1], blocks.shape[2]
    whole = jax.ShapeDtypeStruct((rows, depth_count * quarter, edge, edge), blocks.dtype)
    anywhere = pl.BlockSpec(memory_space=pl.ANY)
    moved = int(blocks.size) * blocks.dtype.itemsize * (3 * depth_count + 3)
    return pl.pallas_call(
        halo_kernel,
        out_shape=(whole, whole, whole),
        in_specs=[anywhere],
        out_specs=(anywhere, anywhere, anywhere),
        scratch_shapes=[
            pltpu.SemaphoreType.DMA((depth_count, rows)),
            pltpu.SemaphoreType.DMA((depth_count, rows)),
            pltpu.SemaphoreType.DMA((3, depth_count, rows)),
            pltpu.SemaphoreType.DMA((2, depth_count, rows)),
            pltpu.SemaphoreType.DMA((2, rows)),
        ],
        compiler_params=pltpu.CompilerParams(collective_id=1, has_side_effects=True),
        cost_estimate=pl.CostEstimate(flops=0, transcendentals=0, bytes_accessed=moved),
    )(blocks)


def local(blocks, block_cols, product_cols):
    row_count = blocks.shape[0]
    block_edge = blocks.shape[2]
    fill_count = block_cols.shape[1]
    order_total = row_count * lax.axis_size(("row", "col"))
    row_place = lax.axis_index(("row", "col"))
    depth_index = lax.axis_index("depth")
    depth_count = lax.axis_size("depth")
    target_share = product_cols.shape[1] // depth_count

    full_rows, from_before, from_after = halo_exchange(blocks, depth_count)
    near = {0: full_rows, 1: from_before, -1: from_after}
    near[2] = shifted(near[1], ("row", "col"), 1)
    near[-2] = shifted(near[-1], ("row", "col"), -1)

    def halo_of(reach):
        return [near[offset] for offset in range(reach, -reach - 1, -1)]

    own_cols = lax.dynamic_slice_in_dim(block_cols, row_place * row_count, row_count, 0)
    own_targets = lax.dynamic_slice_in_dim(
        product_cols, depth_index * target_share, target_share, 1
    )

    across_targets = lax.dynamic_slice_in_dim(
        product_cols, ((depth_index + 2) % depth_count) * target_share, target_share, 1
    )
    halo_first = halo_of(1)
    halo_second = halo_of(2)
    piece_blocks = row_count * fill_count
    inner_rows = jnp.concatenate([own_cols, product_cols], axis=1)
    ahead_last = lax.dynamic_slice_in_dim(
        product_cols, ((depth_index + 1) % depth_count) * target_share + target_share - 1, 1, 1
    )
    behind_last = lax.dynamic_slice_in_dim(
        product_cols,
        ((depth_index + depth_count - 1) % depth_count) * target_share + target_share - 1, 1, 1,
    )
    targets = jnp.concatenate([own_targets, across_targets, ahead_last, behind_last], axis=1)
    table = block_table(
        block_cols, inner_rows, targets, (row_place - 2) * row_count, order_total,
        fill_count, len(halo_second) * piece_blocks,
    )
    row_stride = inner_rows.shape[1] * targets.shape[1]
    first_view = (row_stride, 0, targets.shape[1], piece_blocks, len(halo_first) * piece_blocks)
    second_view = (row_stride, fill_count, targets.shape[1], 0, len(halo_second) * piece_blocks)
    square, square_rows = square_products(
        table, full_rows, halo_first, depth_count, target_share, first_view
    )
    return block_products(
        table, square_rows, halo_second, target_share, second_view, own=square
    )


def solution(mesh):
    placed = (P(("row", "col"), "depth", None, None), P(), P(("row", "col"), None))
    return jax.shard_map(
        local,
        mesh=mesh,
        in_specs=placed,
        out_specs=P(("row", "col"), "depth", None, None),
        check_vma=False,
    )
```

```python
import functools

import jax
import jax.numpy as jnp
from jax import lax
from jax.experimental import pallas as pl
from jax.experimental.pallas import tpu as pltpu
from jax.sharding import PartitionSpec as P


def shifted(value, axis, steps):
    count = lax.axis_size(axis)
    pairs = [(source, (source + steps) % count) for source in range(count)]
    return lax.ppermute(value, axis, pairs)


def block_table(block_cols, rows, targets, start_row, order_total, fill_count, miss):
    cols_of = block_cols[rows]
    matches = cols_of[:, :, None, :] == targets[:, None, :, None]
    has_match = jnp.any(matches, axis=3)
    slot_ids = jnp.arange(fill_count, dtype=jnp.int32)[None, None, None, :]
    position = jnp.sum(jnp.where(matches, slot_ids, 0), axis=3)
    local_rows = (rows - start_row) % order_total
    flat = local_rows[:, :, None] * fill_count + position
    flat = jnp.clip(flat, 0, miss)
    return jnp.where(has_match, flat, miss).astype(jnp.int32)


def table_pick(idx_ref, view, row, inner, col):
    row_stride, first, inner_stride, shift, cap = view
    entry = idx_ref[row * row_stride + (first + inner) * inner_stride + col]
    return jnp.minimum(jnp.maximum(entry - shift, 0), cap)


def product_kernel(n_out, n_inner, n_pieces, final, view, idx_ref, left_hbm, *rest):
    pieces = rest[:n_pieces]
    rest = rest[n_pieces:]
    if final:
        own_ref, out_hbm, halo, lcat, rcat, left_ref, out_ref, sems = rest
    else:
        out_hbm, halo, lcat, rcat, left_ref, out_ref, sems = rest
    edge = left_ref.shape[-1]
    span = pieces[0].shape[0]
    rows = left_ref.shape[0]
    per_row = span // rows
    halo_rows = n_pieces * rows
    reach = (n_pieces - 1) * rows

    def halo_copy(h):
        piece = pieces[h // rows]
        return pltpu.make_async_copy(
            piece.at[pl.ds((h % rows) * per_row, per_row)],
            halo.at[pl.ds(h * per_row, per_row)],
            sems.at[h],
        )

    def left_copy(row):
        return pltpu.make_async_copy(left_hbm.at[row], left_ref.at[row], sems.at[halo_rows + row])

    def out_copy(row):
        return pltpu.make_async_copy(
            out_ref.at[row], out_hbm.at[row], sems.at[halo_rows + rows + row]
        )

    def needed(row):
        first = 0 if row == 0 else min(reach + row, halo_rows)
        return range(first, min(reach + row + 1, halo_rows))

    for row in range(rows):
        for h in needed(row):
            halo_copy(h).start()
        left_copy(row).start()
    halo[n_pieces * span] = jnp.zeros((edge, edge), halo.dtype)

    for row in range(left_ref.shape[0]):
        for h in needed(row):
            halo_copy(h).wait()
        left_copy(row).wait()
        lbuf, rbuf = lcat.at[row % 2], rcat.at[row % 2]
        for inner in range(n_inner):
            lbuf[:, inner * edge:(inner + 1) * edge] = left_ref[row, inner]

        for col in range(n_out):
            for inner in range(n_inner):
                pick = table_pick(idx_ref, view, row, inner, col)
                rbuf[inner * edge:(inner + 1) * edge, col * edge:(col + 1) * edge] = halo[pick]
        acc = jnp.dot(lbuf[...], rbuf[...], preferred_element_type=jnp.float32)
        for col in range(n_out):
            part = acc[:, col * edge:(col + 1) * edge]
            if final:
                value = 3.0 * own_ref[row, col].astype(jnp.float32) - 2.0 * part
            else:
                value = part
            out_ref[row, col] = value.astype(out_ref.dtype)
        out_copy(row).start()
    for row in range(rows):
        out_copy(row).wait()


def block_products(table, left, pieces, n_out, view, own=None):
    rows, n_inner, edge = left.shape[0], left.shape[1], left.shape[2]
    final = own is not None
    flat_pieces = [piece.reshape(-1, edge, edge) for piece in pieces]
    span = flat_pieces[0].shape[0]
    operands = [table.reshape(-1), left] + flat_pieces + ([own] if final else [])
    vmem = pl.BlockSpec(memory_space=pltpu.VMEM)
    anywhere = pl.BlockSpec(memory_space=pl.ANY)
    in_specs = [pl.BlockSpec(memory_space=pltpu.SMEM), anywhere] + [anywhere] * len(pieces)
    in_specs += [vmem] if final else []
    flops = 2 * rows * n_out * n_inner * edge ** 3
    moved = sum(int(x.size) * x.dtype.itemsize for x in operands) + rows * n_out * edge * edge * 2
    return pl.pallas_call(
        functools.partial(product_kernel, n_out, n_inner, len(pieces), final, view),
        out_shape=jax.ShapeDtypeStruct((rows, n_out, edge, edge), jnp.bfloat16),
        in_specs=in_specs,
        out_specs=anywhere,
        scratch_shapes=[
            pltpu.VMEM((len(pieces) * span + 1, edge, edge), left.dtype),
            pltpu.VMEM((2, edge, n_inner * edge), left.dtype),
            pltpu.VMEM((2, n_inner * edge, n_out * edge), left.dtype),
            pltpu.VMEM(left.shape, left.dtype),
            pltpu.VMEM((rows, n_out, edge, edge), jnp.bfloat16),
            pltpu.SemaphoreType.DMA((len(pieces) * rows + 2 * rows,)),
        ],
        compiler_params=pltpu.CompilerParams(vmem_limit_bytes=62 * 1024 * 1024),
        cost_estimate=pl.CostEstimate(flops=flops, transcendentals=0, bytes_accessed=moved),
    )(*operands)


MESH = pl.DeviceIdType.MESH


def square_kernel(n_own, n_inner, n_pieces, view, idx_ref, left_ref, *rest):
    pieces = rest[:n_pieces]
    out_ref, spread_ref, halo, lcat, rcat, sems, send_sems, recv_sems, keep_sems = rest[
        n_pieces:
    ]
    edge = left_ref.shape[-1]
    span = pieces[0].shape[0]
    row_count = left_ref.shape[0]
    row_at = lax.axis_index("row")
    col_at = lax.axis_index("col")
    depth_at = lax.axis_index("depth")
    depth_count = lax.axis_size("depth")
    ahead = lax.rem(depth_at + 1, depth_count)
    behind = lax.rem(depth_at + depth_count - 1, depth_count)
    across = lax.rem(depth_at + 2, depth_count)

    barrier = pltpu.get_barrier_semaphore()
    for peer in (ahead, behind):
        pl.semaphore_signal(
            barrier, inc=1, device_id=(row_at, col_at, peer), device_id_type=MESH
        )
    pl.semaphore_wait(barrier, 2)

    copies = [
        pltpu.make_async_copy(piece, halo.at[pl.ds(k * span, span)], sems.at[k])
        for k, piece in enumerate(pieces)
    ]
    for copy in copies:
        copy.start()
    halo[n_pieces * span] = jnp.zeros((edge, edge), halo.dtype)
    for copy in copies:
        copy.wait()

    def spread(row, k):
        width = n_own if k == 0 else n_own - 1
        source = out_ref.at[row, pl.ds(0, width)]
        target = spread_ref.at[row, pl.ds(depth_at * n_own, width)]
        if k == 0:
            return pltpu.make_async_copy(source, target, send_sems.at[row, 0])
        return pltpu.make_async_remote_copy(
            src_ref=source,
            dst_ref=target,
            send_sem=send_sems.at[row, k],
            recv_sem=recv_sems.at[row, k],
            device_id=(row_at, col_at, ahead if k == 1 else behind),
            device_id_type=MESH,
        )

    def keep(row, j):
        last = n_own - 1
        start, width, slot = [
            (n_own, n_own, across * n_own),
            (2 * n_own, 1, ahead * n_own + last),
            (2 * n_own + 1, 1, behind * n_own + last),
        ][j]
        return pltpu.make_async_copy(
            out_ref.at[row, pl.ds(start, width)],
            spread_ref.at[row, pl.ds(slot, width)],
            keep_sems.at[row, j],
        )

    def products(row, first, count):
        for inner in range(n_inner):
            lcat[:, inner * edge:(inner + 1) * edge] = left_ref[row, inner]

        for part in range(count):
            for inner in range(n_inner):
                pick = table_pick(idx_ref, view, row, inner, first + part)
                rcat[inner * edge:(inner + 1) * edge, part * edge:(part + 1) * edge] = halo[pick]
        acc = jnp.dot(
            lcat[...], rcat[:, : count * edge], preferred_element_type=jnp.float32
        )
        for part in range(count):
            out_ref[row, first + part] = acc[:, part * edge:(part + 1) * edge].astype(out_ref.dtype)

    def own_body(row, carry):
        products(row, 0, n_own)
        for k in range(3):
            spread(row, k).start()
        return carry

    def across_body(row, carry):
        products(row, n_own, n_own + 2)
        for j in range(3):
            keep(row, j).start()
        return carry

    lax.fori_loop(0, row_count, own_body, 0)
    lax.fori_loop(0, row_count, across_body, 0)
    for row in range(row_count):
        for k in range(3):
            spread(row, k).wait()
        for j in range(3):
            keep(row, j).wait()


def square_products(table, left, pieces, depth_count, n_own, view):
    rows, n_inner, edge = left.shape[0], left.shape[1], left.shape[2]
    flat_pieces = [piece.reshape(-1, edge, edge) for piece in pieces]
    span = flat_pieces[0].shape[0]
    operands = [table.reshape(-1), left] + flat_pieces
    vmem = pl.BlockSpec(memory_space=pltpu.VMEM)
    anywhere = pl.BlockSpec(memory_space=pl.ANY)
    in_specs = [pl.BlockSpec(memory_space=pltpu.SMEM), vmem] + [anywhere] * len(pieces)
    flops = 2 * rows * (2 * n_own + 2) * n_inner * edge ** 3
    moved = sum(int(x.size) * x.dtype.itemsize for x in operands) + rows * n_own * edge * edge * 10
    return pl.pallas_call(
        functools.partial(square_kernel, n_own, n_inner, len(pieces), view),
        out_shape=(
            jax.ShapeDtypeStruct((rows, 2 * n_own + 2, edge, edge), jnp.bfloat16),
            jax.ShapeDtypeStruct((rows, depth_count * n_own, edge, edge), jnp.bfloat16),
        ),
        in_specs=in_specs,
        out_specs=(vmem, anywhere),
        scratch_shapes=[
            pltpu.VMEM((len(pieces) * span + 1, edge, edge), left.dtype),
            pltpu.VMEM((edge, n_inner * edge), left.dtype),
            pltpu.VMEM((n_inner * edge, (n_own + 2) * edge), left.dtype),
            pltpu.SemaphoreType.DMA((len(pieces),)),
            pltpu.SemaphoreType.DMA((rows, 3)),
            pltpu.SemaphoreType.DMA((rows, 3)),
            pltpu.SemaphoreType.DMA((rows, 3)),
        ],
        compiler_params=pltpu.CompilerParams(
            vmem_limit_bytes=62 * 1024 * 1024, collective_id=0, has_side_effects=True
        ),
        cost_estimate=pl.CostEstimate(flops=flops, transcendentals=0, bytes_accessed=moved),
    )(*operands)


def halo_kernel(
    blocks_ref, full_ref, left_ref, right_ref, send_sems, recv_sems, side_send, side_recv,
    relay_sems,
):
    quarter = blocks_ref.shape[1]
    row_at = lax.axis_index("row")
    col_at = lax.axis_index("col")
    depth_at = lax.axis_index("depth")
    col_count = lax.axis_size("col")
    depth_count = lax.axis_size("depth")
    ring = lax.axis_size("row") * col_count
    place = row_at * col_count + col_at
    after = lax.rem(place + 1, ring)
    before = lax.rem(place + ring - 1, ring)
    after_id = (after // col_count, after % col_count, depth_at)
    before_id = (before // col_count, before % col_count, depth_at)
    peer_ids = [
        (row_at, col_at, lax.rem(depth_at + k, depth_count)) for k in range(1, depth_count)
    ]

    barrier = pltpu.get_barrier_semaphore()
    for device in peer_ids + [after_id, before_id]:
        pl.semaphore_signal(barrier, inc=1, device_id=device, device_id_type=MESH)
    pl.semaphore_wait(barrier, depth_count + 1)

    own = pl.ds(depth_at * quarter, quarter)
    rows = blocks_ref.shape[0]
    local = pltpu.make_async_copy(blocks_ref, full_ref.at[:, own], side_send.at[2, 0, 0])
    local.start()

    def to_peer(k, row):
        return pltpu.make_async_remote_copy(
            src_ref=blocks_ref.at[row],
            dst_ref=full_ref.at[row, own],
            send_sem=send_sems.at[k, row],
            recv_sem=recv_sems.at[k, row],
            device_id=peer_ids[k - 1],
            device_id_type=MESH,
        )

    def to_side(k, row, way):
        origin = lax.rem(depth_at + depth_count - k, depth_count)
        slot = pl.ds(origin * quarter, quarter)
        source = blocks_ref.at[row] if k == 0 else full_ref.at[row, slot]
        return pltpu.make_async_remote_copy(
            src_ref=source,
            dst_ref=(left_ref if way == 0 else right_ref).at[row, slot],
            send_sem=side_send.at[way, k, row],
            recv_sem=side_recv.at[way, k, row],
            device_id=after_id if way == 0 else before_id,
            device_id_type=MESH,
        )

    def slot_of(k):
        return pl.ds(lax.rem(depth_at + depth_count - k, depth_count) * quarter, quarter)

    def relay(row):
        k, target = (1, peer_ids[0]) if row < rows // 2 else (3, peer_ids[2])
        return pltpu.make_async_remote_copy(
            src_ref=full_ref.at[row, slot_of(k)],
            dst_ref=full_ref.at[row, slot_of(k)],
            send_sem=relay_sems.at[0, row],
            recv_sem=relay_sems.at[1, row],
            device_id=target,
            device_id_type=MESH,
        )

    order = {1: list(range(rows)), 3: list(range(rows - 1, -1, -1))}
    for step in range(rows):
        for k in (1, 3):
            to_peer(k, order[k][step]).start()
    for row in range(rows):
        for way in range(2):
            to_side(0, row, way).start()
    for step in range(rows):
        for k in (1, 3):
            row = order[k][step]
            to_peer(k, row).wait_recv()
            if (k == 1) == (row < rows // 2):
                relay(row).start()
            for way in range(2):
                to_side(k, row, way).start()
    for step in range(rows // 2):
        for row in (step, rows - 1 - step):
            relay(row).wait_recv()
            for way in range(2):
                to_side(2, row, way).start()
    local.wait()
    for row in range(rows):
        for k in (1, 3):
            to_peer(k, row).wait_send()
        relay(row).wait_send()
    for k in range(depth_count):
        for row in range(rows):
            for way in range(2):
                to_side(k, row, way).wait()


def halo_exchange(blocks, depth_count):
    rows, quarter, edge = blocks.shape[0], blocks.shape[1], blocks.shape[2]
    whole = jax.ShapeDtypeStruct((rows, depth_count * quarter, edge, edge), blocks.dtype)
    anywhere = pl.BlockSpec(memory_space=pl.ANY)
    moved = int(blocks.size) * blocks.dtype.itemsize * (3 * depth_count + 3)
    return pl.pallas_call(
        halo_kernel,
        out_shape=(whole, whole, whole),
        in_specs=[anywhere],
        out_specs=(anywhere, anywhere, anywhere),
        scratch_shapes=[
            pltpu.SemaphoreType.DMA((depth_count, rows)),
            pltpu.SemaphoreType.DMA((depth_count, rows)),
            pltpu.SemaphoreType.DMA((3, depth_count, rows)),
            pltpu.SemaphoreType.DMA((2, depth_count, rows)),
            pltpu.SemaphoreType.DMA((2, rows)),
        ],
        compiler_params=pltpu.CompilerParams(collective_id=1, has_side_effects=True),
        cost_estimate=pl.CostEstimate(flops=0, transcendentals=0, bytes_accessed=moved),
    )(blocks)


def local(blocks, block_cols, product_cols):
    row_count = blocks.shape[0]
    block_edge = blocks.shape[2]
    fill_count = block_cols.shape[1]
    order_total = row_count * lax.axis_size(("row", "col"))
    row_place = lax.axis_index(("row", "col"))
    depth_index = lax.axis_index("depth")
    depth_count = lax.axis_size("depth")
    target_share = product_cols.shape[1] // depth_count

    full_rows, from_before, from_after = halo_exchange(blocks, depth_count)
    near = {0: full_rows, 1: from_before, -1: from_after}
    near[2] = shifted(near[1], ("row", "col"), 1)
    near[-2] = shifted(near[-1], ("row", "col"), -1)

    def halo_of(reach):
        return [near[offset] for offset in range(reach, -reach - 1, -1)]

    own_cols = lax.dynamic_slice_in_dim(block_cols, row_place * row_count, row_count, 0)
    own_targets = lax.dynamic_slice_in_dim(
        product_cols, depth_index * target_share, target_share, 1
    )

    across_targets = lax.dynamic_slice_in_dim(
        product_cols, ((depth_index + 2) % depth_count) * target_share, target_share, 1
    )
    halo_first = halo_of(1)
    halo_second = halo_of(2)
    piece_blocks = row_count * fill_count
    inner_rows = jnp.concatenate([own_cols, product_cols], axis=1)
    ahead_last = lax.dynamic_slice_in_dim(
        product_cols, ((depth_index + 1) % depth_count) * target_share + target_share - 1, 1, 1
    )
    behind_last = lax.dynamic_slice_in_dim(
        product_cols,
        ((depth_index + depth_count - 1) % depth_count) * target_share + target_share - 1, 1, 1,
    )
    targets = jnp.concatenate([own_targets, across_targets, ahead_last, behind_last], axis=1)
    table = block_table(
        block_cols, inner_rows, targets, (row_place - 2) * row_count, order_total,
        fill_count, len(halo_second) * piece_blocks,
    )
    row_stride = inner_rows.shape[1] * targets.shape[1]
    first_view = (row_stride, 0, targets.shape[1], piece_blocks, len(halo_first) * piece_blocks)
    second_view = (row_stride, fill_count, targets.shape[1], 0, len(halo_second) * piece_blocks)
    square, square_rows = square_products(
        table, full_rows, halo_first, depth_count, target_share, first_view
    )
    return block_products(
        table, square_rows, halo_second, target_share, second_view, own=square
    )


def solution(mesh):
    placed = (P(("row", "col"), "depth", None, None), P(), P(("row", "col"), None))
    return jax.shard_map(
        local,
        mesh=mesh,
        in_specs=placed,
        out_specs=P(("row", "col"), "depth", None, None),
        check_vma=False,
    )
```
